256 devices in a mesh: dp: 4 (over z_lo), space: 64 (over x, z_hi, y, core).
Axes of the slice: x: 4, y: 4, z: 8 (z_hi: 2, z_lo: 4; z = z_hi * 4 + z_lo), core: 2. Of those that a mesh axis runs over, the one named last changes fastest.
Arguments:
- features: bfloat16 [4, 192, 64, 1024], P('dp', 'space'), may hold values from -6 to 6
- cotangent: bfloat16 [4, 192, 128, 128], P('dp', 'space'), may hold values from -6 to 6
- conv_one: bfloat16 [64, 1728], P('dp'), may hold values from -0.15625 to 0.15625
- down_weight: bfloat16 [128, 512], P('dp'), may hold values from -0.25 to 0.25
- conv_two: bfloat16 [128, 3456], P('dp'), may hold values from -0.109375 to 0.109375
- patch_home: int32 [128], replicated, may hold values from 0 to 191, as said below
- patch_links: int32 [128, 4], replicated, may hold values from -1 to 127, as said below
Outputs:
- level_two: bfloat16 [4, 192, 128, 128], P('dp', 'space')
- grad_conv_one: float32 [64, 1728], P('dp')
- grad_conv_down: float32 [128, 512], P('dp')
- grad_conv_two: float32 [128, 3456], P('dp')
The draws below stay inside these ranges and needn't reach their ends.
Inputs may be any that keep to these rules, and one draw needn't show every extreme that they name: Patch p sits on device patch_home[p] // 3 of the space axis in slot patch_home[p] % 3; no two patches share a slot; every device holds a run of consecutive patch numbers, the runs in the order of the devices, each of 1 to 3 patches; some device holds exactly 3 and some exactly one. `patch_links`: the patches form a grid of 2 columns and 64 rows, patch 2 r + c in row r and column c; the four entries of a patch name p - 1, p + 1, p - 2, p + 2 or -1 where the grid ends or the link is cut; links are symmetric; the first and the last row are linked across x.
All inputs are finite; a program needn't handle non-finite values.
Results may differ from the reference program's by a relative error of at most 0.014.
Values may be sent and summed in bfloat16 or wider, within the bound.
No kernel may reach another device: no remote copies, remote signals or barrier semaphores. Data moves between devices by JAX's collectives and lax.ppermute only.
A program may use at most 128 MiB of HBM per device.

```python
import jax
import jax.numpy as jnp
from jax import lax

C1 = 64
C2 = 128
PXY = 16
PZ = 4
SLOTS = 3
SLABS = 4
SLOTS_ALL = 192
NP = 128
CELLS = 1024
CELLS_TWO = 128
N_DP = 4
N_SPACE = 64


def draw_patch_home(key, part):
    pair_count = N_SPACE // 2
    first_counts = jax.random.randint(jax.random.fold_in(key, 11), (pair_count,), 1, SLOTS + 1)
    first_counts = first_counts.at[0].set(SLOTS).at[pair_count - 1].set(1)
    counts = jnp.stack([first_counts, SLOTS + 1 - first_counts], axis=1).reshape(N_SPACE)
    starts = jnp.cumsum(counts) - counts
    patch_ids = jnp.arange(NP, dtype=jnp.int32)
    device = jnp.sum((starts[None, :] <= patch_ids[:, None]).astype(jnp.int32), axis=1) - 1
    rank_in = patch_ids - starts[device]
    subkeys = jax.random.split(jax.random.fold_in(key, 12), N_SPACE)
    orders = jax.vmap(lambda subkey: jax.random.permutation(subkey, SLOTS))(subkeys)
    slot_ids = orders[device, rank_in]
    return (device * SLOTS + slot_ids).astype(jnp.int32)


def draw_patch_links(key, part):
    row_count = NP // 2
    cross = jax.random.randint(jax.random.fold_in(key, 21), (row_count,), 0, 4) > 0
    cross = cross.at[0].set(True).at[row_count - 1].set(True)
    upward = jax.random.randint(jax.random.fold_in(key, 22), (row_count - 1, 2), 0, 4) > 0
    none_row = jnp.zeros((1, 2), dtype=jnp.bool_)
    below = jnp.concatenate([none_row, upward], axis=0)
    above = jnp.concatenate([upward, none_row], axis=0)
    row_index = jnp.arange(row_count, dtype=jnp.int32)[:, None]
    column = jnp.arange(2, dtype=jnp.int32)[None, :]
    patch_ids = 2 * row_index + column
    minus_x = jnp.where((column == 1) & cross[:, None], patch_ids - 1, -1)
    plus_x = jnp.where((column == 0) & cross[:, None], patch_ids + 1, -1)
    minus_y = jnp.where(below, patch_ids - 2, -1)
    plus_y = jnp.where(above, patch_ids + 2, -1)
    return jnp.stack([minus_x, plus_x, minus_y, plus_y], axis=-1).reshape(NP, 4).astype(jnp.int32)


def level_of(key, dims, cuts, low, high):
    loudness = 1.0
    for axis_at, parts in cuts:
        steps = jax.random.uniform(jax.random.fold_in(jax.random.fold_in(key, 6), axis_at), (parts,), jnp.float32, low / len(cuts), high / len(cuts))
        loudness = loudness * jnp.repeat(jnp.exp(steps), dims[axis_at] // parts).reshape((-1,) + (1,) * (len(dims) - 1 - axis_at))
    return loudness


def scatter_about(own_key, dims, deviation, reach, cuts=(), kind=jnp.bfloat16):
    array = deviation * jax.random.normal(own_key, dims, jnp.float32)
    if cuts:
        array = array * level_of(own_key, dims, cuts, -0.22, 0.18)
    return jnp.clip(array, -reach, reach).astype(kind)


def setup_inputs(seed: int = 0) -> dict:
    key_of = jax.random.split(jax.random.key(seed), 8)
    return {
        "features": scatter_about(key_of[0], (SLABS, SLOTS_ALL, C1, CELLS), 1.0, 6.0, ((0, 4), (1, 64))),
        "cotangent": scatter_about(key_of[1], (SLABS, SLOTS_ALL, C2, CELLS_TWO), 1.0, 6.0, ((0, 4), (1, 64))),
        "conv_one": scatter_about(key_of[2], (C1, 27 * C1), (27 * C1) ** -0.5, 0.15625, ((0, 4),)),
        "down_weight": scatter_about(key_of[3], (C2, 8 * C1), (8 * C1) ** -0.5, 0.25, ((0, 4),)),
        "conv_two": scatter_about(key_of[4], (C2, 27 * C2), (27 * C2) ** -0.5, 0.109375, ((0, 4),)),
        "patch_home": draw_patch_home(jax.random.fold_in(key_of[7], 71), 0),
        "patch_links": draw_patch_links(jax.random.fold_in(key_of[7], 71), 0),
    }


def slope_of(values):
    logistic = jax.nn.sigmoid(values)
    return logistic * (1.0 + values * (1.0 - logistic))

def neighbour_of(source, linkage, column):
    target = linkage[:, column]
    taken_all = jnp.take(source, jnp.maximum(target, 0), axis=0)
    return jnp.where((target >= 0)[:, None, None, None, None], taken_all, jnp.zeros_like(taken_all))

def assemble(field, linkage):
    lower_rim = neighbour_of(field, linkage, 0)[:, :, -1:]
    upper_rim = neighbour_of(field, linkage, 1)[:, :, :1]
    widened = jnp.concatenate([lower_rim, field, upper_rim], axis=2)
    front_rim = neighbour_of(widened, linkage, 2)[:, :, :, -1:]
    back_rim = neighbour_of(widened, linkage, 3)[:, :, :, :1]
    full_block = jnp.concatenate([front_rim, widened, back_rim], axis=3)
    return jnp.pad(full_block, ((0, 0), (0, 0), (0, 0), (0, 0), (1, 1)))

def convolve(padded, kernel_weight):
    channels = padded.shape[1]
    kernel = kernel_weight.reshape(kernel_weight.shape[0], 3, 3, 3, channels).transpose(0, 4, 1, 2, 3)
    return lax.conv_general_dilated(padded, kernel, (1, 1, 1), 'VALID', dimension_numbers=('NCDHW', 'OIDHW', 'NCDHW'), precision=lax.Precision.HIGHEST)

def coarsen_grid(hidden_state, kernel_weight):
    number, channels, size_x, size_y, size_z = hidden_state.shape
    kernel = kernel_weight.reshape(kernel_weight.shape[0], 2, 2, 2, channels)
    blocks = hidden_state.reshape(number, channels, size_x // 2, 2, size_y // 2, 2, size_z // 2, 2)
    return jnp.einsum('oabcm,nmxaybzc->noxyz', kernel, blocks, precision=lax.Precision.HIGHEST)

def reference(features, cotangent, conv_one, down_weight, conv_two, patch_home, patch_links):
    weight_one = conv_one.astype(jnp.float32)
    coarsen_weight = down_weight.astype(jnp.float32)
    weight_two = conv_two.astype(jnp.float32)
    grad_scale = float(N_DP * NP * (PXY // 2) * (PXY // 2) * (PZ // 2)) ** (-0.5)
    sum_one = jnp.zeros(weight_one.shape, jnp.float32)
    sum_down = jnp.zeros(coarsen_weight.shape, jnp.float32)
    sum_two = jnp.zeros(weight_two.shape, jnp.float32)
    outputs = []
    for slab in range(N_DP):
        patch_field = jnp.take(features[slab], patch_home, axis=0).reshape(NP, C1, PXY, PXY, PZ)
        padded = assemble(patch_field, patch_links).astype(jnp.float32)
        pre_one, back_one = jax.vjp(lambda kernel_weight: convolve(padded, kernel_weight), weight_one)
        hidden_state = jax.nn.silu(pre_one).astype(jnp.bfloat16)
        hidden_state_wide = lax.optimization_barrier(hidden_state).astype(jnp.float32)
        channel_reduced_sum, reverse_downward = jax.vjp(coarsen_grid, hidden_state_wide, coarsen_weight)
        reduced = channel_reduced_sum.astype(jnp.bfloat16)
        reduced_wide = lax.optimization_barrier(reduced).astype(jnp.float32)
        padded_two, back_gather = jax.vjp(lambda values: assemble(values, patch_links), reduced_wide)
        pre_two, back_two = jax.vjp(convolve, padded_two, weight_two)
        activated = jax.nn.silu(pre_two).astype(jnp.bfloat16)
        placed = jnp.zeros((N_SPACE * SLOTS, C2, CELLS_TWO), jnp.bfloat16)
        placed = placed.at[patch_home].set(activated.reshape(NP, C2, CELLS_TWO))
        outputs.append(placed)
        incoming = jnp.take(cotangent[slab], patch_home, axis=0).reshape(pre_two.shape).astype(jnp.float32)
        grad_two = (incoming * slope_of(pre_two) * grad_scale).astype(jnp.bfloat16)
        grad_padded, dw_two = back_two(lax.optimization_barrier(grad_two).astype(jnp.float32))
        grad_reduced_sum, = back_gather(grad_padded)
        grad_reduced = grad_reduced_sum.astype(jnp.bfloat16)
        grad_hidden, dw_down = reverse_downward(lax.optimization_barrier(grad_reduced).astype(jnp.float32))
        grad_one = (grad_hidden * slope_of(pre_one)).astype(jnp.bfloat16)
        dw_one, = back_one(lax.optimization_barrier(grad_one).astype(jnp.float32))
        sum_one = sum_one + dw_one
        sum_down = sum_down + dw_down
        sum_two = sum_two + dw_two
    return (jnp.stack(outputs), sum_one, sum_down, sum_two)
```

```python
import functools
import types

import jax
import jax.numpy as jnp
from jax import lax
from jax.experimental import pallas as pl
from jax.experimental.pallas import tpu as pltpu
from jax.sharding import Mesh
from jax.sharding import PartitionSpec as P

BF = jnp.bfloat16
F32 = jnp.float32
SPACE = ("x", "zh", "y", "core")
NCHIP = 32
ONE = types.SimpleNamespace(C=64, g=64, R=256, N=1024, W=1152, zs=4, nx=16)
TWO = types.SimpleNamespace(C=128, g=16, R=128, N=128, W=256, zs=2, nx=8)
NOWHERE = -8192


def mm(a, b, contract=((1,), (0,))):
    return lax.dot_general(a, b, (contract, ((), ())), preferred_element_type=F32)


NT = ((1,), (1,))
TN = ((0,), (0,))


def one_hot(shape, rule):
    r = lax.broadcasted_iota(jnp.int32, shape, 0)
    l = lax.broadcasted_iota(jnp.int32, shape, 1)
    return jnp.where(rule(r, l), 1.0, 0.0).astype(BF)


def picker(level, off, dst):
    return one_hot(
        (level.R, 128),
        lambda r, l: (r - off == l - dst) & (l >= dst) & (l < dst + level.g),
    )


def corner_picker(level, off, xc):
    g, zs = level.g, level.zs
    return one_hot(
        (level.R, 128),
        lambda r, l: (r - off == l - g) & (l >= g) & (l < 2 * g) & ((l - g) // zs == xc),
    )


def rim_rows(level, y_off):
    g, zs, N, W, nx = level.g, level.zs, level.N, level.W, level.nx

    def rule(r, l):
        face = (r < g) & (l == (r // zs) * g + r % zs + y_off)
        q = r - g
        low = (q >= 0) & (q < zs) & (l == N + q + y_off)
        high = (q >= g - zs) & (q < g) & (l == W - g + q - (g - zs) + y_off)
        return face | low | high

    return one_hot((128, W), rule)


def where_am_i(sc):
    core = sc[6]
    s = types.SimpleNamespace(core=core, dev=sc[5])
    n0, n1 = sc[2] - sc[1], sc[3] - sc[2]
    s.n0 = n0
    s.total = n0 + n1
    s.start = sc[1]
    s.a = jnp.where(core == 0, sc[1], sc[2])
    s.n = jnp.where(core == 0, n0, n1)
    s.other = jnp.where(core == 0, n1, n0)
    s.chip_before = sc[1] - sc[0]
    s.chip_after = sc[4] - sc[3]
    return s


def locate(s, q, up, level, sub):
    g = level.g
    rec_off = jnp.int32(0 if up else g)
    own = (q >= s.a) & (q < s.a + s.n)
    if up:
        k = s.a - q
        near = jnp.where(s.core == 1, s.other, 0)
        o_idx = 3 + s.other - k
        m_idx = jnp.where(s.core == 0, 6, 8)
        chip = s.chip_before
    else:
        k = q - (s.a + s.n) + 1
        near = jnp.where(s.core == 0, s.other, 0)
        o_idx = 3 + k - 1
        m_idx = jnp.where(s.core == 0, 8, 6)
        chip = s.chip_after
    t = k - near
    in_o = k <= near
    far = t > chip
    idx = jnp.where(own, q - s.a, jnp.where(in_o, o_idx, jnp.where(far, m_idx + 1, m_idx)))
    in_rec = own | in_o
    main = jnp.where(in_rec, rec_off, jnp.where(far, 0, sub * (t - 1) * g))
    corner = jnp.where(in_rec, 3 * g if up else 4 * g, main + g) if sub == 2 else main
    return jnp.clip(idx, 0, 9), main, corner


def locate_x(s, q, level, sub):
    g = level.g
    rec_off = jnp.where(q % 2 == 0, 3 * g, 2 * g) if sub == 1 else jnp.int32(2 * g)
    msg_off = 3 * g if sub == 1 else 6 * g
    own = (q >= s.a) & (q < s.a + s.n)
    before = q < s.a
    in_o = jnp.where(before, s.core == 1, s.core == 0)
    o_idx = jnp.where(before, 3 + s.other - 1, 3)
    m_idx = jnp.where(before == (s.core == 0), 6, 8)
    idx = jnp.where(own, q - s.a, jnp.where(in_o, o_idx, m_idx))
    return jnp.clip(idx, 0, 9), jnp.where(own | in_o, rec_off, msg_off)


def gather_records(recs, own, other, got, swapped):
    for k in range(3):
        recs[k] = own[k]
        recs[3 + k] = other[k]
    for k in range(2):
        recs[6 + k] = got[k][...]
        recs[8 + k] = swapped[k][...]


def link_at(links, q, column):
    return links[jnp.clip(q, 0, 127) * 4 + column]


def x_link(links, q):
    return link_at(links, q, jnp.where(q % 2 == 0, 1, 0))


def extended(level, s, links, recs, rows, field, p):
    even = p % 2 == 0
    partner = jnp.where(even, p + 1, p - 1)
    idx, off = locate_x(s, partner, level, 1)
    off = jnp.where(x_link(links, p) >= 0, off, NOWHERE)
    rim = mm(recs[idx], picker(level, off, jnp.where(even, 0, 128 - level.g)))
    block = jnp.concatenate([field, rim], axis=1)
    rims = []
    for side, up in ((0, True), (1, False)):
        q = p - 2 if up else p + 2
        c = jnp.where(even, q + 1, q - 1)
        ok = link_at(links, p, 2 + side) >= 0
        idx, off, _ = locate(s, q, up, level, 1)
        face = mm(recs[idx], picker(level, jnp.where(ok, off, NOWHERE), 0))
        ok_c = ok & (x_link(links, q) >= 0)
        idx, off, _ = locate(s, c, up, level, 1)
        xc = jnp.where(even, 0, level.nx - 1)
        face += mm(recs[idx], corner_picker(level, jnp.where(ok_c, off, NOWHERE), xc))
        rims.append(mm(face.astype(BF), rows[side]))
    return block, rims[0], rims[1]


def coords(level):
    lane = lax.broadcasted_iota(jnp.int32, (level.C, level.W), 1)
    return (lane % level.g) // level.zs, lane % level.zs


def tap_rows(level, block, low, high, store):
    W, zs = level.W, level.zs
    y, z = coords(level)
    for dy in (-1, 0, 1):
        if dy == 0:
            f = block
        elif dy == -1:
            f = jnp.where(y == 0, low, pltpu.roll(block, zs, 1))
        else:
            f = jnp.where(y == level.nx - 1, high, pltpu.roll(block, W - zs, 1))
        for dz in (-1, 0, 1):
            if dz == 0:
                v = f
            elif dz == -1:
                v = jnp.where(z == 0, 0.0, pltpu.roll(f, 1, 1))
            else:
                v = jnp.where(z == zs - 1, 0.0, pltpu.roll(f, W - 1, 1))
            store(3 * (dy + 1) + dz + 1, v.astype(BF))


def three_shifts(level, y):
    C, W, g = level.C, level.W, level.g
    total = pltpu.roll(y[:C], g, 1) + y[C : 2 * C] + pltpu.roll(y[2 * C :], W - g, 1)
    return total[:, : level.N]


def parity_order():
    def rule(r, l):
        y, z = (r % 64) // 4, r % 4
        e = 4 * (r // 64) + 2 * (y % 2) + z % 2
        return l == e * 16 + (y // 2) * 2 + z // 2

    return one_hot((128, 128), rule)


def swap_groups(arrays):
    group = lax.broadcasted_iota(jnp.int32, (64, 128), 1) // 16
    arrays = list(arrays)
    for b in (1, 2, 4):
        bit = (group & b) != 0
        for i in range(8):
            if i & b:
                continue
            lo, hi = arrays[i], arrays[i + b]
            arrays[i] = jnp.where(bit, pltpu.roll(hi, 16 * b, 1), lo)
            arrays[i + b] = jnp.where(bit, hi, pltpu.roll(lo, 128 - 16 * b, 1))
    return arrays


def faces_kernel(sc, home, x_ref, rec_ref):
    s = where_am_i(sc)

    def rule(r, l):
        group, m = l // 64, l % 64
        high = (group == 0) & (r == (m // 4) * 64 + 60 + m % 4)
        low = (group == 1) & (r == (m // 4) * 64 + m % 4)
        return high | low | ((group == 2) & (r == m)) | ((group == 3) & (r == 960 + m))

    pick = one_hot((1024, 256), rule)
    for i in range(3):
        p = s.a + jnp.minimum(i, s.n - 1)
        slot = home[p] - 3 * s.dev
        rec_ref[i] = mm(x_ref[slot], pick).astype(BF)


def message_kernel(level, sub, sc, own, other, out, both):
    s = where_am_i(sc)
    g = level.g
    for k in range(3):
        both[k] = own[k]
        both[3 + k] = other[k]
    up = s.core == 0
    main = jnp.where(up, 0, g)
    corner = jnp.where(up, 3 * g, 4 * g)
    total = None
    for k in range(3):
        t = jnp.maximum(jnp.where(up, s.total - 1 - k, k), 0)
        t = jnp.minimum(t, s.total - 1)
        first = t < s.n0
        mine = first == (s.core == 0)
        idx = jnp.where(first, t, t - s.n0) + jnp.where(mine, 0, 3)
        q = s.start + t
        base = sub * k * g

        def rule(r, l):
            hit = (r - main == l - base) & (l >= base) & (l < base + g)
            if sub == 2:
                c = base + g
                hit |= (r - corner == l - c) & (l >= c) & (l < c + g)
            if k == 0:
                to = 3 * g if sub == 1 else 6 * g
                src = jnp.where(q % 2 == 0, 3 * g, 2 * g) if sub == 1 else 2 * g
                hit |= (r - src == l - to) & (l >= to) & (l < to + g)
            return hit

        part = mm(both[idx], one_hot((level.R, level.R), rule))
        total = part if total is None else total + part
    out[...] = total.astype(BF)


def stage_one_kernel(sc, home, links, x_ref, own, other, got1, got2, sw1, sw2, w_a, w_b, w_c, w_d,
                     d_a, d_b, d_c, d_d, taps, hid, slope, red, rec2, down_out,
                     recs, low_rows, high_rows, w_all, d_all, w_one):
    s = where_am_i(sc)
    dp = sc[7]
    gather_records(recs, own, other, (got1, got2), (sw1, sw2))
    low_rows[...] = rim_rows(ONE, 0)
    high_rows[...] = rim_rows(ONE, 60)
    for k, (w, d) in enumerate(((w_a, d_a), (w_b, d_b), (w_c, d_c), (w_d, d_d))):
        w_all[k] = w[...]
        d_all[k] = d[...]
    for d in range(4):
        at = jnp.bitwise_xor(jnp.int32(d), dp)
        for dx in range(3):
            w_one[dx * 64 + d * 16 : dx * 64 + d * 16 + 16, :] = w_all[at, dx]
        down_out[d * 32 : d * 32 + 32, :] = d_all[at]
    order = parity_order()
    for i in range(3):
        p = s.a + jnp.minimum(i, s.n - 1)
        slot = home[p] - 3 * s.dev
        block, low, high = extended(
            ONE, s, links, recs, (low_rows[...], high_rows[...]), x_ref[slot].astype(F32), p
        )

        def store(t, v):
            taps[i, t * 64 : t * 64 + 64, :] = v

        tap_rows(ONE, block, low, high, store)
        taps[i, 576:640, :] = jnp.zeros((64, 1152), BF)
        pre = three_shifts(ONE, mm(w_one[...], taps[i, 0:576, :]))
        tall = jnp.concatenate([pre[:, 128 * b : 128 * b + 128] for b in range(8)], axis=0)
        top = tall.astype(BF)
        rest = (tall - top.astype(F32)).astype(BF)
        tall = mm(top, order) + mm(rest, order)
        parts = swap_groups([tall[64 * b : 64 * b + 64] for b in range(8)])
        for e in range(8):
            v = parts[e]
            sig = 1.0 / (1.0 + jnp.exp(-v))
            hid[e * 64 : e * 64 + 64, i * 128 : i * 128 + 128] = (v * sig).astype(BF)
            slope[e * 64 : e * 64 + 64, i * 128 : i * 128 + 128] = sig * (1.0 + v * (1.0 - sig))
    red[...] = mm(down_out[...], hid[...]).astype(BF)

    def rule(r, l):
        group, m = l // 16, l % 16
        high = (group == 0) & (r == (m // 2) * 16 + 14 + m % 2)
        low = (group == 1) & (r == (m // 2) * 16 + m % 2)
        return high | low | ((group == 2) & (r == m)) | ((group == 3) & (r == 112 + m))

    pick = one_hot((128, 128), rule)
    for i in range(3):
        rec2[i] = mm(red[:, i * 128 : i * 128 + 128], pick).astype(BF)


def stage_two_kernel(scale, sc, home, links, red, cot, own, other, got1, got2, sw1, sw2,
                     w_a, w_b, w_c, w_d, out, dw, grad, brec,
                     recs, low_rows, high_rows, w_all, w_two, taps, spread):
    s = where_am_i(sc)
    dp = sc[7]
    gather_records(recs, own, other, (got1, got2), (sw1, sw2))
    low_rows[...] = rim_rows(TWO, 0)
    high_rows[...] = rim_rows(TWO, 14)
    for k, w in enumerate((w_a, w_b, w_c, w_d)):
        w_all[k] = w[...]
    for d in range(4):
        at = jnp.bitwise_xor(jnp.int32(d), dp)
        for dx in range(3):
            w_two[dx * 128 + d * 32 : dx * 128 + d * 32 + 32, :] = w_all[
                at, :, dx * 1152 : dx * 1152 + 1152
            ]
    for i in range(3):
        p = s.a + jnp.minimum(i, s.n - 1)
        block, low, high = extended(
            TWO, s, links, recs, (low_rows[...], high_rows[...]),
            red[:, i * 128 : i * 128 + 128].astype(F32), p,
        )

        def store(t, v):
            taps[t * 128 : t * 128 + 128, i * 256 : i * 256 + 256] = v

        tap_rows(TWO, block, low, high, store)
    y = mm(w_two[...], taps[...])
    out[...] = jnp.zeros_like(out)
    for i in range(3):
        p = s.a + jnp.minimum(i, s.n - 1)
        slot = home[p] - 3 * s.dev
        v = three_shifts(TWO, y[:, i * 256 : i * 256 + 256])
        sig = 1.0 / (1.0 + jnp.exp(-v))

        @pl.when(i < s.n)
        def _():
            out[slot] = (v * sig).astype(BF)

        g = cot[slot].astype(F32) * (sig * (1.0 + v * (1.0 - sig))) * scale
        g = jnp.where(i < s.n, g, 0.0).astype(BF).astype(F32)
        g = jnp.concatenate([g, jnp.zeros_like(g)], axis=1)
        for dx in (-1, 0, 1):
            w = g if dx == 0 else pltpu.roll(g, (dx * 16) % 256, 1)
            spread[(dx + 1) * 128 : (dx + 2) * 128, i * 256 : i * 256 + 256] = w.astype(BF)
    dw[...] = mm(spread[...], taps[...], NT)
    back = mm(w_two[...], spread[...], TN)
    yy, zz = coords(TWO)
    for i in range(3):
        p = s.a + jnp.minimum(i, s.n - 1)
        even = p % 2 == 0
        by_dy = []
        for dy in range(3):
            total = None
            for dz in (-1, 0, 1):
                t = 3 * dy + dz + 1
                v = back[t * 128 : t * 128 + 128, i * 256 : i * 256 + 256]
                if dz == -1:
                    v = pltpu.roll(jnp.where(zz == 0, 0.0, v), 255, 1)
                elif dz == 1:
                    v = pltpu.roll(jnp.where(zz == 1, 0.0, v), 1, 1)
                total = v if total is None else total + v
            by_dy.append(total)
        mid = (
            by_dy[1]
            + pltpu.roll(jnp.where(yy == 0, 0.0, by_dy[0]), 254, 1)
            + pltpu.roll(jnp.where(yy == 7, 0.0, by_dy[2]), 2, 1)
        )
        grad[:, i * 128 : i * 128 + 128] = mid[:, :128]
        rim_low = mm(by_dy[0].astype(BF), low_rows[...], NT).astype(BF)
        rim_high = mm(by_dy[2].astype(BF), high_rows[...], NT).astype(BF)
        xc = jnp.where(even, 0, 7)

        def side(main_to, corner_to):
            def rule(r, l):
                main = (l >= main_to) & (l < main_to + 16) & (r == l - main_to)
                m = l - corner_to
                return main | ((m >= 0) & (m < 16) & (r - 16 == m) & (m // 2 == xc))

            return one_hot((128, 128), rule)

        x_off = jnp.where(even, 0, 112)
        x_pick = one_hot((128, 128), lambda r, l: (l >= 32) & (l < 48) & (r - x_off == l - 32))
        brec[i] = (
            mm(rim_high, side(0, 48))
            + mm(rim_low, side(16, 64))
            + mm(mid[:, 128:].astype(BF), x_pick)
        ).astype(BF)


def stage_three_kernel(sc, links, grad, own, other, got1, got2, sw1, sw2, down, hid, slope, taps,
                       out, recs, gred, g_one, spread):
    s = where_am_i(sc)
    gather_records(recs, own, other, (got1, got2), (sw1, sw2))

    def rows(y_off):
        return one_hot(
            (128, 128), lambda r, l: (r < 32) & (l == ((r % 16) // 2) * 16 + r % 2 + y_off)
        )

    side_rows = (rows(0), rows(14))
    for i in range(3):
        p = s.a + jnp.minimum(i, s.n - 1)
        even = p % 2 == 0
        partner = jnp.where(even, p + 1, p - 1)
        ok_x = x_link(links, p) >= 0
        idx, off = locate_x(s, partner, TWO, 2)
        off = jnp.where(ok_x, off, NOWHERE)
        total = grad[:, i * 128 : i * 128 + 128] + mm(
            recs[idx], picker(TWO, off, jnp.where(even, 112, 0))
        )
        for side, up in ((0, True), (1, False)):
            q = p - 2 if up else p + 2
            c = partner - 2 if up else partner + 2
            ok = link_at(links, p, 2 + side) >= 0
            idx, off, _ = locate(s, q, up, TWO, 2)
            face = mm(recs[idx], picker(TWO, jnp.where(ok, off, NOWHERE), 0))
            ok_c = ok_x & (link_at(links, partner, 2 + side) >= 0)
            idx, _, off = locate(s, c, up, TWO, 2)
            face += mm(recs[idx], picker(TWO, jnp.where(ok_c, off, NOWHERE), 16))
            total += mm(face.astype(BF), side_rows[side])
        gred[:, i * 128 : i * 128 + 128] = jnp.where(i < s.n, total, 0.0).astype(BF)
    dw_down = mm(gred[...], hid[...], NT)
    g_one[...] = (mm(down[...], gred[...], TN) * slope[...]).astype(BF)
    order = parity_order()
    dw = None
    for i in range(3):
        parts = [
            g_one[e * 64 : e * 64 + 64, i * 128 : i * 128 + 128].astype(F32) for e in range(8)
        ]
        tall = jnp.concatenate(swap_groups(parts), axis=0).astype(BF)
        tall = mm(tall, order, NT)
        g = jnp.concatenate(
            [tall[64 * b : 64 * b + 64] for b in range(8)] + [jnp.zeros((64, 128), F32)], axis=1
        )
        for dx in (-1, 0, 1):
            w = g if dx == 0 else pltpu.roll(g, (dx * 64) % 1152, 1)
            spread[(dx + 1) * 64 : (dx + 2) * 64, :] = w.astype(BF)
        part = mm(spread[...], taps[i], NT)
        dw = part if dw is None else dw + part
    out[...] = jnp.zeros_like(out)
    for d in range(4):
        for h in range(2):
            for dx in range(3):
                at = dx * 64 + d * 16 + h * 8
                out[d, h, dx * 8 : dx * 8 + 8, :] = dw[at : at + 8]
            at = d * 32 + h * 16
            out[d, h, 24:40, 0:512] = dw_down[at : at + 16]


def final_kernel(sc, two_own, two_other, small_own, small_other, one_out, down_out, two_out):
    core = sc[6]
    lane = lax.broadcasted_iota(jnp.int32, (8, 128), 1)
    for h in range(2):
        mine = core == h
        two = jnp.where(mine, two_own[...].astype(F32), two_other[...].astype(F32))
        small = jnp.where(mine, small_own[...].astype(F32), small_other[...].astype(F32))
        for dx in range(3):
            two_out[h * 16 : h * 16 + 16, dx * 1152 : dx * 1152 + 1152] = two[dx]
        down_out[h * 16 : h * 16 + 16, :] = small[24:40, :512]
        first, last = small[0:8], small[16:24]
        middle = pltpu.roll(small[8:16], 64, 1)
        one_out[h * 8 : h * 8 + 8, 0:512] = first[:, :512]
        one_out[h * 8 : h * 8 + 8, 512:640] = jnp.where(lane < 64, first[:, 512:], middle[:, :128])
        one_out[h * 8 : h * 8 + 8, 640:1152] = middle[:, 128:]
        one_out[h * 8 : h * 8 + 8, 1152:1728] = last[:, :576]


def call(kernel, scalars, arrays, outs, scratch, name):
    smem = pl.BlockSpec(memory_space=pltpu.SMEM)
    vmem = pl.BlockSpec(memory_space=pltpu.VMEM)
    return pl.pallas_call(
        kernel,
        out_shape=[jax.ShapeDtypeStruct(*o) for o in outs],
        in_specs=[smem] * len(scalars) + [vmem] * len(arrays),
        out_specs=[vmem] * len(outs),
        scratch_shapes=[pltpu.VMEM(*t) for t in scratch],
        compiler_params=pltpu.CompilerParams(vmem_limit_bytes=60 << 20),
        name=name,
    )(*scalars, *arrays)


def swap_cores(v):
    return lax.ppermute(v, "core", [(0, 1), (1, 0)])


def chips_on(v, by):
    up = [(2 * c, 2 * (c + by)) for c in range(NCHIP - by)]
    down = [(2 * c + 1, 2 * (c - by) + 1) for c in range(by, NCHIP)]
    return lax.ppermute(v, SPACE, up + down)


def across(v, axis, k):
    return lax.ppermute(v, axis, [(i, i ^ k) for i in range(lax.axis_size(axis))])


def exchange(level, sub, sc, own):
    other = swap_cores(own)
    (message,) = call(
        functools.partial(message_kernel, level, sub), (sc,), (own, other),
        [((level.C, level.R), BF)], [((6, level.C, level.R), BF)], "message",
    )
    got1, got2 = chips_on(message, 1), chips_on(message, 2)
    return other, got1, got2, swap_cores(got1), swap_cores(got2)


def gathered(shard):
    return [shard] + [across(shard, "dp", k) for k in (1, 2, 3)]


def total_of(parts, dp_axis, core, dp):
    half = dp_axis + 1
    keep = lax.dynamic_index_in_dim(parts, core, half, keepdims=False)
    give = lax.dynamic_index_in_dim(parts, 1 - core, half, keepdims=False)
    kept = keep + swap_cores(give.astype(BF)).astype(F32)

    def block(d):
        return lax.dynamic_index_in_dim(kept, d, dp_axis, keepdims=False)

    got = [across(block(dp ^ k).astype(BF), "dp", k).astype(F32) for k in (1, 2, 3)]
    value = (block(dp) + got[0] + (got[1] + got[2])).astype(BF)
    for axis in ("y", "x"):
        got = [across(value, axis, k).astype(F32) for k in (1, 2, 3)]
        value = ((value.astype(F32) + got[0]) + (got[1] + got[2])).astype(BF)
    return (value.astype(F32) + across(value, "zh", 1).astype(F32)).astype(BF)


def on_device(features, cotangent, conv_one, down_weight, conv_two, patch_home, patch_links):
    core, dp = lax.axis_index("core"), lax.axis_index("dp")
    dev = lax.axis_index(SPACE)
    chip = dev // 2
    slots = jnp.arange(8, dtype=jnp.int32)
    marks = jnp.where(slots == 0, -2, jnp.where(slots == 4, 4, slots - 1))
    starts = jnp.sum(
        (patch_home[None, :] < 3 * (2 * chip + marks)[:, None]).astype(jnp.int32), axis=1
    )
    sc = jnp.where(
        slots < 5, starts, jnp.where(slots == 5, dev, jnp.where(slots == 6, core, dp))
    ).astype(jnp.int32)
    links = patch_links.reshape(-1)
    x = features[0]
    (rec_one,) = call(faces_kernel, (sc, patch_home), (x,), [((3, 64, 256), BF)], [], "faces")
    rims_one = exchange(ONE, 1, sc, rec_one)
    w_one = gathered(conv_one.reshape(16, 3, 576).swapaxes(0, 1))
    w_down = gathered(down_weight)
    w_two = gathered(conv_two)
    taps, hid, slope, red, rec_two, down_full = call(
        stage_one_kernel, (sc, patch_home, links),
        (x, rec_one, *rims_one, *w_one, *w_down),
        [((3, 640, 1152), BF), ((512, 384), BF), ((512, 384), F32), ((128, 384), BF),
         ((3, 128, 128), BF), ((128, 512), BF)],
        [((10, 64, 256), BF), ((128, 1152), BF), ((128, 1152), BF), ((4, 3, 16, 576), BF),
         ((4, 32, 512), BF), ((192, 576), BF)],
        "stage_one",
    )
    rims_two = exchange(TWO, 1, sc, rec_two)
    cells = lax.axis_size("dp") * patch_links.shape[0] * 128
    out, dw_two, grad, rec_back = call(
        functools.partial(stage_two_kernel, float(cells) ** (-0.5)), (sc, patch_home, links),
        (red, cotangent[0], rec_two, *rims_two, *w_two),
        [((3, 128, 128), BF), ((384, 1152), F32), ((128, 384), F32), ((3, 128, 128), BF)],
        [((10, 128, 128), BF), ((128, 256), BF), ((128, 256), BF), ((4, 32, 3456), BF),
         ((384, 1152), BF), ((1152, 768), BF), ((384, 768), BF)],
        "stage_two",
    )
    rims_back = exchange(TWO, 2, sc, rec_back)
    two_half = total_of(dw_two.reshape(3, 4, 2, 16, 1152), 1, core, dp)
    (small,) = call(
        stage_three_kernel, (sc, links),
        (grad, rec_back, *rims_back, down_full, hid, slope, taps),
        [((4, 2, 40, 640), F32)],
        [((10, 128, 128), BF), ((128, 384), BF), ((512, 384), BF), ((192, 1152), BF)],
        "stage_three",
    )
    small_half = total_of(small, 0, core, dp)
    grads = call(
        final_kernel, (sc,), (two_half, swap_cores(two_half), small_half, swap_cores(small_half)),
        [((16, 1728), F32), ((32, 512), F32), ((32, 3456), F32)], [], "final",
    )
    return (out[None], *grads)


def solution(mesh):
    split = Mesh(
        mesh.devices.reshape(mesh.shape["dp"], 4, 2, 4, 2), ("dp", "x", "zh", "y", "core")
    )
    return jax.shard_map(
        on_device,
        mesh=split,
        in_specs=(
            P("dp", SPACE, None, None),
            P("dp", SPACE, None, None),
            P("dp", None),
            P("dp", None),
            P("dp", None),
            P(),
            P(),
        ),
        out_specs=(P("dp", SPACE, None, None), P("dp", None), P("dp", None), P("dp", None)),
        check_vma=False,
    )
```

```python
import functools
import types

import jax
import jax.numpy as jnp
from jax import lax
from jax.experimental import pallas as pl
from jax.experimental.pallas import tpu as pltpu
from jax.sharding import Mesh
from jax.sharding import PartitionSpec as P


BF = jnp.bfloat16
F32 = jnp.float32
SPACE = ("x", "zh", "y", "core")
NCHIP = 32
ONE = types.SimpleNamespace(C=64, g=64, R=256, N=1024, W=1152, zs=4, nx=16)
TWO = types.SimpleNamespace(C=128, g=16, R=128, N=128, W=256, zs=2, nx=8)
NOWHERE = -8192


def mm(a, b, contract=((1,), (0,))):
    return lax.dot_general(a, b, (contract, ((), ())), preferred_element_type=F32)


NT = ((1,), (1,))
TN = ((0,), (0,))


def one_hot(shape, rule):
    r = lax.broadcasted_iota(jnp.int32, shape, 0)
    l = lax.broadcasted_iota(jnp.int32, shape, 1)
    return jnp.where(rule(r, l), 1.0, 0.0).astype(BF)


def picker(level, off, dst):
    return one_hot(
        (level.R, 128),
        lambda r, l: (r - off == l - dst) & (l >= dst) & (l < dst + level.g),
    )


def corner_picker(level, off, xc):
    g, zs = level.g, level.zs
    return one_hot(
        (level.R, 128),
        lambda r, l: (r - off == l - g) & (l >= g) & (l < 2 * g) & ((l - g) // zs == xc),
    )


def rim_rows(level, y_off):
    g, zs, N, W = level.g, level.zs, level.N, level.W

    def rule(r, l):
        face = (r < g) & (l == (r // zs) * g + r % zs + y_off)
        q = r - g
        low = (q >= 0) & (q < zs) & (l == N + q + y_off)
        high = (q >= g - zs) & (q < g) & (l == W - g + q - (g - zs) + y_off)
        return face | low | high

    return one_hot((128, W), rule)


def where_am_i(sc):
    core = sc[6]
    s = types.SimpleNamespace(core=core, dev=sc[5])
    n0, n1 = sc[2] - sc[1], sc[3] - sc[2]
    s.n0 = n0
    s.total = n0 + n1
    s.start = sc[1]
    s.a = jnp.where(core == 0, sc[1], sc[2])
    s.n = jnp.where(core == 0, n0, n1)
    s.other = jnp.where(core == 0, n1, n0)
    s.chip_before = sc[1] - sc[0]
    s.chip_after = sc[4] - sc[3]
    return s


def locate(s, q, up, level, sub):
    g = level.g
    rec_off = jnp.int32(0 if up else g)
    own = (q >= s.a) & (q < s.a + s.n)
    if up:
        k = s.a - q
        near = jnp.where(s.core == 1, s.other, 0)
        o_idx = 3 + s.other - k
        m_idx = jnp.where(s.core == 0, 6, 8)
        chip = s.chip_before
    else:
        k = q - (s.a + s.n) + 1
        near = jnp.where(s.core == 0, s.other, 0)
        o_idx = 3 + k - 1
        m_idx = jnp.where(s.core == 0, 8, 6)
        chip = s.chip_after
    t = k - near
    in_o = k <= near
    far = t > chip
    idx = jnp.where(own, q - s.a, jnp.where(in_o, o_idx, jnp.where(far, m_idx + 1, m_idx)))
    in_rec = own | in_o
    main = jnp.where(in_rec, rec_off, jnp.where(far, 0, sub * (t - 1) * g))
    corner = jnp.where(in_rec, 3 * g if up else 4 * g, main + g) if sub == 2 else main
    return jnp.clip(idx, 0, 9), main, corner


def locate_x(s, q, level, sub):
    g = level.g
    rec_off = jnp.where(q % 2 == 0, 3 * g, 2 * g) if sub == 1 else jnp.int32(2 * g)
    msg_off = 3 * g if sub == 1 else 6 * g
    own = (q >= s.a) & (q < s.a + s.n)
    before = q < s.a
    in_o = jnp.where(before, s.core == 1, s.core == 0)
    o_idx = jnp.where(before, 3 + s.other - 1, 3)
    m_idx = jnp.where(before == (s.core == 0), 6, 8)
    idx = jnp.where(own, q - s.a, jnp.where(in_o, o_idx, m_idx))
    return jnp.clip(idx, 0, 9), jnp.where(own | in_o, rec_off, msg_off)


def gather_records(recs, own, other, got, swapped):
    for k in range(3):
        recs[k] = own[k]
        recs[3 + k] = other[k]
    for k in range(2):
        recs[6 + k] = got[k][...]
        recs[8 + k] = swapped[k][...]


def link_at(links, q, column):
    return links[jnp.clip(q, 0, 127) * 4 + column]


def x_link(links, q):
    return link_at(links, q, jnp.where(q % 2 == 0, 1, 0))


def extended(level, s, links, recs, rows, field, p):
    even = p % 2 == 0
    partner = jnp.where(even, p + 1, p - 1)
    idx, off = locate_x(s, partner, level, 1)
    off = jnp.where(x_link(links, p) >= 0, off, NOWHERE)
    rim = mm(recs[idx], picker(level, off, jnp.where(even, 0, 128 - level.g)))
    block = jnp.concatenate([field, rim], axis=1)
    rims = []
    for side, up in ((0, True), (1, False)):
        q = p - 2 if up else p + 2
        c = jnp.where(even, q + 1, q - 1)
        ok = link_at(links, p, 2 + side) >= 0
        idx, off, _ = locate(s, q, up, level, 1)
        face = mm(recs[idx], picker(level, jnp.where(ok, off, NOWHERE), 0))
        ok_c = ok & (x_link(links, q) >= 0)
        idx, off, _ = locate(s, c, up, level, 1)
        xc = jnp.where(even, 0, level.nx - 1)
        face += mm(recs[idx], corner_picker(level, jnp.where(ok_c, off, NOWHERE), xc))
        rims.append(mm(face.astype(BF), rows[side]))
    return block, rims[0], rims[1]


def coords(level):
    lane = lax.broadcasted_iota(jnp.int32, (level.C, level.W), 1)
    return (lane % level.g) // level.zs, lane % level.zs


def tap_rows(level, block, low, high, store):
    W, zs = level.W, level.zs
    y, z = coords(level)
    for dy in (-1, 0, 1):
        if dy == 0:
            f = block
        elif dy == -1:
            f = jnp.where(y == 0, low, pltpu.roll(block, zs, 1))
        else:
            f = jnp.where(y == level.nx - 1, high, pltpu.roll(block, W - zs, 1))
        for dz in (-1, 0, 1):
            if dz == 0:
                v = f
            elif dz == -1:
                v = jnp.where(z == 0, 0.0, pltpu.roll(f, 1, 1))
            else:
                v = jnp.where(z == zs - 1, 0.0, pltpu.roll(f, W - 1, 1))
            store(3 * (dy + 1) + dz + 1, v.astype(BF))


def three_shifts(level, y):
    C, W, g = level.C, level.W, level.g
    total = pltpu.roll(y[:C], g, 1) + y[C : 2 * C] + pltpu.roll(y[2 * C :], W - g, 1)
    return total[:, : level.N]


def parity_order():
    def rule(r, l):
        y, z = (r % 64) // 4, r % 4
        e = 4 * (r // 64) + 2 * (y % 2) + z % 2
        return l == e * 16 + (y // 2) * 2 + z // 2

    return one_hot((128, 128), rule)


def swap_groups(arrays):
    group = lax.broadcasted_iota(jnp.int32, (64, 128), 1) // 16
    arrays = list(arrays)
    for b in (1, 2, 4):
        bit = (group & b) != 0
        for i in range(8):
            if i & b:
                continue
            lo, hi = arrays[i], arrays[i + b]
            arrays[i] = jnp.where(bit, pltpu.roll(hi, 16 * b, 1), lo)
            arrays[i + b] = jnp.where(bit, hi, pltpu.roll(lo, 128 - 16 * b, 1))
    return arrays


def faces_kernel(sc, home, x_ref, rec_ref):
    s = where_am_i(sc)

    def rule(r, l):
        group, m = l // 64, l % 64
        high = (group == 0) & (r == (m // 4) * 64 + 60 + m % 4)
        low = (group == 1) & (r == (m // 4) * 64 + m % 4)
        return high | low | ((group == 2) & (r == m)) | ((group == 3) & (r == 960 + m))

    pick = one_hot((1024, 256), rule)
    for i in range(3):
        p = s.a + jnp.minimum(i, s.n - 1)
        slot = home[p] - 3 * s.dev
        rec_ref[i] = mm(x_ref[slot], pick).astype(BF)


def message_kernel(level, sub, sc, own, other, out, both):
    s = where_am_i(sc)
    g = level.g
    for k in range(3):
        both[k] = own[k]
        both[3 + k] = other[k]
    up = s.core == 0
    main = jnp.where(up, 0, g)
    corner = jnp.where(up, 3 * g, 4 * g)
    total = None
    for k in range(3):
        t = jnp.maximum(jnp.where(up, s.total - 1 - k, k), 0)
        t = jnp.minimum(t, s.total - 1)
        first = t < s.n0
        mine = first == (s.core == 0)
        idx = jnp.where(first, t, t - s.n0) + jnp.where(mine, 0, 3)
        q = s.start + t
        base = sub * k * g

        def rule(r, l):
            hit = (r - main == l - base) & (l >= base) & (l < base + g)
            if sub == 2:
                c = base + g
                hit |= (r - corner == l - c) & (l >= c) & (l < c + g)
            if k == 0:
                to = 3 * g if sub == 1 else 6 * g
                src = jnp.where(q % 2 == 0, 3 * g, 2 * g) if sub == 1 else 2 * g
                hit |= (r - src == l - to) & (l >= to) & (l < to + g)
            return hit

        part = mm(both[idx], one_hot((level.R, level.R), rule))
        total = part if total is None else total + part
    out[...] = total.astype(BF)


def stage_one_kernel(sc, home, links, x_ref, own, other, got1, got2, sw1, sw2, w_a, w_b, w_c, w_d,
                     taps, hid, slope, red, rec2, down_out,
                     recs, low_rows, high_rows, w_all, w_one):
    s = where_am_i(sc)
    dp = sc[7]
    gather_records(recs, own, other, (got1, got2), (sw1, sw2))
    low_rows[...] = rim_rows(ONE, 0)
    high_rows[...] = rim_rows(ONE, 60)
    for k, w in enumerate((w_a, w_b, w_c, w_d)):
        w_all[k] = w[...]
    for d in range(4):
        at = jnp.bitwise_xor(jnp.int32(d), dp)
        for dx in range(3):
            w_one[dx * 64 + d * 16 : dx * 64 + d * 16 + 16, :] = w_all[
                at, dx * 16 : dx * 16 + 16, 0:576
            ]
        down_out[d * 32 : d * 32 + 32, :] = w_all[at, 48:80, 0:512]
    order = parity_order()

    @pl.loop(0, 3)
    def _(i):
        at = pl.ds(pl.multiple_of(i * 128, 128), 128)
        p = s.a + jnp.minimum(i, s.n - 1)
        slot = home[p] - 3 * s.dev
        block, low, high = extended(
            ONE, s, links, recs, (low_rows[...], high_rows[...]), x_ref[slot].astype(F32), p
        )

        def store(t, v):
            taps[i, t * 64 : t * 64 + 64, :] = v

        tap_rows(ONE, block, low, high, store)
        taps[i, 576:640, :] = jnp.zeros((64, 1152), BF)
        pre = three_shifts(ONE, mm(w_one[...], taps[i, 0:576, :]))
        tall = jnp.concatenate([pre[:, 128 * b : 128 * b + 128] for b in range(8)], axis=0)
        top = tall.astype(BF)
        rest = (tall - top.astype(F32)).astype(BF)
        tall = mm(top, order) + mm(rest, order)
        parts = swap_groups([tall[64 * b : 64 * b + 64] for b in range(8)])
        for e in range(8):
            v = parts[e]
            sig = 1.0 / (1.0 + jnp.exp(-v))
            hid[e * 64 : e * 64 + 64, at] = (v * sig).astype(BF)
            slope[e * 64 : e * 64 + 64, at] = sig * (1.0 + v * (1.0 - sig))

    red[...] = mm(down_out[...], hid[...]).astype(BF)

    def rule(r, l):
        group, m = l // 16, l % 16
        high = (group == 0) & (r == (m // 2) * 16 + 14 + m % 2)
        low = (group == 1) & (r == (m // 2) * 16 + m % 2)
        return high | low | ((group == 2) & (r == m)) | ((group == 3) & (r == 112 + m))

    pick = one_hot((128, 128), rule)
    for i in range(3):
        rec2[i] = mm(red[:, i * 128 : i * 128 + 128], pick).astype(BF)


def stage_two_kernel(scale, sc, home, links, red, cot, own, other, got1, got2, sw1, sw2,
                     w_a, w_b, w_c, w_d, out, dw, grad, brec,
                     recs, low_rows, high_rows, w_all, w_two, taps, spread):
    s = where_am_i(sc)
    dp = sc[7]
    gather_records(recs, own, other, (got1, got2), (sw1, sw2))
    low_rows[...] = rim_rows(TWO, 0)
    high_rows[...] = rim_rows(TWO, 14)
    for k, w in enumerate((w_a, w_b, w_c, w_d)):
        w_all[k] = w[...]
    for d in range(4):
        at = jnp.bitwise_xor(jnp.int32(d), dp)
        for dx in range(3):
            w_two[dx * 128 + d * 32 : dx * 128 + d * 32 + 32, :] = w_all[
                at, :, dx * 1152 : dx * 1152 + 1152
            ]
    for i in range(3):
        p = s.a + jnp.minimum(i, s.n - 1)
        block, low, high = extended(
            TWO, s, links, recs, (low_rows[...], high_rows[...]),
            red[:, i * 128 : i * 128 + 128].astype(F32), p,
        )

        def store(t, v):
            taps[t * 128 : t * 128 + 128, i * 256 : i * 256 + 256] = v

        tap_rows(TWO, block, low, high, store)
    y = mm(w_two[...], taps[...])
    out[...] = jnp.zeros_like(out)
    for i in range(3):
        p = s.a + jnp.minimum(i, s.n - 1)
        slot = home[p] - 3 * s.dev
        v = three_shifts(TWO, y[:, i * 256 : i * 256 + 256])
        sig = 1.0 / (1.0 + jnp.exp(-v))

        @pl.when(i < s.n)
        def _():
            out[slot] = (v * sig).astype(BF)

        g = cot[slot].astype(F32) * (sig * (1.0 + v * (1.0 - sig))) * scale
        g = jnp.where(i < s.n, g, 0.0).astype(BF).astype(F32)
        g = jnp.concatenate([g, jnp.zeros_like(g)], axis=1)
        for dx in (-1, 0, 1):
            w = g if dx == 0 else pltpu.roll(g, (dx * 16) % 256, 1)
            spread[(dx + 1) * 128 : (dx + 2) * 128, i * 256 : i * 256 + 256] = w.astype(BF)
    whole = mm(spread[...], taps[...], NT)
    for dx in range(3):
        for og in range(2):
            for j in range(9):
                t = (dx * 2 + og) * 9 + j
                row = (t % 2) * 16
                for d in range(4):
                    at = dx * 128 + d * 32 + og * 16
                    dw[t // 2, d, row : row + 16, :] = whole[
                        at : at + 16, j * 128 : j * 128 + 128
                    ].astype(BF)
    dw[27:, :, :, :] = jnp.zeros((5, 4, 32, 128), BF)
    back = mm(w_two[...], spread[...], TN)
    yy, zz = coords(TWO)
    for i in range(3):
        p = s.a + jnp.minimum(i, s.n - 1)
        even = p % 2 == 0
        by_dy = []
        for dy in range(3):
            total = None
            for dz in (-1, 0, 1):
                t = 3 * dy + dz + 1
                v = back[t * 128 : t * 128 + 128, i * 256 : i * 256 + 256]
                if dz == -1:
                    v = pltpu.roll(jnp.where(zz == 0, 0.0, v), 255, 1)
                elif dz == 1:
                    v = pltpu.roll(jnp.where(zz == 1, 0.0, v), 1, 1)
                total = v if total is None else total + v
            by_dy.append(total)
        mid = (
            by_dy[1]
            + pltpu.roll(jnp.where(yy == 0, 0.0, by_dy[0]), 254, 1)
            + pltpu.roll(jnp.where(yy == 7, 0.0, by_dy[2]), 2, 1)
        )
        grad[:, i * 128 : i * 128 + 128] = mid[:, :128]
        rim_low = mm(by_dy[0].astype(BF), low_rows[...], NT).astype(BF)
        rim_high = mm(by_dy[2].astype(BF), high_rows[...], NT).astype(BF)
        xc = jnp.where(even, 0, 7)

        def side(main_to, corner_to):
            def rule(r, l):
                main = (l >= main_to) & (l < main_to + 16) & (r == l - main_to)
                m = l - corner_to
                return main | ((m >= 0) & (m < 16) & (r - 16 == m) & (m // 2 == xc))

            return one_hot((128, 128), rule)

        x_off = jnp.where(even, 0, 112)
        x_pick = one_hot((128, 128), lambda r, l: (l >= 32) & (l < 48) & (r - x_off == l - 32))
        brec[i] = (
            mm(rim_high, side(0, 48))
            + mm(rim_low, side(16, 64))
            + mm(mid[:, 128:].astype(BF), x_pick)
        ).astype(BF)


def stage_three_kernel(sc, links, grad, own, other, got1, got2, sw1, sw2, down, hid, slope, taps,
                       out, recs, gred, g_one, spread, dw):
    s = where_am_i(sc)
    gather_records(recs, own, other, (got1, got2), (sw1, sw2))

    def rows(y_off):
        return one_hot(
            (128, 128), lambda r, l: (r < 32) & (l == ((r % 16) // 2) * 16 + r % 2 + y_off)
        )

    side_rows = (rows(0), rows(14))
    for i in range(3):
        p = s.a + jnp.minimum(i, s.n - 1)
        even = p % 2 == 0
        partner = jnp.where(even, p + 1, p - 1)
        ok_x = x_link(links, p) >= 0
        idx, off = locate_x(s, partner, TWO, 2)
        off = jnp.where(ok_x, off, NOWHERE)
        total = grad[:, i * 128 : i * 128 + 128] + mm(
            recs[idx], picker(TWO, off, jnp.where(even, 112, 0))
        )
        for side, up in ((0, True), (1, False)):
            q = p - 2 if up else p + 2
            c = partner - 2 if up else partner + 2
            ok = link_at(links, p, 2 + side) >= 0
            idx, off, _ = locate(s, q, up, TWO, 2)
            face = mm(recs[idx], picker(TWO, jnp.where(ok, off, NOWHERE), 0))
            ok_c = ok_x & (link_at(links, partner, 2 + side) >= 0)
            idx, _, off = locate(s, c, up, TWO, 2)
            face += mm(recs[idx], picker(TWO, jnp.where(ok_c, off, NOWHERE), 16))
            total += mm(face.astype(BF), side_rows[side])
        gred[:, i * 128 : i * 128 + 128] = jnp.where(i < s.n, total, 0.0).astype(BF)
    dw_down = mm(gred[...], hid[...], NT)
    g_one[...] = (mm(down[...], gred[...], TN) * slope[...]).astype(BF)
    order = parity_order()
    dw[...] = jnp.zeros_like(dw)

    @pl.loop(0, 3)
    def _(i):
        at = pl.ds(pl.multiple_of(i * 128, 128), 128)
        parts = [g_one[e * 64 : e * 64 + 64, at].astype(F32) for e in range(8)]
        tall = jnp.concatenate(swap_groups(parts), axis=0).astype(BF)
        tall = mm(tall, order, NT)
        g = jnp.concatenate(
            [tall[64 * b : 64 * b + 64] for b in range(8)] + [jnp.zeros((64, 128), F32)], axis=1
        )
        for dx in (-1, 0, 1):
            w = g if dx == 0 else pltpu.roll(g, (dx * 64) % 1152, 1)
            spread[(dx + 1) * 64 : (dx + 2) * 64, :] = w.astype(BF)
        dw[...] += mm(spread[...], taps[i], NT)

    for d in range(4):
        for j in range(5):
            for dx in range(3):
                at = dx * 64 + d * 16
                out[dx * 5 + j, d] = dw[at : at + 16, j * 128 : j * 128 + 128].astype(BF)
        for og in range(2):
            for j in range(4):
                at = d * 32 + og * 16
                out[15 + og * 4 + j, d] = dw_down[at : at + 16, j * 128 : j * 128 + 128].astype(BF)
    out[23:, :, :, :] = jnp.zeros((9, 4, 16, 128), BF)


def final_kernel(pieces, one_out, down_out, two_out):
    lane = lax.broadcasted_iota(jnp.int32, (16, 128), 1)
    for dx in range(3):
        for og in range(2):
            for j in range(9):
                t = (dx * 2 + og) * 9 + j
                row = (t % 2) * 16
                two_out[og * 16 : og * 16 + 16, dx * 1152 + j * 128 : dx * 1152 + j * 128 + 128] = (
                    pieces[t // 2, row : row + 16, :].astype(F32)
                )
    for og in range(2):
        for j in range(4):
            down_out[og * 16 : og * 16 + 16, j * 128 : j * 128 + 128] = pieces[
                15 + og * 4 + j, 32:48, :
            ].astype(F32)

    def tile(dx, j):
        return pieces[dx * 5 + j, 32:48, :].astype(F32)

    middle = jnp.concatenate([tile(1, j) for j in range(5)], axis=1)
    middle = pltpu.roll(middle, 64, 1)
    for j in range(4):
        one_out[:, j * 128 : j * 128 + 128] = tile(0, j)
        one_out[:, 1152 + j * 128 : 1280 + j * 128] = tile(2, j)
    one_out[:, 512:640] = jnp.where(lane < 64, tile(0, 4), middle[:, :128])
    one_out[:, 640:1152] = middle[:, 128:]
    one_out[:, 1664:1728] = tile(2, 4)[:, :64]


def call(kernel, scalars, arrays, outs, scratch):
    smem = pl.BlockSpec(memory_space=pltpu.SMEM)
    vmem = pl.BlockSpec(memory_space=pltpu.VMEM)
    return pl.pallas_call(
        kernel,
        out_shape=[jax.ShapeDtypeStruct(*o) for o in outs],
        in_specs=[smem] * len(scalars) + [vmem] * len(arrays),
        out_specs=[vmem] * len(outs),
        scratch_shapes=[pltpu.VMEM(*t) for t in scratch],
        compiler_params=pltpu.CompilerParams(vmem_limit_bytes=60 << 20),
    )(*scalars, *arrays)


def swap_cores(v):
    return lax.ppermute(v, "core", [(0, 1), (1, 0)])


def chips_on(v, by):
    up = [(2 * c, 2 * (c + by)) for c in range(NCHIP - by)]
    down = [(2 * c + 1, 2 * (c - by) + 1) for c in range(by, NCHIP)]
    return lax.ppermute(v, SPACE, up + down)


def across(v, axis, k):
    return lax.ppermute(v, axis, [(i, i ^ k) for i in range(lax.axis_size(axis))])


def exchange(level, sub, sc, own):
    other = swap_cores(own)
    (message,) = call(
        functools.partial(message_kernel, level, sub), (sc,), (own, other),
        [((level.C, level.R), BF)], [((6, level.C, level.R), BF)],
    )
    got1, got2 = chips_on(message, 1), chips_on(message, 2)
    return other, got1, got2, swap_cores(got1), swap_cores(got2)


def gathered(shard):
    return [shard] + [across(shard, "dp", k) for k in (1, 2, 3)]


def scattered(pieces):
    got = lax.all_to_all(pieces, ("x", "y", "core"), 0, 0, tiled=True)
    return got.astype(F32).sum(axis=0).astype(BF)


def on_device(features, cotangent, conv_one, down_weight, conv_two, patch_home, patch_links):
    core, dp = lax.axis_index("core"), lax.axis_index("dp")
    dev = lax.axis_index(SPACE)
    chip = dev // 2
    slots = jnp.arange(8, dtype=jnp.int32)
    marks = jnp.where(slots == 0, -2, jnp.where(slots == 4, 4, slots - 1))
    starts = jnp.sum(
        (patch_home[None, :] < 3 * (2 * chip + marks)[:, None]).astype(jnp.int32), axis=1
    )
    sc = jnp.where(
        slots < 5, starts, jnp.where(slots == 5, dev, jnp.where(slots == 6, core, dp))
    ).astype(jnp.int32)
    links = patch_links.reshape(-1)
    x = features[0]
    (rec_one,) = call(faces_kernel, (sc, patch_home), (x,), [((3, 64, 256), BF)], [])
    rims_one = exchange(ONE, 1, sc, rec_one)
    rows_one = jnp.pad(conv_one.reshape(16, 3, 576).swapaxes(0, 1).reshape(48, 576), ((0, 0), (0, 64)))
    w_one = gathered(jnp.concatenate([rows_one, jnp.pad(down_weight, ((0, 0), (0, 128)))]))
    w_two = gathered(conv_two)
    taps, hid, slope, red, rec_two, down_full = call(
        stage_one_kernel, (sc, patch_home, links),
        (x, rec_one, *rims_one, *w_one),
        [((3, 640, 1152), BF), ((512, 384), BF), ((512, 384), F32), ((128, 384), BF),
         ((3, 128, 128), BF), ((128, 512), BF)],
        [((10, 64, 256), BF), ((128, 1152), BF), ((128, 1152), BF), ((4, 80, 640), BF),
         ((192, 576), BF)],
    )
    rims_two = exchange(TWO, 1, sc, rec_two)
    cells = lax.axis_size("dp") * patch_links.shape[0] * 128
    out, dw_two, grad, rec_back = call(
        functools.partial(stage_two_kernel, float(cells) ** (-0.5)), (sc, patch_home, links),
        (red, cotangent[0], rec_two, *rims_two, *w_two),
        [((3, 128, 128), BF), ((32, 4, 32, 128), BF), ((128, 384), F32), ((3, 128, 128), BF)],
        [((10, 128, 128), BF), ((128, 256), BF), ((128, 256), BF), ((4, 32, 3456), BF),
         ((384, 1152), BF), ((1152, 768), BF), ((384, 768), BF)],
    )
    rims_back = exchange(TWO, 2, sc, rec_back)
    two_sum = scattered(dw_two)
    (small,) = call(
        stage_three_kernel, (sc, links),
        (grad, rec_back, *rims_back, down_full, hid, slope, taps),
        [((32, 4, 16, 128), BF)],
        [((10, 128, 128), BF), ((128, 384), BF), ((512, 384), BF), ((192, 1152), BF),
         ((192, 640), F32)],
    )
    two_sum, small = lax.optimization_barrier((two_sum, small))
    mine = jnp.concatenate([two_sum, scattered(small)], axis=1)
    got = lax.all_to_all(jnp.concatenate([mine, mine]), ("zh", "dp"), 0, 0, tiled=True)
    mine = got.astype(F32).sum(axis=0).astype(BF)
    copies = jnp.broadcast_to(mine[None], (32, *mine.shape))
    pieces = lax.all_to_all(copies, ("x", "y", "core"), 0, 0, tiled=True)
    grads = call(
        final_kernel, (), (pieces,),
        [((16, 1728), F32), ((32, 512), F32), ((32, 3456), F32)], [],
    )
    return (out[None], *grads)


def solution(mesh):
    split = Mesh(
        mesh.devices.reshape(mesh.shape["dp"], 4, 2, 4, 2), ("dp", "x", "zh", "y", "core")
    )
    return jax.shard_map(
        on_device,
        mesh=split,
        in_specs=(
            P("dp", SPACE, None, None),
            P("dp", SPACE, None, None),
            P("dp", None),
            P("dp", None),
            P("dp", None),
            P(),
            P(),
        ),
        out_specs=(P("dp", SPACE, None, None), P("dp", None), P("dp", None), P("dp", None)),
        check_vma=False,
    )
```

```python
import functools
import types

import jax
import jax.numpy as jnp
from jax import lax
from jax.experimental import pallas as pl
from jax.experimental.pallas import tpu as pltpu
from jax.sharding import Mesh
from jax.sharding import PartitionSpec as P

BF = jnp.bfloat16
F32 = jnp.float32
SPACE = ("x", "zh", "y", "core")
NCHIP = 32
ONE = types.SimpleNamespace(C=64, g=64, R=256, N=1024, W=1152, zs=4, nx=16)
TWO = types.SimpleNamespace(C=128, g=16, R=128, N=128, W=256, zs=2, nx=8)
NOWHERE = -8192


def mm(a, b, contract=((1,), (0,))):
    return lax.dot_general(a, b, (contract, ((), ())), preferred_element_type=F32)


NT = ((1,), (1,))
TN = ((0,), (0,))


def one_hot(shape, rule):
    r = lax.broadcasted_iota(jnp.int32, shape, 0)
    l = lax.broadcasted_iota(jnp.int32, shape, 1)
    return jnp.where(rule(r, l), 1.0, 0.0).astype(BF)


def picker(level, off, dst):
    return one_hot(
        (level.R, 128),
        lambda r, l: (r - off == l - dst) & (l >= dst) & (l < dst + level.g),
    )


def corner_picker(level, off, xc):
    g, zs = level.g, level.zs
    return one_hot(
        (level.R, 128),
        lambda r, l: (r - off == l - g) & (l >= g) & (l < 2 * g) & ((l - g) // zs == xc),
    )


def rim_rows(level, y_off):
    g, zs, N, W = level.g, level.zs, level.N, level.W

    def rule(r, l):
        face = (r < g) & (l == (r // zs) * g + r % zs + y_off)
        q = r - g
        low = (q >= 0) & (q < zs) & (l == N + q + y_off)
        high = (q >= g - zs) & (q < g) & (l == W - g + q - (g - zs) + y_off)
        return face | low | high

    return one_hot((128, W), rule)


def where_am_i(sc):
    core = sc[6]
    s = types.SimpleNamespace(core=core, dev=sc[5])
    n0, n1 = sc[2] - sc[1], sc[3] - sc[2]
    s.n0 = n0
    s.total = n0 + n1
    s.start = sc[1]
    s.a = jnp.where(core == 0, sc[1], sc[2])
    s.n = jnp.where(core == 0, n0, n1)
    s.other = jnp.where(core == 0, n1, n0)
    s.chip_before = sc[1] - sc[0]
    s.chip_after = sc[4] - sc[3]
    return s


def locate(s, q, up, level, sub):
    g = level.g
    rec_off = jnp.int32(0 if up else g)
    own = (q >= s.a) & (q < s.a + s.n)
    if up:
        k = s.a - q
        near = jnp.where(s.core == 1, s.other, 0)
        o_idx = 3 + s.other - k
        m_idx = jnp.where(s.core == 0, 6, 8)
        chip = s.chip_before
    else:
        k = q - (s.a + s.n) + 1
        near = jnp.where(s.core == 0, s.other, 0)
        o_idx = 3 + k - 1
        m_idx = jnp.where(s.core == 0, 8, 6)
        chip = s.chip_after
    t = k - near
    in_o = k <= near
    far = t > chip
    idx = jnp.where(own, q - s.a, jnp.where(in_o, o_idx, jnp.where(far, m_idx + 1, m_idx)))
    in_rec = own | in_o
    main = jnp.where(in_rec, rec_off, jnp.where(far, 0, sub * (t - 1) * g))
    corner = jnp.where(in_rec, 3 * g if up else 4 * g, main + g) if sub == 2 else main
    return jnp.clip(idx, 0, 9), main, corner


def locate_x(s, q, level, sub):
    g = level.g
    rec_off = jnp.where(q % 2 == 0, 3 * g, 2 * g) if sub == 1 else jnp.int32(2 * g)
    msg_off = 3 * g if sub == 1 else 6 * g
    own = (q >= s.a) & (q < s.a + s.n)
    before = q < s.a
    in_o = jnp.where(before, s.core == 1, s.core == 0)
    o_idx = jnp.where(before, 3 + s.other - 1, 3)
    m_idx = jnp.where(before == (s.core == 0), 6, 8)
    idx = jnp.where(own, q - s.a, jnp.where(in_o, o_idx, m_idx))
    return jnp.clip(idx, 0, 9), jnp.where(own | in_o, rec_off, msg_off)


def gather_records(recs, own, other, got, swapped):
    for k in range(3):
        recs[k] = own[k]
        recs[3 + k] = other[k]
    for k in range(2):
        recs[6 + k] = got[k][...]
        recs[8 + k] = swapped[k][...]


def link_at(links, q, column):
    return links[column, jnp.clip(q, 0, 127)]


def x_link(links, q):
    return link_at(links, q, jnp.where(q % 2 == 0, 1, 0))


def extended(level, s, links, recs, rows, field, p):
    even = p % 2 == 0
    partner = jnp.where(even, p + 1, p - 1)
    idx, off = locate_x(s, partner, level, 1)
    off = jnp.where(x_link(links, p) >= 0, off, NOWHERE)
    rim = mm(recs[idx], picker(level, off, jnp.where(even, 0, 128 - level.g)))
    block = jnp.concatenate([field, rim], axis=1)
    rims = []
    for side, up in ((0, True), (1, False)):
        q = p - 2 if up else p + 2
        c = jnp.where(even, q + 1, q - 1)
        ok = link_at(links, p, 2 + side) >= 0
        idx, off, _ = locate(s, q, up, level, 1)
        face = mm(recs[idx], picker(level, jnp.where(ok, off, NOWHERE), 0))
        ok_c = ok & (x_link(links, q) >= 0)
        idx, off, _ = locate(s, c, up, level, 1)
        xc = jnp.where(even, 0, level.nx - 1)
        face += mm(recs[idx], corner_picker(level, jnp.where(ok_c, off, NOWHERE), xc))
        rims.append(mm(face.astype(BF), rows[side]))
    return block, rims[0], rims[1]


def coords(level):
    lane = lax.broadcasted_iota(jnp.int32, (level.C, level.W), 1)
    return (lane % level.g) // level.zs, lane % level.zs


def tap_rows(level, block, low, high, store):
    W, zs = level.W, level.zs
    y, z = coords(level)
    for dy in (-1, 0, 1):
        if dy == 0:
            f = block
        elif dy == -1:
            f = jnp.where(y == 0, low, pltpu.roll(block, zs, 1))
        else:
            f = jnp.where(y == level.nx - 1, high, pltpu.roll(block, W - zs, 1))
        for dz in (-1, 0, 1):
            if dz == 0:
                v = f
            elif dz == -1:
                v = jnp.where(z == 0, 0.0, pltpu.roll(f, 1, 1))
            else:
                v = jnp.where(z == zs - 1, 0.0, pltpu.roll(f, W - 1, 1))
            store(3 * (dy + 1) + dz + 1, v.astype(BF))


def three_shifts(level, y):
    C, W, g = level.C, level.W, level.g
    total = pltpu.roll(y[:C], g, 1) + y[C : 2 * C] + pltpu.roll(y[2 * C :], W - g, 1)
    return total[:, : level.N]


def parity_order():
    def rule(r, l):
        y, z = (r % 64) // 4, r % 4
        e = 4 * (r // 64) + 2 * (y % 2) + z % 2
        return l == e * 16 + (y // 2) * 2 + z // 2

    return one_hot((128, 128), rule)


def swap_groups(arrays):
    group = lax.broadcasted_iota(jnp.int32, (64, 128), 1) // 16
    arrays = list(arrays)
    for b in (1, 2, 4):
        bit = (group & b) != 0
        for i in range(8):
            if i & b:
                continue
            lo, hi = arrays[i], arrays[i + b]
            arrays[i] = jnp.where(bit, pltpu.roll(hi, 16 * b, 1), lo)
            arrays[i + b] = jnp.where(bit, hi, pltpu.roll(lo, 128 - 16 * b, 1))
    return arrays


def faces_kernel(sc, home, x_ref, rec_ref):
    s = where_am_i(sc)

    def rule(r, l):
        group, m = l // 64, l % 64
        high = (group == 0) & (r == (m // 4) * 64 + 60 + m % 4)
        low = (group == 1) & (r == (m // 4) * 64 + m % 4)
        return high | low | ((group == 2) & (r == m)) | ((group == 3) & (r == 960 + m))

    pick = one_hot((1024, 256), rule)
    for i in range(3):
        p = s.a + jnp.minimum(i, s.n - 1)
        slot = home[p] - 3 * s.dev
        rec_ref[i] = mm(x_ref[slot], pick).astype(BF)


def message_kernel(level, sub, sc, own, other, out, both):
    s = where_am_i(sc)
    g = level.g
    for k in range(3):
        both[k] = own[k]
        both[3 + k] = other[k]
    up = s.core == 0
    main = jnp.where(up, 0, g)
    corner = jnp.where(up, 3 * g, 4 * g)
    total = None
    for k in range(3):
        t = jnp.maximum(jnp.where(up, s.total - 1 - k, k), 0)
        t = jnp.minimum(t, s.total - 1)
        first = t < s.n0
        mine = first == (s.core == 0)
        idx = jnp.where(first, t, t - s.n0) + jnp.where(mine, 0, 3)
        q = s.start + t
        base = sub * k * g

        def rule(r, l):
            hit = (r - main == l - base) & (l >= base) & (l < base + g)
            if sub == 2:
                c = base + g
                hit |= (r - corner == l - c) & (l >= c) & (l < c + g)
            if k == 0:
                to = 3 * g if sub == 1 else 6 * g
                src = jnp.where(q % 2 == 0, 3 * g, 2 * g) if sub == 1 else 2 * g
                hit |= (r - src == l - to) & (l >= to) & (l < to + g)
            return hit

        part = mm(both[idx], one_hot((level.R, level.R), rule))
        total = part if total is None else total + part
    out[...] = total.astype(BF)


def stage_one_kernel(sc, home, links, x_ref, own, other, got1, got2, sw1, sw2, w_a, w_b, w_c, w_d,
                     taps, hid, slope, red, rec2, down_out,
                     recs, low_rows, high_rows, w_all, w_one):
    s = where_am_i(sc)
    dp = sc[7]
    gather_records(recs, own, other, (got1, got2), (sw1, sw2))
    low_rows[...] = rim_rows(ONE, 0)
    high_rows[...] = rim_rows(ONE, 60)
    for k, w in enumerate((w_a, w_b, w_c, w_d)):
        w_all[k] = w[...]
    for d in range(4):
        at = jnp.bitwise_xor(jnp.int32(d), dp)
        for dx in range(3):
            w_one[dx * 64 + d * 16 : dx * 64 + d * 16 + 16, :] = w_all[
                at, dx * 16 : dx * 16 + 16, 0:576
            ]
        down_out[d * 32 : d * 32 + 32, :] = w_all[at, 48:80, 0:512]
    order = parity_order()

    @pl.loop(0, 3)
    def _(i):
        at = pl.ds(pl.multiple_of(i * 128, 128), 128)
        p = s.a + jnp.minimum(i, s.n - 1)
        slot = home[p] - 3 * s.dev
        block, low, high = extended(
            ONE, s, links, recs, (low_rows[...], high_rows[...]), x_ref[slot].astype(F32), p
        )

        def store(t, v):
            taps[i, t * 64 : t * 64 + 64, :] = v

        tap_rows(ONE, block, low, high, store)
        taps[i, 576:640, :] = jnp.zeros((64, 1152), BF)
        pre = three_shifts(ONE, mm(w_one[...], taps[i, 0:576, :]))
        tall = jnp.concatenate([pre[:, 128 * b : 128 * b + 128] for b in range(8)], axis=0)
        top = tall.astype(BF)
        rest = (tall - top.astype(F32)).astype(BF)
        tall = mm(top, order) + mm(rest, order)
        parts = swap_groups([tall[64 * b : 64 * b + 64] for b in range(8)])
        for e in range(8):
            v = parts[e]
            sig = 1.0 / (1.0 + jnp.exp(-v))
            hid[e * 64 : e * 64 + 64, at] = (v * sig).astype(BF)
            slope[e * 64 : e * 64 + 64, at] = sig * (1.0 + v * (1.0 - sig))

    red[...] = mm(down_out[...], hid[...]).astype(BF)

    def rule(r, l):
        group, m = l // 16, l % 16
        high = (group == 0) & (r == (m // 2) * 16 + 14 + m % 2)
        low = (group == 1) & (r == (m // 2) * 16 + m % 2)
        return high | low | ((group == 2) & (r == m)) | ((group == 3) & (r == 112 + m))

    pick = one_hot((128, 128), rule)
    for i in range(3):
        rec2[i] = mm(red[:, i * 128 : i * 128 + 128], pick).astype(BF)


def stage_two_kernel(scale, sc, home, links, red, cot, own, other, got1, got2, sw1, sw2,
                     w_a, w_b, w_c, w_d, out, dw, grad, brec,
                     recs, low_rows, high_rows, w_all, w_two, taps, spread):
    s = where_am_i(sc)
    dp = sc[7]
    gather_records(recs, own, other, (got1, got2), (sw1, sw2))
    low_rows[...] = rim_rows(TWO, 0)
    high_rows[...] = rim_rows(TWO, 14)
    for k, w in enumerate((w_a, w_b, w_c, w_d)):
        w_all[k] = w[...]
    for d in range(4):
        at = jnp.bitwise_xor(jnp.int32(d), dp)
        for dx in range(3):
            w_two[dx * 128 + d * 32 : dx * 128 + d * 32 + 32, :] = w_all[
                at, :, dx * 1152 : dx * 1152 + 1152
            ]
    for i in range(3):
        p = s.a + jnp.minimum(i, s.n - 1)
        block, low, high = extended(
            TWO, s, links, recs, (low_rows[...], high_rows[...]),
            red[:, i * 128 : i * 128 + 128].astype(F32), p,
        )

        def store(t, v):
            taps[t * 128 : t * 128 + 128, i * 256 : i * 256 + 256] = v

        tap_rows(TWO, block, low, high, store)
    y = mm(w_two[...], taps[...])
    out[...] = jnp.zeros_like(out)
    for i in range(3):
        p = s.a + jnp.minimum(i, s.n - 1)
        slot = home[p] - 3 * s.dev
        v = three_shifts(TWO, y[:, i * 256 : i * 256 + 256])
        sig = 1.0 / (1.0 + jnp.exp(-v))

        @pl.when(i < s.n)
        def _():
            out[slot] = (v * sig).astype(BF)

        g = cot[slot].astype(F32) * (sig * (1.0 + v * (1.0 - sig))) * scale
        g = jnp.where(i < s.n, g, 0.0).astype(BF).astype(F32)
        g = jnp.concatenate([g, jnp.zeros_like(g)], axis=1)
        for dx in (-1, 0, 1):
            w = g if dx == 0 else pltpu.roll(g, (dx * 16) % 256, 1)
            spread[(dx + 1) * 128 : (dx + 2) * 128, i * 256 : i * 256 + 256] = w.astype(BF)
    whole = mm(spread[...], taps[...], NT)
    for dx in range(3):
        for j in range(9):
            for og in range(2):
                for d in range(4):
                    at = dx * 128 + d * 32 + og * 16
                    dw[og, dx * 9 + j, d] = whole[at : at + 16, j * 128 : j * 128 + 128].astype(BF)
    dw[:, 27:, :, :, :] = jnp.zeros((2, 5, 4, 16, 128), BF)
    back = mm(w_two[...], spread[...], TN)
    yy, zz = coords(TWO)
    for i in range(3):
        p = s.a + jnp.minimum(i, s.n - 1)
        even = p % 2 == 0
        by_dy = []
        for dy in range(3):
            total = None
            for dz in (-1, 0, 1):
                t = 3 * dy + dz + 1
                v = back[t * 128 : t * 128 + 128, i * 256 : i * 256 + 256]
                if dz == -1:
                    v = pltpu.roll(jnp.where(zz == 0, 0.0, v), 255, 1)
                elif dz == 1:
                    v = pltpu.roll(jnp.where(zz == 1, 0.0, v), 1, 1)
                total = v if total is None else total + v
            by_dy.append(total)
        mid = (
            by_dy[1]
            + pltpu.roll(jnp.where(yy == 0, 0.0, by_dy[0]), 254, 1)
            + pltpu.roll(jnp.where(yy == 7, 0.0, by_dy[2]), 2, 1)
        )
        grad[:, i * 128 : i * 128 + 128] = mid[:, :128]
        rim_low = mm(by_dy[0].astype(BF), low_rows[...], NT).astype(BF)
        rim_high = mm(by_dy[2].astype(BF), high_rows[...], NT).astype(BF)
        xc = jnp.where(even, 0, 7)

        def side(main_to, corner_to):
            def rule(r, l):
                main = (l >= main_to) & (l < main_to + 16) & (r == l - main_to)
                m = l - corner_to
                return main | ((m >= 0) & (m < 16) & (r - 16 == m) & (m // 2 == xc))

            return one_hot((128, 128), rule)

        x_off = jnp.where(even, 0, 112)
        x_pick = one_hot((128, 128), lambda r, l: (l >= 32) & (l < 48) & (r - x_off == l - 32))
        brec[i] = (
            mm(rim_high, side(0, 48))
            + mm(rim_low, side(16, 64))
            + mm(mid[:, 128:].astype(BF), x_pick)
        ).astype(BF)


def stage_three_kernel(sc, links, grad, own, other, got1, got2, sw1, sw2, down, hid, slope, taps,
                       two, out, recs, gred, g_one, spread, dw):
    s = where_am_i(sc)
    gather_records(recs, own, other, (got1, got2), (sw1, sw2))

    def rows(y_off):
        return one_hot(
            (128, 128), lambda r, l: (r < 32) & (l == ((r % 16) // 2) * 16 + r % 2 + y_off)
        )

    side_rows = (rows(0), rows(14))
    for i in range(3):
        p = s.a + jnp.minimum(i, s.n - 1)
        even = p % 2 == 0
        partner = jnp.where(even, p + 1, p - 1)
        ok_x = x_link(links, p) >= 0
        idx, off = locate_x(s, partner, TWO, 2)
        off = jnp.where(ok_x, off, NOWHERE)
        total = grad[:, i * 128 : i * 128 + 128] + mm(
            recs[idx], picker(TWO, off, jnp.where(even, 112, 0))
        )
        for side, up in ((0, True), (1, False)):
            q = p - 2 if up else p + 2
            c = partner - 2 if up else partner + 2
            ok = link_at(links, p, 2 + side) >= 0
            idx, off, _ = locate(s, q, up, TWO, 2)
            face = mm(recs[idx], picker(TWO, jnp.where(ok, off, NOWHERE), 0))
            ok_c = ok_x & (link_at(links, partner, 2 + side) >= 0)
            idx, _, off = locate(s, c, up, TWO, 2)
            face += mm(recs[idx], picker(TWO, jnp.where(ok_c, off, NOWHERE), 16))
            total += mm(face.astype(BF), side_rows[side])
        gred[:, i * 128 : i * 128 + 128] = jnp.where(i < s.n, total, 0.0).astype(BF)
    dw_down = mm(gred[...], hid[...], NT)
    g_one[...] = (mm(down[...], gred[...], TN) * slope[...]).astype(BF)
    order = parity_order()
    dw[...] = jnp.zeros_like(dw)

    @pl.loop(0, 3)
    def _(i):
        at = pl.ds(pl.multiple_of(i * 128, 128), 128)
        parts = [g_one[e * 64 : e * 64 + 64, at].astype(F32) for e in range(8)]
        tall = jnp.concatenate(swap_groups(parts), axis=0).astype(BF)
        tall = mm(tall, order, NT)
        g = jnp.concatenate(
            [tall[64 * b : 64 * b + 64] for b in range(8)] + [jnp.zeros((64, 128), F32)], axis=1
        )
        for dx in (-1, 0, 1):
            w = g if dx == 0 else pltpu.roll(g, (dx * 64) % 1152, 1)
            spread[(dx + 1) * 64 : (dx + 2) * 64, :] = w.astype(BF)
        dw[...] += mm(spread[...], taps[i], NT)

    for d in range(4):
        for j in range(5):
            for dx in range(3):
                at = dx * 64 + d * 16
                out[dx * 5 + j, d, 0:16, :] = dw[at : at + 16, j * 128 : j * 128 + 128].astype(BF)
        for og in range(2):
            for j in range(4):
                at = d * 32 + og * 16
                out[15 + og * 4 + j, d, 0:16, :] = dw_down[
                    at : at + 16, j * 128 : j * 128 + 128
                ].astype(BF)
    out[23:, :, 0:16, :] = jnp.zeros((9, 4, 16, 128), BF)
    out[:, :, 16:32, :] = two[...]


def sum_kernel(got, out):
    for d in range(4):
        small, halves = [None, None], [None, None]
        for k in range(32):
            v = got[k, d].astype(F32)
            h = k % 2
            small[h] = v[:16] if small[h] is None else small[h] + v[:16]
            halves[h] = v[16:] if halves[h] is None else halves[h] + v[16:]
        total = jnp.concatenate([small[0] + small[1], halves[0], halves[1]], axis=0).astype(BF)
        out[d] = total
        out[4 + d] = total


def spread_kernel(got, out):
    total = got[0].astype(F32)
    for k in range(1, 8):
        total += got[k].astype(F32)
    total = total.astype(BF)
    for k in range(32):
        out[k] = total


def final_kernel(pieces, one_out, down_out, two_out):
    lane = lax.broadcasted_iota(jnp.int32, (16, 128), 1)
    for dx in range(3):
        for og in range(2):
            for j in range(9):
                two_out[og * 16 : og * 16 + 16, dx * 1152 + j * 128 : dx * 1152 + j * 128 + 128] = (
                    pieces[dx * 9 + j, 16 + og * 16 : 32 + og * 16, :].astype(F32)
                )
    for og in range(2):
        for j in range(4):
            down_out[og * 16 : og * 16 + 16, j * 128 : j * 128 + 128] = pieces[
                15 + og * 4 + j, 0:16, :
            ].astype(F32)

    def tile(dx, j):
        return pieces[dx * 5 + j, 0:16, :].astype(F32)

    middle = jnp.concatenate([tile(1, j) for j in range(5)], axis=1)
    middle = pltpu.roll(middle, 64, 1)
    for j in range(4):
        one_out[:, j * 128 : j * 128 + 128] = tile(0, j)
        one_out[:, 1152 + j * 128 : 1280 + j * 128] = tile(2, j)
    one_out[:, 512:640] = jnp.where(lane < 64, tile(0, 4), middle[:, :128])
    one_out[:, 640:1152] = middle[:, 128:]
    one_out[:, 1664:1728] = tile(2, 4)[:, :64]


def call(kernel, scalars, arrays, outs, scratch):
    smem = pl.BlockSpec(memory_space=pltpu.SMEM)
    vmem = pl.BlockSpec(memory_space=pltpu.VMEM)
    return pl.pallas_call(
        kernel,
        out_shape=[jax.ShapeDtypeStruct(*o) for o in outs],
        in_specs=[smem] * len(scalars) + [vmem] * len(arrays),
        out_specs=[vmem] * len(outs),
        scratch_shapes=[pltpu.VMEM(*t) for t in scratch],
        compiler_params=pltpu.CompilerParams(vmem_limit_bytes=60 << 20),
    )(*scalars, *arrays)


def swap_cores(v):
    return lax.ppermute(v, "core", [(0, 1), (1, 0)])


def chips_on(v, by):
    up = [(2 * c, 2 * (c + by)) for c in range(NCHIP - by)]
    down = [(2 * c + 1, 2 * (c - by) + 1) for c in range(by, NCHIP)]
    return lax.ppermute(v, SPACE, up + down)


def across(v, axis, k):
    return lax.ppermute(v, axis, [(i, i ^ k) for i in range(lax.axis_size(axis))])


def exchange(level, sub, sc, own):
    other = swap_cores(own)
    (message,) = call(
        functools.partial(message_kernel, level, sub), (sc,), (own, other),
        [((level.C, level.R), BF)], [((6, level.C, level.R), BF)],
    )
    got1, got2 = chips_on(message, 1), chips_on(message, 2)
    return other, got1, got2, swap_cores(got1), swap_cores(got2)


def gathered(shard):
    return [shard] + [across(shard, "dp", k) for k in (1, 2, 3)]


def on_device(features, cotangent, conv_one, down_weight, conv_two, patch_home, patch_links):
    core, dp = lax.axis_index("core"), lax.axis_index("dp")
    dev = lax.axis_index(SPACE)
    chip = dev // 2
    slots = jnp.arange(8, dtype=jnp.int32)
    marks = jnp.where(slots == 0, -2, jnp.where(slots == 4, 4, slots - 1))
    starts = jnp.sum(
        (patch_home[None, :] < 3 * (2 * chip + marks)[:, None]).astype(jnp.int32), axis=1
    )
    sc = jnp.where(
        slots < 5, starts, jnp.where(slots == 5, dev, jnp.where(slots == 6, core, dp))
    ).astype(jnp.int32)
    links = patch_links.T
    x = features[0]
    (rec_one,) = call(faces_kernel, (sc, patch_home), (x,), [((3, 64, 256), BF)], [])
    rims_one = exchange(ONE, 1, sc, rec_one)
    rows_one = jnp.pad(conv_one.reshape(16, 3, 576).swapaxes(0, 1).reshape(48, 576), ((0, 0), (0, 64)))
    w_one = gathered(jnp.concatenate([rows_one, jnp.pad(down_weight, ((0, 0), (0, 128)))]))
    w_two = gathered(conv_two)
    taps, hid, slope, red, rec_two, down_full = call(
        stage_one_kernel, (sc, patch_home, links),
        (x, rec_one, *rims_one, *w_one),
        [((3, 640, 1152), BF), ((512, 384), BF), ((512, 384), F32), ((128, 384), BF),
         ((3, 128, 128), BF), ((128, 512), BF)],
        [((10, 64, 256), BF), ((128, 1152), BF), ((128, 1152), BF), ((4, 80, 640), BF),
         ((192, 576), BF)],
    )
    rims_two = exchange(TWO, 1, sc, rec_two)
    cells = lax.axis_size("dp") * patch_links.shape[0] * 128
    out, dw_two, grad, rec_back = call(
        functools.partial(stage_two_kernel, float(cells) ** (-0.5)), (sc, patch_home, links),
        (red, cotangent[0], rec_two, *rims_two, *w_two),
        [((3, 128, 128), BF), ((2, 32, 4, 16, 128), BF), ((128, 384), F32), ((3, 128, 128), BF)],
        [((10, 128, 128), BF), ((128, 256), BF), ((128, 256), BF), ((4, 32, 3456), BF),
         ((384, 1152), BF), ((1152, 768), BF), ((384, 768), BF)],
    )
    rims_back = exchange(TWO, 2, sc, rec_back)
    keep = lax.dynamic_index_in_dim(dw_two, core, 0, keepdims=False)
    give = lax.dynamic_index_in_dim(dw_two, 1 - core, 0, keepdims=False)
    two_part = (keep.astype(F32) + swap_cores(give).astype(F32)).astype(BF)
    (small,) = call(
        stage_three_kernel, (sc, links),
        (grad, rec_back, *rims_back, down_full, hid, slope, taps, two_part),
        [((32, 4, 32, 128), BF)],
        [((10, 128, 128), BF), ((128, 384), BF), ((512, 384), BF), ((192, 1152), BF),
         ((192, 640), F32)],
    )
    got = lax.all_to_all(small, ("x", "y", "core"), 0, 0, tiled=True)
    (mine,) = call(sum_kernel, (), (got,), [((8, 48, 128), BF)], [])
    got = lax.all_to_all(mine, ("zh", "dp"), 0, 0, tiled=True)
    (copies,) = call(spread_kernel, (), (got,), [((32, 48, 128), BF)], [])
    pieces = lax.all_to_all(copies, ("x", "y", "core"), 0, 0, tiled=True)
    grads = call(
        final_kernel, (), (pieces,),
        [((16, 1728), F32), ((32, 512), F32), ((32, 3456), F32)], [],
    )
    return (out[None], *grads)


def solution(mesh):
    split = Mesh(
        mesh.devices.reshape(mesh.shape["dp"], 4, 2, 4, 2), ("dp", "x", "zh", "y", "core")
    )
    return jax.shard_map(
        on_device,
        mesh=split,
        in_specs=(
            P("dp", SPACE, None, None),
            P("dp", SPACE, None, None),
            P("dp", None),
            P("dp", None),
            P("dp", None),
            P(),
            P(),
        ),
        out_specs=(P("dp", SPACE, None, None), P("dp", None), P("dp", None), P("dp", None)),
        check_vma=False,
    )
```

```python
import functools
import types

import jax
import jax.numpy as jnp
from jax import lax
from jax.experimental import pallas as pl
from jax.experimental.pallas import tpu as pltpu
from jax.sharding import Mesh
from jax.sharding import PartitionSpec as P


BF = jnp.bfloat16
F32 = jnp.float32
SPACE = ("x", "zh", "y", "core")
NCHIP = 32
ONE = types.SimpleNamespace(C=64, g=64, R=256, N=1024, W=1152, zs=4, nx=16)
TWO = types.SimpleNamespace(C=128, g=16, R=128, N=128, W=256, zs=2, nx=8)
NOWHERE = -8192


def mm(a, b, contract=((1,), (0,))):
    return lax.dot_general(a, b, (contract, ((), ())), preferred_element_type=F32)


NT = ((1,), (1,))
TN = ((0,), (0,))


def one_hot(shape, rule):
    r = lax.broadcasted_iota(jnp.int32, shape, 0)
    l = lax.broadcasted_iota(jnp.int32, shape, 1)
    return jnp.where(rule(r, l), 1.0, 0.0).astype(BF)


def picker(level, off, dst):
    return one_hot(
        (level.R, 128),
        lambda r, l: (r - off == l - dst) & (l >= dst) & (l < dst + level.g),
    )


def corner_picker(level, off, xc):
    g, zs = level.g, level.zs
    return one_hot(
        (level.R, 128),
        lambda r, l: (r - off == l - g) & (l >= g) & (l < 2 * g) & ((l - g) // zs == xc),
    )


def rim_rows(level, y_off):
    g, zs, N, W = level.g, level.zs, level.N, level.W

    def rule(r, l):
        face = (r < g) & (l == (r // zs) * g + r % zs + y_off)
        q = r - g
        low = (q >= 0) & (q < zs) & (l == N + q + y_off)
        high = (q >= g - zs) & (q < g) & (l == W - g + q - (g - zs) + y_off)
        return face | low | high

    return one_hot((128, W), rule)


def where_am_i(sc):
    core = sc[6]
    s = types.SimpleNamespace(core=core, dev=sc[5])
    n0, n1 = sc[2] - sc[1], sc[3] - sc[2]
    s.n0 = n0
    s.total = n0 + n1
    s.start = sc[1]
    s.a = jnp.where(core == 0, sc[1], sc[2])
    s.n = jnp.where(core == 0, n0, n1)
    s.other = jnp.where(core == 0, n1, n0)
    s.chip_before = sc[1] - sc[0]
    s.chip_after = sc[4] - sc[3]
    return s


def locate(s, q, up, level, sub):
    g = level.g
    rec_off = jnp.int32(0 if up else g)
    own = (q >= s.a) & (q < s.a + s.n)
    if up:
        k = s.a - q
        near = jnp.where(s.core == 1, s.other, 0)
        o_idx = 3 + s.other - k
        m_idx = jnp.where(s.core == 0, 6, 8)
        chip = s.chip_before
    else:
        k = q - (s.a + s.n) + 1
        near = jnp.where(s.core == 0, s.other, 0)
        o_idx = 3 + k - 1
        m_idx = jnp.where(s.core == 0, 8, 6)
        chip = s.chip_after
    t = k - near
    in_o = k <= near
    far = t > chip
    idx = jnp.where(own, q - s.a, jnp.where(in_o, o_idx, jnp.where(far, m_idx + 1, m_idx)))
    in_rec = own | in_o
    main = jnp.where(in_rec, rec_off, jnp.where(far, 0, sub * (t - 1) * g))
    corner = jnp.where(in_rec, 3 * g if up else 4 * g, main + g) if sub == 2 else main
    return jnp.clip(idx, 0, 9), main, corner


def locate_x(s, q, level, sub):
    g = level.g
    rec_off = jnp.where(q % 2 == 0, 3 * g, 2 * g) if sub == 1 else jnp.int32(2 * g)
    msg_off = 3 * g if sub == 1 else 6 * g
    own = (q >= s.a) & (q < s.a + s.n)
    before = q < s.a
    in_o = jnp.where(before, s.core == 1, s.core == 0)
    o_idx = jnp.where(before, 3 + s.other - 1, 3)
    m_idx = jnp.where(before == (s.core == 0), 6, 8)
    idx = jnp.where(own, q - s.a, jnp.where(in_o, o_idx, m_idx))
    return jnp.clip(idx, 0, 9), jnp.where(own | in_o, rec_off, msg_off)


def gather_records(recs, own, other, got, swapped):
    for k in range(3):
        recs[k] = own[k]
        recs[3 + k] = other[k]
    for k in range(2):
        recs[6 + k] = got[k][...]
        recs[8 + k] = swapped[k][...]


def link_at(links, q, column):
    return links[column, jnp.clip(q, 0, 127)]


def x_link(links, q):
    return link_at(links, q, jnp.where(q % 2 == 0, 1, 0))


def extended(level, s, links, recs, rows, field, p):
    even = p % 2 == 0
    partner = jnp.where(even, p + 1, p - 1)
    idx, off = locate_x(s, partner, level, 1)
    off = jnp.where(x_link(links, p) >= 0, off, NOWHERE)
    rim = mm(recs[idx], picker(level, off, jnp.where(even, 0, 128 - level.g)))
    block = jnp.concatenate([field, rim], axis=1)
    rims = []
    for side, up in ((0, True), (1, False)):
        q = p - 2 if up else p + 2
        c = jnp.where(even, q + 1, q - 1)
        ok = link_at(links, p, 2 + side) >= 0
        idx, off, _ = locate(s, q, up, level, 1)
        face = mm(recs[idx], picker(level, jnp.where(ok, off, NOWHERE), 0))
        ok_c = ok & (x_link(links, q) >= 0)
        idx, off, _ = locate(s, c, up, level, 1)
        xc = jnp.where(even, 0, level.nx - 1)
        face += mm(recs[idx], corner_picker(level, jnp.where(ok_c, off, NOWHERE), xc))
        rims.append(mm(face.astype(BF), rows[side]))
    return block, rims[0], rims[1]


def coords(level):
    lane = lax.broadcasted_iota(jnp.int32, (level.C, level.W), 1)
    return (lane % level.g) // level.zs, lane % level.zs


def tap_rows(level, block, low, high, store):
    W, zs = level.W, level.zs
    y, z = coords(level)
    for dy in (-1, 0, 1):
        if dy == 0:
            f = block
        elif dy == -1:
            f = jnp.where(y == 0, low, pltpu.roll(block, zs, 1))
        else:
            f = jnp.where(y == level.nx - 1, high, pltpu.roll(block, W - zs, 1))
        for dz in (-1, 0, 1):
            if dz == 0:
                v = f
            elif dz == -1:
                v = jnp.where(z == 0, 0.0, pltpu.roll(f, 1, 1))
            else:
                v = jnp.where(z == zs - 1, 0.0, pltpu.roll(f, W - 1, 1))
            store(3 * (dy + 1) + dz + 1, v.astype(BF))


def three_shifts(level, y):
    C, W, g = level.C, level.W, level.g
    total = pltpu.roll(y[:C], g, 1) + y[C : 2 * C] + pltpu.roll(y[2 * C :], W - g, 1)
    return total[:, : level.N]


def parity_order():
    def rule(r, l):
        y, z = (r % 64) // 4, r % 4
        e = 4 * (r // 64) + 2 * (y % 2) + z % 2
        return l == e * 16 + (y // 2) * 2 + z // 2

    return one_hot((128, 128), rule)


def swap_groups(arrays):
    group = lax.broadcasted_iota(jnp.int32, (64, 128), 1) // 16
    arrays = list(arrays)
    for b in (1, 2, 4):
        bit = (group & b) != 0
        for i in range(8):
            if i & b:
                continue
            lo, hi = arrays[i], arrays[i + b]
            arrays[i] = jnp.where(bit, pltpu.roll(hi, 16 * b, 1), lo)
            arrays[i + b] = jnp.where(bit, hi, pltpu.roll(lo, 128 - 16 * b, 1))
    return arrays


def faces_kernel(sc, home, x_ref, rec_ref):
    s = where_am_i(sc)

    def rule(r, l):
        group, m = l // 64, l % 64
        high = (group == 0) & (r == (m // 4) * 64 + 60 + m % 4)
        low = (group == 1) & (r == (m // 4) * 64 + m % 4)
        return high | low | ((group == 2) & (r == m)) | ((group == 3) & (r == 960 + m))

    pick = one_hot((1024, 256), rule)
    for i in range(3):
        p = s.a + jnp.minimum(i, s.n - 1)
        slot = home[p] - 3 * s.dev
        rec_ref[i] = mm(x_ref[slot], pick).astype(BF)


def message_kernel(level, sub, sc, own, other, out, both):
    s = where_am_i(sc)
    g = level.g
    for k in range(3):
        both[k] = own[k]
        both[3 + k] = other[k]
    up = s.core == 0
    main = jnp.where(up, 0, g)
    corner = jnp.where(up, 3 * g, 4 * g)
    total = None
    for k in range(3):
        t = jnp.maximum(jnp.where(up, s.total - 1 - k, k), 0)
        t = jnp.minimum(t, s.total - 1)
        first = t < s.n0
        mine = first == (s.core == 0)
        idx = jnp.where(first, t, t - s.n0) + jnp.where(mine, 0, 3)
        q = s.start + t
        base = sub * k * g

        def rule(r, l):
            hit = (r - main == l - base) & (l >= base) & (l < base + g)
            if sub == 2:
                c = base + g
                hit |= (r - corner == l - c) & (l >= c) & (l < c + g)
            if k == 0:
                to = 3 * g if sub == 1 else 6 * g
                src = jnp.where(q % 2 == 0, 3 * g, 2 * g) if sub == 1 else 2 * g
                hit |= (r - src == l - to) & (l >= to) & (l < to + g)
            return hit

        part = mm(both[idx], one_hot((level.R, level.R), rule))
        total = part if total is None else total + part
    out[...] = total.astype(BF)


def stage_one_kernel(sc, home, links, x_ref, own, other, got1, got2, sw1, sw2, w_a, w_b, w_c, w_d,
                     taps, hid, slope, red, rec2, down_out,
                     recs, low_rows, high_rows, w_all, w_one):
    s = where_am_i(sc)
    dp = sc[7]
    gather_records(recs, own, other, (got1, got2), (sw1, sw2))
    low_rows[...] = rim_rows(ONE, 0)
    high_rows[...] = rim_rows(ONE, 60)
    for k, w in enumerate((w_a, w_b, w_c, w_d)):
        w_all[k] = w[...]
    for d in range(4):
        at = jnp.bitwise_xor(jnp.int32(d), dp)
        for dx in range(3):
            w_one[dx * 64 + d * 16 : dx * 64 + d * 16 + 16, :] = w_all[
                at, dx * 16 : dx * 16 + 16, 0:576
            ]
        down_out[d * 32 : d * 32 + 32, :] = w_all[at, 48:80, 0:512]
    order = parity_order()

    @pl.loop(0, 3)
    def _(i):
        at = pl.ds(pl.multiple_of(i * 128, 128), 128)
        p = s.a + jnp.minimum(i, s.n - 1)
        slot = home[p] - 3 * s.dev
        block, low, high = extended(
            ONE, s, links, recs, (low_rows[...], high_rows[...]), x_ref[slot].astype(F32), p
        )

        def store(t, v):
            taps[i, t * 64 : t * 64 + 64, :] = v

        tap_rows(ONE, block, low, high, store)
        taps[i, 576:640, :] = jnp.zeros((64, 1152), BF)
        pre = three_shifts(ONE, mm(w_one[...], taps[i, 0:576, :]))
        tall = jnp.concatenate([pre[:, 128 * b : 128 * b + 128] for b in range(8)], axis=0)
        top = tall.astype(BF)
        rest = (tall - top.astype(F32)).astype(BF)
        tall = mm(top, order) + mm(rest, order)
        parts = swap_groups([tall[64 * b : 64 * b + 64] for b in range(8)])
        for e in range(8):
            v = parts[e]
            sig = 1.0 / (1.0 + jnp.exp(-v))
            hid[e * 64 : e * 64 + 64, at] = (v * sig).astype(BF)
            slope[e * 64 : e * 64 + 64, at] = sig * (1.0 + v * (1.0 - sig))

    red[...] = mm(down_out[...], hid[...]).astype(BF)

    def rule(r, l):
        group, m = l // 16, l % 16
        high = (group == 0) & (r == (m // 2) * 16 + 14 + m % 2)
        low = (group == 1) & (r == (m // 2) * 16 + m % 2)
        return high | low | ((group == 2) & (r == m)) | ((group == 3) & (r == 112 + m))

    pick = one_hot((128, 128), rule)
    for i in range(3):
        rec2[i] = mm(red[:, i * 128 : i * 128 + 128], pick).astype(BF)


def stage_two_kernel(scale, sc, home, links, red, cot, own, other, got1, got2, sw1, sw2,
                     w_a, w_b, w_c, w_d, out, keep, give, grad, brec,
                     recs, low_rows, high_rows, w_all, w_two, taps, spread):
    s = where_am_i(sc)
    dp = sc[7]
    gather_records(recs, own, other, (got1, got2), (sw1, sw2))
    low_rows[...] = rim_rows(TWO, 0)
    high_rows[...] = rim_rows(TWO, 14)
    for k, w in enumerate((w_a, w_b, w_c, w_d)):
        w_all[k] = w[...]
    for d in range(4):
        at = jnp.bitwise_xor(jnp.int32(d), dp)
        for dx in range(3):
            w_two[dx * 128 + d * 32 : dx * 128 + d * 32 + 32, :] = w_all[
                at, :, dx * 1152 : dx * 1152 + 1152
            ]
    for i in range(3):
        p = s.a + jnp.minimum(i, s.n - 1)
        block, low, high = extended(
            TWO, s, links, recs, (low_rows[...], high_rows[...]),
            red[:, i * 128 : i * 128 + 128].astype(F32), p,
        )

        def store(t, v):
            taps[t * 128 : t * 128 + 128, i * 256 : i * 256 + 256] = v

        tap_rows(TWO, block, low, high, store)
    y = mm(w_two[...], taps[...])
    out[...] = jnp.zeros_like(out)
    for i in range(3):
        p = s.a + jnp.minimum(i, s.n - 1)
        slot = home[p] - 3 * s.dev
        v = three_shifts(TWO, y[:, i * 256 : i * 256 + 256])
        sig = 1.0 / (1.0 + jnp.exp(-v))

        @pl.when(i < s.n)
        def _():
            out[slot] = (v * sig).astype(BF)

        g = cot[slot].astype(F32) * (sig * (1.0 + v * (1.0 - sig))) * scale
        g = jnp.where(i < s.n, g, 0.0).astype(BF).astype(F32)
        g = jnp.concatenate([g, jnp.zeros_like(g)], axis=1)
        for dx in (-1, 0, 1):
            w = g if dx == 0 else pltpu.roll(g, (dx * 16) % 256, 1)
            spread[(dx + 1) * 128 : (dx + 2) * 128, i * 256 : i * 256 + 256] = w.astype(BF)
    whole = mm(spread[...], taps[...], NT)
    for dx in range(3):
        for j in range(9):
            for d in range(4):
                at, lanes = dx * 128 + d * 32, slice(j * 128, j * 128 + 128)
                first, second = whole[at : at + 16, lanes], whole[at + 16 : at + 32, lanes]
                keep[dx * 9 + j, d] = jnp.where(s.core == 0, first, second).astype(BF)
                give[dx * 9 + j, d] = jnp.where(s.core == 0, second, first).astype(BF)
    keep[27:, :, :, :] = jnp.zeros((5, 4, 16, 128), BF)
    give[27:, :, :, :] = jnp.zeros((5, 4, 16, 128), BF)
    back = mm(w_two[...], spread[...], TN)
    yy, zz = coords(TWO)
    for i in range(3):
        p = s.a + jnp.minimum(i, s.n - 1)
        even = p % 2 == 0
        by_dy = []
        for dy in range(3):
            total = None
            for dz in (-1, 0, 1):
                t = 3 * dy + dz + 1
                v = back[t * 128 : t * 128 + 128, i * 256 : i * 256 + 256]
                if dz == -1:
                    v = pltpu.roll(jnp.where(zz == 0, 0.0, v), 255, 1)
                elif dz == 1:
                    v = pltpu.roll(jnp.where(zz == 1, 0.0, v), 1, 1)
                total = v if total is None else total + v
            by_dy.append(total)
        mid = (
            by_dy[1]
            + pltpu.roll(jnp.where(yy == 0, 0.0, by_dy[0]), 254, 1)
            + pltpu.roll(jnp.where(yy == 7, 0.0, by_dy[2]), 2, 1)
        )
        grad[:, i * 128 : i * 128 + 128] = mid[:, :128]
        rim_low = mm(by_dy[0].astype(BF), low_rows[...], NT).astype(BF)
        rim_high = mm(by_dy[2].astype(BF), high_rows[...], NT).astype(BF)
        xc = jnp.where(even, 0, 7)

        def side(main_to, corner_to):
            def rule(r, l):
                main = (l >= main_to) & (l < main_to + 16) & (r == l - main_to)
                m = l - corner_to
                return main | ((m >= 0) & (m < 16) & (r - 16 == m) & (m // 2 == xc))

            return one_hot((128, 128), rule)

        x_off = jnp.where(even, 0, 112)
        x_pick = one_hot((128, 128), lambda r, l: (l >= 32) & (l < 48) & (r - x_off == l - 32))
        brec[i] = (
            mm(rim_high, side(0, 48))
            + mm(rim_low, side(16, 64))
            + mm(mid[:, 128:].astype(BF), x_pick)
        ).astype(BF)


def stage_three_kernel(sc, links, grad, own, other, got1, got2, sw1, sw2, down, hid, slope, taps,
                       out, recs, gred, g_one, spread, dw):
    s = where_am_i(sc)
    gather_records(recs, own, other, (got1, got2), (sw1, sw2))

    def rows(y_off):
        return one_hot(
            (128, 128), lambda r, l: (r < 32) & (l == ((r % 16) // 2) * 16 + r % 2 + y_off)
        )

    side_rows = (rows(0), rows(14))
    for i in range(3):
        p = s.a + jnp.minimum(i, s.n - 1)
        even = p % 2 == 0
        partner = jnp.where(even, p + 1, p - 1)
        ok_x = x_link(links, p) >= 0
        idx, off = locate_x(s, partner, TWO, 2)
        off = jnp.where(ok_x, off, NOWHERE)
        total = grad[:, i * 128 : i * 128 + 128] + mm(
            recs[idx], picker(TWO, off, jnp.where(even, 112, 0))
        )
        for side, up in ((0, True), (1, False)):
            q = p - 2 if up else p + 2
            c = partner - 2 if up else partner + 2
            ok = link_at(links, p, 2 + side) >= 0
            idx, off, _ = locate(s, q, up, TWO, 2)
            face = mm(recs[idx], picker(TWO, jnp.where(ok, off, NOWHERE), 0))
            ok_c = ok_x & (link_at(links, partner, 2 + side) >= 0)
            idx, _, off = locate(s, c, up, TWO, 2)
            face += mm(recs[idx], picker(TWO, jnp.where(ok_c, off, NOWHERE), 16))
            total += mm(face.astype(BF), side_rows[side])
        gred[:, i * 128 : i * 128 + 128] = jnp.where(i < s.n, total, 0.0).astype(BF)
    dw_down = mm(gred[...], hid[...], NT)
    g_one[...] = (mm(down[...], gred[...], TN) * slope[...]).astype(BF)
    order = parity_order()
    dw[...] = jnp.zeros_like(dw)

    @pl.loop(0, 3)
    def _(i):
        at = pl.ds(pl.multiple_of(i * 128, 128), 128)
        parts = [g_one[e * 64 : e * 64 + 64, at].astype(F32) for e in range(8)]
        tall = jnp.concatenate(swap_groups(parts), axis=0).astype(BF)
        tall = mm(tall, order, NT)
        g = jnp.concatenate(
            [tall[64 * b : 64 * b + 64] for b in range(8)] + [jnp.zeros((64, 128), F32)], axis=1
        )
        for dx in (-1, 0, 1):
            w = g if dx == 0 else pltpu.roll(g, (dx * 64) % 1152, 1)
            spread[(dx + 1) * 64 : (dx + 2) * 64, :] = w.astype(BF)
        dw[...] += mm(spread[...], taps[i], NT)

    for d in range(4):
        for j in range(5):
            for dx in range(3):
                at = dx * 64 + d * 16
                out[dx * 5 + j, d] = dw[at : at + 16, j * 128 : j * 128 + 128].astype(BF)
        for og in range(2):
            for j in range(4):
                at = d * 32 + og * 16
                out[15 + og * 4 + j, d] = dw_down[
                    at : at + 16, j * 128 : j * 128 + 128
                ].astype(BF)
    out[23:, :, :, :] = jnp.zeros((9, 4, 16, 128), BF)


def final_kernel(pieces, one_out, down_out, two_out):
    lane = lax.broadcasted_iota(jnp.int32, (16, 128), 1)
    for dx in range(3):
        for og in range(2):
            for j in range(9):
                two_out[og * 16 : og * 16 + 16, dx * 1152 + j * 128 : dx * 1152 + j * 128 + 128] = (
                    pieces[dx * 9 + j, 16 + og * 16 : 32 + og * 16, :].astype(F32)
                )
    for og in range(2):
        for j in range(4):
            down_out[og * 16 : og * 16 + 16, j * 128 : j * 128 + 128] = pieces[
                15 + og * 4 + j, 0:16, :
            ].astype(F32)

    def tile(dx, j):
        return pieces[dx * 5 + j, 0:16, :].astype(F32)

    middle = jnp.concatenate([tile(1, j) for j in range(5)], axis=1)
    middle = pltpu.roll(middle, 64, 1)
    for j in range(4):
        one_out[:, j * 128 : j * 128 + 128] = tile(0, j)
        one_out[:, 1152 + j * 128 : 1280 + j * 128] = tile(2, j)
    one_out[:, 512:640] = jnp.where(lane < 64, tile(0, 4), middle[:, :128])
    one_out[:, 640:1152] = middle[:, 128:]
    one_out[:, 1664:1728] = tile(2, 4)[:, :64]


def call(kernel, scalars, arrays, outs, scratch):
    smem = pl.BlockSpec(memory_space=pltpu.SMEM)
    vmem = pl.BlockSpec(memory_space=pltpu.VMEM)
    return pl.pallas_call(
        kernel,
        out_shape=[jax.ShapeDtypeStruct(*o) for o in outs],
        in_specs=[smem] * len(scalars) + [vmem] * len(arrays),
        out_specs=[vmem] * len(outs),
        scratch_shapes=[pltpu.VMEM(*t) for t in scratch],
        compiler_params=pltpu.CompilerParams(vmem_limit_bytes=60 << 20),
    )(*scalars, *arrays)


def swap_cores(v):
    return lax.ppermute(v, "core", [(0, 1), (1, 0)])


def chips_on(v, by):
    up = [(2 * c, 2 * (c + by)) for c in range(NCHIP - by)]
    down = [(2 * c + 1, 2 * (c - by) + 1) for c in range(by, NCHIP)]
    return lax.ppermute(v, SPACE, up + down)


def across(v, axis, k):
    return lax.ppermute(v, axis, [(i, i ^ k) for i in range(lax.axis_size(axis))])


def exchange(level, sub, sc, own):
    other = swap_cores(own)
    (message,) = call(
        functools.partial(message_kernel, level, sub), (sc,), (own, other),
        [((level.C, level.R), BF)], [((6, level.C, level.R), BF)],
    )
    got1, got2 = chips_on(message, 1), chips_on(message, 2)
    return other, got1, got2, swap_cores(got1), swap_cores(got2)


def gathered(shard):
    return [shard] + [across(shard, "dp", k) for k in (1, 2, 3)]


def on_device(features, cotangent, conv_one, down_weight, conv_two, patch_home, patch_links):
    core, dp = lax.axis_index("core"), lax.axis_index("dp")
    dev = lax.axis_index(SPACE)
    chip = dev // 2
    slots = jnp.arange(8, dtype=jnp.int32)
    marks = jnp.where(slots == 0, -2, jnp.where(slots == 4, 4, slots - 1))
    starts = jnp.sum(
        (patch_home[None, :] < 3 * (2 * chip + marks)[:, None]).astype(jnp.int32), axis=1
    )
    sc = jnp.where(
        slots < 5, starts, jnp.where(slots == 5, dev, jnp.where(slots == 6, core, dp))
    ).astype(jnp.int32)
    links = patch_links.T
    x = features[0]
    (rec_one,) = call(faces_kernel, (sc, patch_home), (x,), [((3, 64, 256), BF)], [])
    rims_one = exchange(ONE, 1, sc, rec_one)
    rows_one = jnp.pad(conv_one.reshape(16, 3, 576).swapaxes(0, 1).reshape(48, 576), ((0, 0), (0, 64)))
    w_one = gathered(jnp.concatenate([rows_one, jnp.pad(down_weight, ((0, 0), (0, 128)))]))
    w_two = gathered(conv_two)
    taps, hid, slope, red, rec_two, down_full = call(
        stage_one_kernel, (sc, patch_home, links),
        (x, rec_one, *rims_one, *w_one),
        [((3, 640, 1152), BF), ((512, 384), BF), ((512, 384), F32), ((128, 384), BF),
         ((3, 128, 128), BF), ((128, 512), BF)],
        [((10, 64, 256), BF), ((128, 1152), BF), ((128, 1152), BF), ((4, 80, 640), BF),
         ((192, 576), BF)],
    )
    rims_two = exchange(TWO, 1, sc, rec_two)
    cells = lax.axis_size("dp") * patch_links.shape[0] * 128
    out, keep, give, grad, rec_back = call(
        functools.partial(stage_two_kernel, float(cells) ** (-0.5)), (sc, patch_home, links),
        (red, cotangent[0], rec_two, *rims_two, *w_two),
        [((3, 128, 128), BF), ((32, 4, 16, 128), BF), ((32, 4, 16, 128), BF),
         ((128, 384), F32), ((3, 128, 128), BF)],
        [((10, 128, 128), BF), ((128, 256), BF), ((128, 256), BF), ((4, 32, 3456), BF),
         ((384, 1152), BF), ((1152, 768), BF), ((384, 768), BF)],
    )
    rims_back = exchange(TWO, 2, sc, rec_back)
    two = (keep.astype(F32) + swap_cores(give).astype(F32)).astype(BF)
    two = lax.all_to_all(two, ("x", "y", "core"), 0, 0, tiled=True)
    (small,) = call(
        stage_three_kernel, (sc, links),
        (grad, rec_back, *rims_back, down_full, hid, slope, taps),
        [((32, 4, 16, 128), BF)],
        [((10, 128, 128), BF), ((128, 384), BF), ((512, 384), BF), ((192, 1152), BF),
         ((192, 640), F32)],
    )
    two = two.astype(F32).reshape(16, 2, 4, 16, 128).sum(axis=0).astype(BF)
    two, small = lax.optimization_barrier((two, small))
    small = lax.all_to_all(small, ("x", "y", "core"), 0, 0, tiled=True)
    small = small.astype(F32).sum(axis=0).astype(BF)
    mine = jnp.concatenate([small, two[0], two[1]], axis=1)
    got = lax.all_to_all(jnp.concatenate([mine, mine]), ("zh", "dp"), 0, 0, tiled=True)
    mine = got.astype(F32).sum(axis=0).astype(BF)
    copies = jnp.broadcast_to(mine[None], (32, *mine.shape))
    pieces = lax.all_to_all(copies, ("x", "y", "core"), 0, 0, tiled=True)
    grads = call(
        final_kernel, (), (pieces,),
        [((16, 1728), F32), ((32, 512), F32), ((32, 3456), F32)], [],
    )
    return (out[None], *grads)


def solution(mesh):
    split = Mesh(
        mesh.devices.reshape(mesh.shape["dp"], 4, 2, 4, 2), ("dp", "x", "zh", "y", "core")
    )
    return jax.shard_map(
        on_device,
        mesh=split,
        in_specs=(
            P("dp", SPACE, None, None),
            P("dp", SPACE, None, None),
            P("dp", None),
            P("dp", None),
            P("dp", None),
            P(),
            P(),
        ),
        out_specs=(P("dp", SPACE, None, None), P("dp", None), P("dp", None), P("dp", None)),
        check_vma=False,
    )
```

```python
import functools
import types

import jax
import jax.numpy as jnp
from jax import lax
from jax.experimental import pallas as pl
from jax.experimental.pallas import tpu as pltpu
from jax.sharding import Mesh
from jax.sharding import PartitionSpec as P


BF = jnp.bfloat16
F32 = jnp.float32
SPACE = ("x", "zh", "y", "core")
NCHIP = 32
ONE = types.SimpleNamespace(C=64, g=64, R=256, N=1024, W=1152, zs=4, nx=16)
TWO = types.SimpleNamespace(C=128, g=16, R=128, N=128, W=256, zs=2, nx=8)
NOWHERE = -8192


def mm(a, b, contract=((1,), (0,))):
    return lax.dot_general(a, b, (contract, ((), ())), preferred_element_type=F32)


NT = ((1,), (1,))
TN = ((0,), (0,))


def one_hot(shape, rule):
    r = lax.broadcasted_iota(jnp.int32, shape, 0)
    l = lax.broadcasted_iota(jnp.int32, shape, 1)
    return jnp.where(rule(r, l), 1.0, 0.0).astype(BF)


def picker(level, off, dst):
    return one_hot(
        (level.R, 128),
        lambda r, l: (r - off == l - dst) & (l >= dst) & (l < dst + level.g),
    )


def corner_picker(level, off, xc):
    g, zs = level.g, level.zs
    return one_hot(
        (level.R, 128),
        lambda r, l: (r - off == l - g) & (l >= g) & (l < 2 * g) & ((l - g) // zs == xc),
    )


def rim_rows(level, y_off):
    g, zs, N, W = level.g, level.zs, level.N, level.W

    def rule(r, l):
        face = (r < g) & (l == (r // zs) * g + r % zs + y_off)
        q = r - g
        low = (q >= 0) & (q < zs) & (l == N + q + y_off)
        high = (q >= g - zs) & (q < g) & (l == W - g + q - (g - zs) + y_off)
        return face | low | high

    return one_hot((128, W), rule)


def where_am_i(sc):
    core = sc[6]
    s = types.SimpleNamespace(core=core, dev=sc[5])
    n0, n1 = sc[2] - sc[1], sc[3] - sc[2]
    s.n0 = n0
    s.total = n0 + n1
    s.start = sc[1]
    s.a = jnp.where(core == 0, sc[1], sc[2])
    s.n = jnp.where(core == 0, n0, n1)
    s.other = jnp.where(core == 0, n1, n0)
    s.chip_before = sc[1] - sc[0]
    s.chip_after = sc[4] - sc[3]
    return s


def locate(s, q, up, level, sub):
    g = level.g
    rec_off = jnp.int32(0 if up else g)
    own = (q >= s.a) & (q < s.a + s.n)
    if up:
        k = s.a - q
        near = jnp.where(s.core == 1, s.other, 0)
        o_idx = 3 + s.other - k
        m_idx = jnp.where(s.core == 0, 6, 8)
        chip = s.chip_before
    else:
        k = q - (s.a + s.n) + 1
        near = jnp.where(s.core == 0, s.other, 0)
        o_idx = 3 + k - 1
        m_idx = jnp.where(s.core == 0, 8, 6)
        chip = s.chip_after
    t = k - near
    in_o = k <= near
    far = t > chip
    idx = jnp.where(own, q - s.a, jnp.where(in_o, o_idx, jnp.where(far, m_idx + 1, m_idx)))
    in_rec = own | in_o
    main = jnp.where(in_rec, rec_off, jnp.where(far, 0, sub * (t - 1) * g))
    corner = jnp.where(in_rec, 3 * g if up else 4 * g, main + g) if sub == 2 else main
    return jnp.clip(idx, 0, 9), main, corner


def locate_x(s, q, level, sub):
    g = level.g
    rec_off = jnp.where(q % 2 == 0, 3 * g, 2 * g) if sub == 1 else jnp.int32(2 * g)
    msg_off = 3 * g if sub == 1 else 6 * g
    own = (q >= s.a) & (q < s.a + s.n)
    before = q < s.a
    in_o = jnp.where(before, s.core == 1, s.core == 0)
    o_idx = jnp.where(before, 3 + s.other - 1, 3)
    m_idx = jnp.where(before == (s.core == 0), 6, 8)
    idx = jnp.where(own, q - s.a, jnp.where(in_o, o_idx, m_idx))
    return jnp.clip(idx, 0, 9), jnp.where(own | in_o, rec_off, msg_off)


def gather_records(recs, own, other, got, swapped):
    for k in range(3):
        recs[k] = own[k]
        recs[3 + k] = other[k]
    for k in range(2):
        recs[6 + k] = got[k][...]
        recs[8 + k] = swapped[k][...]


def link_at(links, q, column):
    return links[column, jnp.clip(q, 0, 127)]


def x_link(links, q):
    return link_at(links, q, jnp.where(q % 2 == 0, 1, 0))


def extended(level, s, links, recs, rows, field, p):
    even = p % 2 == 0
    partner = jnp.where(even, p + 1, p - 1)
    idx, off = locate_x(s, partner, level, 1)
    off = jnp.where(x_link(links, p) >= 0, off, NOWHERE)
    rim = mm(recs[idx], picker(level, off, jnp.where(even, 0, 128 - level.g)))
    block = jnp.concatenate([field, rim], axis=1)
    rims = []
    for side, up in ((0, True), (1, False)):
        q = p - 2 if up else p + 2
        c = jnp.where(even, q + 1, q - 1)
        ok = link_at(links, p, 2 + side) >= 0
        idx, off, _ = locate(s, q, up, level, 1)
        face = mm(recs[idx], picker(level, jnp.where(ok, off, NOWHERE), 0))
        ok_c = ok & (x_link(links, q) >= 0)
        idx, off, _ = locate(s, c, up, level, 1)
        xc = jnp.where(even, 0, level.nx - 1)
        face += mm(recs[idx], corner_picker(level, jnp.where(ok_c, off, NOWHERE), xc))
        rims.append(mm(face.astype(BF), rows[side]))
    return block, rims[0], rims[1]


def coords(level):
    lane = lax.broadcasted_iota(jnp.int32, (level.C, level.W), 1)
    return (lane % level.g) // level.zs, lane % level.zs


def tap_rows(level, block, low, high, store):
    W, zs = level.W, level.zs
    y, z = coords(level)
    for dy in (-1, 0, 1):
        if dy == 0:
            f = block
        elif dy == -1:
            f = jnp.where(y == 0, low, pltpu.roll(block, zs, 1))
        else:
            f = jnp.where(y == level.nx - 1, high, pltpu.roll(block, W - zs, 1))
        for dz in (-1, 0, 1):
            if dz == 0:
                v = f
            elif dz == -1:
                v = jnp.where(z == 0, 0.0, pltpu.roll(f, 1, 1))
            else:
                v = jnp.where(z == zs - 1, 0.0, pltpu.roll(f, W - 1, 1))
            store(3 * (dy + 1) + dz + 1, v.astype(BF))


def three_shifts(level, y):
    C, W, g = level.C, level.W, level.g
    total = pltpu.roll(y[:C], g, 1) + y[C : 2 * C] + pltpu.roll(y[2 * C :], W - g, 1)
    return total[:, : level.N]


def parity_order():
    def rule(r, l):
        y, z = (r % 64) // 4, r % 4
        e = 4 * (r // 64) + 2 * (y % 2) + z % 2
        return l == e * 16 + (y // 2) * 2 + z // 2

    return one_hot((128, 128), rule)


def swap_groups(arrays):
    group = lax.broadcasted_iota(jnp.int32, (64, 128), 1) // 16
    arrays = list(arrays)
    for b in (1, 2, 4):
        bit = (group & b) != 0
        for i in range(8):
            if i & b:
                continue
            lo, hi = arrays[i], arrays[i + b]
            arrays[i] = jnp.where(bit, pltpu.roll(hi, 16 * b, 1), lo)
            arrays[i + b] = jnp.where(bit, hi, pltpu.roll(lo, 128 - 16 * b, 1))
    return arrays


def faces_kernel(sc, home, x_ref, rec_ref):
    s = where_am_i(sc)

    def rule(r, l):
        group, m = l // 64, l % 64
        high = (group == 0) & (r == (m // 4) * 64 + 60 + m % 4)
        low = (group == 1) & (r == (m // 4) * 64 + m % 4)
        return high | low | ((group == 2) & (r == m)) | ((group == 3) & (r == 960 + m))

    pick = one_hot((1024, 256), rule)
    for i in range(3):
        p = s.a + jnp.minimum(i, s.n - 1)
        slot = home[p] - 3 * s.dev
        rec_ref[i] = mm(x_ref[slot], pick).astype(BF)


def message_kernel(level, sub, sc, own, other, out, both):
    s = where_am_i(sc)
    g = level.g
    for k in range(3):
        both[k] = own[k]
        both[3 + k] = other[k]
    up = s.core == 0
    main = jnp.where(up, 0, g)
    corner = jnp.where(up, 3 * g, 4 * g)
    total = None
    for k in range(3):
        t = jnp.maximum(jnp.where(up, s.total - 1 - k, k), 0)
        t = jnp.minimum(t, s.total - 1)
        first = t < s.n0
        mine = first == (s.core == 0)
        idx = jnp.where(first, t, t - s.n0) + jnp.where(mine, 0, 3)
        q = s.start + t
        base = sub * k * g

        def rule(r, l):
            hit = (r - main == l - base) & (l >= base) & (l < base + g)
            if sub == 2:
                c = base + g
                hit |= (r - corner == l - c) & (l >= c) & (l < c + g)
            if k == 0:
                to = 3 * g if sub == 1 else 6 * g
                src = jnp.where(q % 2 == 0, 3 * g, 2 * g) if sub == 1 else 2 * g
                hit |= (r - src == l - to) & (l >= to) & (l < to + g)
            return hit

        part = mm(both[idx], one_hot((level.R, level.R), rule))
        total = part if total is None else total + part
    out[...] = total.astype(BF)


def both_halves(s, dp, w_all, d):
    at = jnp.bitwise_xor(jnp.int32(d), dp)
    mine, other = w_all[at].astype(F32), w_all[4 + at].astype(F32)
    return jnp.where(s.core == 0, mine, other), jnp.where(s.core == 0, other, mine)


def stage_one_kernel(sc, home, links, x_ref, own, other, got1, got2, sw1, sw2, *rest):
    weights, (taps, hid, slope, red, rec2, down_out,
                       recs, low_rows, high_rows, w_all, w_one) = rest[:8], rest[8:]
    s = where_am_i(sc)
    dp = sc[7]
    gather_records(recs, own, other, (got1, got2), (sw1, sw2))
    low_rows[...] = rim_rows(ONE, 0)
    high_rows[...] = rim_rows(ONE, 60)
    for k in range(8):
        w_all[k] = weights[k][:, :1408]
    for d in range(4):
        first, second = both_halves(s, dp, w_all, d)
        w = jnp.concatenate([first[:, :896], second[:, :896]], axis=1)
        w_one[d * 16 : d * 16 + 16, :] = w[:, :576].astype(BF)
        w_one[64 + d * 16 : 80 + d * 16, :] = pltpu.roll(w, 1792 - 576, 1)[:, :576].astype(BF)
        w_one[128 + d * 16 : 144 + d * 16, :] = w[:, 1152:1728].astype(BF)
        down_out[d * 32 : d * 32 + 16, :] = first[:, 896:].astype(BF)
        down_out[d * 32 + 16 : d * 32 + 32, :] = second[:, 896:].astype(BF)
    order = parity_order()

    @pl.loop(0, 3)
    def _(i):
        at = pl.ds(pl.multiple_of(i * 128, 128), 128)
        p = s.a + jnp.minimum(i, s.n - 1)
        slot = home[p] - 3 * s.dev
        block, low, high = extended(
            ONE, s, links, recs, (low_rows[...], high_rows[...]), x_ref[slot].astype(F32), p
        )

        def store(t, v):
            taps[i, t * 64 : t * 64 + 64, :] = v

        tap_rows(ONE, block, low, high, store)
        taps[i, 576:640, :] = jnp.zeros((64, 1152), BF)
        pre = three_shifts(ONE, mm(w_one[...], taps[i, 0:576, :]))
        tall = jnp.concatenate([pre[:, 128 * b : 128 * b + 128] for b in range(8)], axis=0)
        top = tall.astype(BF)
        rest = (tall - top.astype(F32)).astype(BF)
        tall = mm(top, order) + mm(rest, order)
        parts = swap_groups([tall[64 * b : 64 * b + 64] for b in range(8)])
        for e in range(8):
            v = parts[e]
            sig = 1.0 / (1.0 + jnp.exp(-v))
            hid[e * 64 : e * 64 + 64, at] = (v * sig).astype(BF)
            slope[e * 64 : e * 64 + 64, at] = sig * (1.0 + v * (1.0 - sig))

    red[...] = mm(down_out[...], hid[...]).astype(BF)

    def rule(r, l):
        group, m = l // 16, l % 16
        high = (group == 0) & (r == (m // 2) * 16 + 14 + m % 2)
        low = (group == 1) & (r == (m // 2) * 16 + m % 2)
        return high | low | ((group == 2) & (r == m)) | ((group == 3) & (r == 112 + m))

    pick = one_hot((128, 128), rule)
    for i in range(3):
        rec2[i] = mm(red[:, i * 128 : i * 128 + 128], pick).astype(BF)


def stage_two_kernel(scale, sc, home, links, red, cot, own, other, got1, got2, sw1, sw2,
                     *rest):
    weights, (out, keep, give, grad, brec, recs, low_rows, high_rows, w_all, w_two, taps,
              spread) = rest[:8], rest[8:]
    s = where_am_i(sc)
    dp = sc[7]
    gather_records(recs, own, other, (got1, got2), (sw1, sw2))
    low_rows[...] = rim_rows(TWO, 0)
    high_rows[...] = rim_rows(TWO, 14)
    for k in range(8):
        w_all[k] = weights[k][:, 1408:]
    for d in range(4):
        first, second = both_halves(s, dp, w_all, d)
        for dx in range(3):
            row = dx * 128 + d * 32
            w_two[row : row + 16, :] = first[:, dx * 1152 : dx * 1152 + 1152].astype(BF)
            w_two[row + 16 : row + 32, :] = second[:, dx * 1152 : dx * 1152 + 1152].astype(BF)
    for i in range(3):
        p = s.a + jnp.minimum(i, s.n - 1)
        block, low, high = extended(
            TWO, s, links, recs, (low_rows[...], high_rows[...]),
            red[:, i * 128 : i * 128 + 128].astype(F32), p,
        )

        def store(t, v):
            taps[t * 128 : t * 128 + 128, i * 256 : i * 256 + 256] = v

        tap_rows(TWO, block, low, high, store)
    y = mm(w_two[...], taps[...])
    out[...] = jnp.zeros_like(out)
    for i in range(3):
        p = s.a + jnp.minimum(i, s.n - 1)
        slot = home[p] - 3 * s.dev
        v = three_shifts(TWO, y[:, i * 256 : i * 256 + 256])
        sig = 1.0 / (1.0 + jnp.exp(-v))

        @pl.when(i < s.n)
        def _():
            out[slot] = (v * sig).astype(BF)

        g = cot[slot].astype(F32) * (sig * (1.0 + v * (1.0 - sig))) * scale
        g = jnp.where(i < s.n, g, 0.0).astype(BF).astype(F32)
        g = jnp.concatenate([g, jnp.zeros_like(g)], axis=1)
        for dx in (-1, 0, 1):
            w = g if dx == 0 else pltpu.roll(g, (dx * 16) % 256, 1)
            spread[(dx + 1) * 128 : (dx + 2) * 128, i * 256 : i * 256 + 256] = w.astype(BF)
    whole = mm(spread[...], taps[...], NT)
    for dx in range(3):
        for j in range(9):
            for d in range(4):
                at, lanes = dx * 128 + d * 32, slice(j * 128, j * 128 + 128)
                first, second = whole[at : at + 16, lanes], whole[at + 16 : at + 32, lanes]
                keep[dx * 9 + j, d] = jnp.where(s.core == 0, first, second).astype(BF)
                give[dx * 9 + j, d] = jnp.where(s.core == 0, second, first).astype(BF)
    keep[27:, :, :, :] = jnp.zeros((5, 4, 16, 128), BF)
    give[27:, :, :, :] = jnp.zeros((5, 4, 16, 128), BF)
    back = mm(w_two[...], spread[...], TN)
    yy, zz = coords(TWO)
    for i in range(3):
        p = s.a + jnp.minimum(i, s.n - 1)
        even = p % 2 == 0
        by_dy = []
        for dy in range(3):
            total = None
            for dz in (-1, 0, 1):
                t = 3 * dy + dz + 1
                v = back[t * 128 : t * 128 + 128, i * 256 : i * 256 + 256]
                if dz == -1:
                    v = pltpu.roll(jnp.where(zz == 0, 0.0, v), 255, 1)
                elif dz == 1:
                    v = pltpu.roll(jnp.where(zz == 1, 0.0, v), 1, 1)
                total = v if total is None else total + v
            by_dy.append(total)
        mid = (
            by_dy[1]
            + pltpu.roll(jnp.where(yy == 0, 0.0, by_dy[0]), 254, 1)
            + pltpu.roll(jnp.where(yy == 7, 0.0, by_dy[2]), 2, 1)
        )
        grad[:, i * 128 : i * 128 + 128] = mid[:, :128]
        rim_low = mm(by_dy[0].astype(BF), low_rows[...], NT).astype(BF)
        rim_high = mm(by_dy[2].astype(BF), high_rows[...], NT).astype(BF)
        xc = jnp.where(even, 0, 7)

        def side(main_to, corner_to):
            def rule(r, l):
                main = (l >= main_to) & (l < main_to + 16) & (r == l - main_to)
                m = l - corner_to
                return main | ((m >= 0) & (m < 16) & (r - 16 == m) & (m // 2 == xc))

            return one_hot((128, 128), rule)

        x_off = jnp.where(even, 0, 112)
        x_pick = one_hot((128, 128), lambda r, l: (l >= 32) & (l < 48) & (r - x_off == l - 32))
        brec[i] = (
            mm(rim_high, side(0, 48))
            + mm(rim_low, side(16, 64))
            + mm(mid[:, 128:].astype(BF), x_pick)
        ).astype(BF)


def stage_three_kernel(sc, links, grad, own, other, got1, got2, sw1, sw2, down, hid, slope, taps,
                       out, recs, gred, g_one, spread, dw):
    s = where_am_i(sc)
    gather_records(recs, own, other, (got1, got2), (sw1, sw2))

    def rows(y_off):
        return one_hot(
            (128, 128), lambda r, l: (r < 32) & (l == ((r % 16) // 2) * 16 + r % 2 + y_off)
        )

    side_rows = (rows(0), rows(14))
    for i in range(3):
        p = s.a + jnp.minimum(i, s.n - 1)
        even = p % 2 == 0
        partner = jnp.where(even, p + 1, p - 1)
        ok_x = x_link(links, p) >= 0
        idx, off = locate_x(s, partner, TWO, 2)
        off = jnp.where(ok_x, off, NOWHERE)
        total = grad[:, i * 128 : i * 128 + 128] + mm(
            recs[idx], picker(TWO, off, jnp.where(even, 112, 0))
        )
        for side, up in ((0, True), (1, False)):
            q = p - 2 if up else p + 2
            c = partner - 2 if up else partner + 2
            ok = link_at(links, p, 2 + side) >= 0
            idx, off, _ = locate(s, q, up, TWO, 2)
            face = mm(recs[idx], picker(TWO, jnp.where(ok, off, NOWHERE), 0))
            ok_c = ok_x & (link_at(links, partner, 2 + side) >= 0)
            idx, _, off = locate(s, c, up, TWO, 2)
            face += mm(recs[idx], picker(TWO, jnp.where(ok_c, off, NOWHERE), 16))
            total += mm(face.astype(BF), side_rows[side])
        gred[:, i * 128 : i * 128 + 128] = jnp.where(i < s.n, total, 0.0).astype(BF)
    dw_down = mm(gred[...], hid[...], NT)
    g_one[...] = (mm(down[...], gred[...], TN) * slope[...]).astype(BF)
    order = parity_order()
    dw[...] = jnp.zeros_like(dw)

    @pl.loop(0, 3)
    def _(i):
        at = pl.ds(pl.multiple_of(i * 128, 128), 128)
        parts = [g_one[e * 64 : e * 64 + 64, at].astype(F32) for e in range(8)]
        tall = jnp.concatenate(swap_groups(parts), axis=0).astype(BF)
        tall = mm(tall, order, NT)
        g = jnp.concatenate(
            [tall[64 * b : 64 * b + 64] for b in range(8)] + [jnp.zeros((64, 128), F32)], axis=1
        )
        for dx in (-1, 0, 1):
            w = g if dx == 0 else pltpu.roll(g, (dx * 64) % 1152, 1)
            spread[(dx + 1) * 64 : (dx + 2) * 64, :] = w.astype(BF)
        dw[...] += mm(spread[...], taps[i], NT)

    for d in range(4):
        for j in range(5):
            for dx in range(3):
                at = dx * 64 + d * 16
                out[dx * 5 + j, d] = dw[at : at + 16, j * 128 : j * 128 + 128].astype(BF)
        for og in range(2):
            for j in range(4):
                at = d * 32 + og * 16
                out[15 + og * 4 + j, d] = dw_down[
                    at : at + 16, j * 128 : j * 128 + 128
                ].astype(BF)
    out[23:, :, :, :] = jnp.zeros((9, 4, 16, 128), BF)


def final_kernel(pieces, one_out, down_out, two_out):
    lane = lax.broadcasted_iota(jnp.int32, (16, 128), 1)
    for dx in range(3):
        for og in range(2):
            for j in range(9):
                two_out[og * 16 : og * 16 + 16, dx * 1152 + j * 128 : dx * 1152 + j * 128 + 128] = (
                    pieces[dx * 9 + j, 16 + og * 16 : 32 + og * 16, :].astype(F32)
                )
    for og in range(2):
        for j in range(4):
            down_out[og * 16 : og * 16 + 16, j * 128 : j * 128 + 128] = pieces[
                15 + og * 4 + j, 0:16, :
            ].astype(F32)

    def tile(dx, j):
        return pieces[dx * 5 + j, 0:16, :].astype(F32)

    middle = jnp.concatenate([tile(1, j) for j in range(5)], axis=1)
    middle = pltpu.roll(middle, 64, 1)
    for j in range(4):
        one_out[:, j * 128 : j * 128 + 128] = tile(0, j)
        one_out[:, 1152 + j * 128 : 1280 + j * 128] = tile(2, j)
    one_out[:, 512:640] = jnp.where(lane < 64, tile(0, 4), middle[:, :128])
    one_out[:, 640:1152] = middle[:, 128:]
    one_out[:, 1664:1728] = tile(2, 4)[:, :64]


def call(kernel, scalars, arrays, outs, scratch):
    smem = pl.BlockSpec(memory_space=pltpu.SMEM)
    vmem = pl.BlockSpec(memory_space=pltpu.VMEM)
    return pl.pallas_call(
        kernel,
        out_shape=[jax.ShapeDtypeStruct(*o) for o in outs],
        in_specs=[smem] * len(scalars) + [vmem] * len(arrays),
        out_specs=[vmem] * len(outs),
        scratch_shapes=[pltpu.VMEM(*t) for t in scratch],
        compiler_params=pltpu.CompilerParams(vmem_limit_bytes=60 << 20),
    )(*scalars, *arrays)


def swap_cores(v):
    return lax.ppermute(v, "core", [(0, 1), (1, 0)])


def chips_on(v, by):
    up = [(2 * c, 2 * (c + by)) for c in range(NCHIP - by)]
    down = [(2 * c + 1, 2 * (c - by) + 1) for c in range(by, NCHIP)]
    return lax.ppermute(v, SPACE, up + down)


def across(v, axis, k):
    return lax.ppermute(v, axis, [(i, i ^ k) for i in range(lax.axis_size(axis))])


def exchange(level, sub, sc, own):
    other = swap_cores(own)
    (message,) = call(
        functools.partial(message_kernel, level, sub), (sc,), (own, other),
        [((level.C, level.R), BF)], [((6, level.C, level.R), BF)],
    )
    got1, got2 = chips_on(message, 1), chips_on(message, 2)
    return other, got1, got2, swap_cores(got1), swap_cores(got2)


def gathered(shard):
    return [shard] + [across(shard, "dp", k) for k in (1, 2, 3)]


def on_device(features, cotangent, conv_one, down_weight, conv_two, patch_home, patch_links):
    core, dp = lax.axis_index("core"), lax.axis_index("dp")
    dev = lax.axis_index(SPACE)
    chip = dev // 2
    slots = jnp.arange(8, dtype=jnp.int32)
    marks = jnp.where(slots == 0, -2, jnp.where(slots == 4, 4, slots - 1))
    starts = jnp.sum(
        (patch_home[None, :] < 3 * (2 * chip + marks)[:, None]).astype(jnp.int32), axis=1
    )
    sc = jnp.where(
        slots < 5, starts, jnp.where(slots == 5, dev, jnp.where(slots == 6, core, dp))
    ).astype(jnp.int32)
    links = patch_links.T
    x = features[0]
    (rec_one,) = call(faces_kernel, (sc, patch_home), (x,), [((3, 64, 256), BF)], [])
    rims_one = exchange(ONE, 1, sc, rec_one)
    one_half = jnp.where(core == 0, conv_one[:, :896], jnp.pad(conv_one[:, 896:], ((0, 0), (0, 64))))
    halves = [one_half]
    for w in (down_weight, conv_two):
        halves.append(lax.dynamic_index_in_dim(w.reshape(2, 16, -1), core, 0, keepdims=False))
    mine = gathered(jnp.concatenate(halves, axis=1))
    weights = mine + [swap_cores(w) for w in mine]
    taps, hid, slope, red, rec_two, down_full = call(
        stage_one_kernel, (sc, patch_home, links),
        (x, rec_one, *rims_one, *weights),
        [((3, 640, 1152), BF), ((512, 384), BF), ((512, 384), F32), ((128, 384), BF),
         ((3, 128, 128), BF), ((128, 512), BF)],
        [((10, 64, 256), BF), ((128, 1152), BF), ((128, 1152), BF), ((8, 16, 1408), BF),
         ((192, 576), BF)],
    )
    rims_two = exchange(TWO, 1, sc, rec_two)
    cells = lax.axis_size("dp") * patch_links.shape[0] * 128
    out, keep, give, grad, rec_back = call(
        functools.partial(stage_two_kernel, float(cells) ** (-0.5)), (sc, patch_home, links),
        (red, cotangent[0], rec_two, *rims_two, *weights),
        [((3, 128, 128), BF), ((32, 4, 16, 128), BF), ((32, 4, 16, 128), BF),
         ((128, 384), F32), ((3, 128, 128), BF)],
        [((10, 128, 128), BF), ((128, 256), BF), ((128, 256), BF), ((8, 16, 3456), BF),
         ((384, 1152), BF), ((1152, 768), BF), ((384, 768), BF)],
    )
    rims_back = exchange(TWO, 2, sc, rec_back)
    two = (keep.astype(F32) + swap_cores(give).astype(F32)).astype(BF)
    two = lax.all_to_all(two, ("x", "y", "core"), 0, 0, tiled=True)
    (small,) = call(
        stage_three_kernel, (sc, links),
        (grad, rec_back, *rims_back, down_full, hid, slope, taps),
        [((32, 4, 16, 128), BF)],
        [((10, 128, 128), BF), ((128, 384), BF), ((512, 384), BF), ((192, 1152), BF),
         ((192, 640), F32)],
    )
    two = two.astype(F32).reshape(16, 2, 4, 16, 128).sum(axis=0).astype(BF)
    two, small = lax.optimization_barrier((two, small))
    small = lax.all_to_all(small, ("x", "y", "core"), 0, 0, tiled=True)
    small = small.astype(F32).sum(axis=0).astype(BF)
    mine = jnp.concatenate([small, two[0], two[1]], axis=1)
    got = lax.all_to_all(jnp.concatenate([mine, mine]), ("zh", "dp"), 0, 0, tiled=True)
    mine = got.astype(F32).sum(axis=0).astype(BF)
    copies = jnp.broadcast_to(mine[None], (32, *mine.shape))
    pieces = lax.all_to_all(copies, ("x", "y", "core"), 0, 0, tiled=True)
    grads = call(
        final_kernel, (), (pieces,),
        [((16, 1728), F32), ((32, 512), F32), ((32, 3456), F32)], [],
    )
    return (out[None], *grads)


def solution(mesh):
    split = Mesh(
        mesh.devices.reshape(mesh.shape["dp"], 4, 2, 4, 2), ("dp", "x", "zh", "y", "core")
    )
    return jax.shard_map(
        on_device,
        mesh=split,
        in_specs=(
            P("dp", SPACE, None, None),
            P("dp", SPACE, None, None),
            P("dp", None),
            P("dp", None),
            P("dp", None),
            P(),
            P(),
        ),
        out_specs=(P("dp", SPACE, None, None), P("dp", None), P("dp", None), P("dp", None)),
        check_vma=False,
    )
```

```python
import functools
import types

import jax
import jax.numpy as jnp
from jax import lax
from jax.experimental import pallas as pl
from jax.experimental.pallas import tpu as pltpu
from jax.sharding import Mesh
from jax.sharding import PartitionSpec as P


BF = jnp.bfloat16
F32 = jnp.float32
SPACE = ("x", "zh", "y", "core")
NCHIP = 32
ONE = types.SimpleNamespace(C=64, g=64, R=256, N=1024, W=1152, zs=4, nx=16)
TWO = types.SimpleNamespace(C=128, g=16, R=128, N=128, W=256, zs=2, nx=8)
NOWHERE = -8192


def mm(a, b, contract=((1,), (0,))):
    return lax.dot_general(a, b, (contract, ((), ())), preferred_element_type=F32)


NT = ((1,), (1,))
TN = ((0,), (0,))


def one_hot(shape, rule):
    r = lax.broadcasted_iota(jnp.int32, shape, 0)
    l = lax.broadcasted_iota(jnp.int32, shape, 1)
    return jnp.where(rule(r, l), 1.0, 0.0).astype(BF)


def picker(level, off, dst):
    return one_hot(
        (level.R, 128),
        lambda r, l: (r - off == l - dst) & (l >= dst) & (l < dst + level.g),
    )


def corner_picker(level, off, xc):
    g, zs = level.g, level.zs
    return one_hot(
        (level.R, 128),
        lambda r, l: (r - off == l - g) & (l >= g) & (l < 2 * g) & ((l - g) // zs == xc),
    )


def rim_rows(level, y_off):
    g, zs, N, W = level.g, level.zs, level.N, level.W

    def rule(r, l):
        face = (r < g) & (l == (r // zs) * g + r % zs + y_off)
        q = r - g
        low = (q >= 0) & (q < zs) & (l == N + q + y_off)
        high = (q >= g - zs) & (q < g) & (l == W - g + q - (g - zs) + y_off)
        return face | low | high

    return one_hot((128, W), rule)


def where_am_i(sc):
    core = sc[6]
    s = types.SimpleNamespace(core=core, dev=sc[5])
    n0, n1 = sc[2] - sc[1], sc[3] - sc[2]
    s.n0 = n0
    s.total = n0 + n1
    s.start = sc[1]
    s.a = jnp.where(core == 0, sc[1], sc[2])
    s.n = jnp.where(core == 0, n0, n1)
    s.other = jnp.where(core == 0, n1, n0)
    s.chip_before = sc[1] - sc[0]
    s.chip_after = sc[4] - sc[3]
    return s


def locate(s, q, up, level, sub):
    g = level.g
    rec_off = jnp.int32(0 if up else g)
    own = (q >= s.a) & (q < s.a + s.n)
    if up:
        k = s.a - q
        near = jnp.where(s.core == 1, s.other, 0)
        o_idx = 3 + s.other - k
        m_idx = jnp.where(s.core == 0, 6, 8)
        chip = s.chip_before
    else:
        k = q - (s.a + s.n) + 1
        near = jnp.where(s.core == 0, s.other, 0)
        o_idx = 3 + k - 1
        m_idx = jnp.where(s.core == 0, 8, 6)
        chip = s.chip_after
    t = k - near
    in_o = k <= near
    far = t > chip
    idx = jnp.where(own, q - s.a, jnp.where(in_o, o_idx, jnp.where(far, m_idx + 1, m_idx)))
    in_rec = own | in_o
    main = jnp.where(in_rec, rec_off, jnp.where(far, 0, sub * (t - 1) * g))
    corner = jnp.where(in_rec, 3 * g if up else 4 * g, main + g) if sub == 2 else main
    return jnp.clip(idx, 0, 9), main, corner


def locate_x(s, q, level, sub):
    g = level.g
    rec_off = jnp.where(q % 2 == 0, 3 * g, 2 * g) if sub == 1 else jnp.int32(2 * g)
    msg_off = 3 * g if sub == 1 else 6 * g
    own = (q >= s.a) & (q < s.a + s.n)
    before = q < s.a
    in_o = jnp.where(before, s.core == 1, s.core == 0)
    o_idx = jnp.where(before, 3 + s.other - 1, 3)
    m_idx = jnp.where(before == (s.core == 0), 6, 8)
    idx = jnp.where(own, q - s.a, jnp.where(in_o, o_idx, m_idx))
    return jnp.clip(idx, 0, 9), jnp.where(own | in_o, rec_off, msg_off)


def gather_records(recs, own, other, got, swapped):
    for k in range(3):
        recs[k] = own[k]
        recs[3 + k] = other[k]
    for k in range(2):
        recs[6 + k] = got[k][...]
        recs[8 + k] = swapped[k][...]


def link_at(links, q, column):
    return links[column, jnp.clip(q, 0, 127)]


def x_link(links, q):
    return link_at(links, q, jnp.where(q % 2 == 0, 1, 0))


def extended(level, s, links, recs, rows, field, p):
    even = p % 2 == 0
    partner = jnp.where(even, p + 1, p - 1)
    idx, off = locate_x(s, partner, level, 1)
    off = jnp.where(x_link(links, p) >= 0, off, NOWHERE)
    rim = mm(recs[idx], picker(level, off, jnp.where(even, 0, 128 - level.g)))
    block = jnp.concatenate([field, rim], axis=1)
    rims = []
    for side, up in ((0, True), (1, False)):
        q = p - 2 if up else p + 2
        c = jnp.where(even, q + 1, q - 1)
        ok = link_at(links, p, 2 + side) >= 0
        idx, off, _ = locate(s, q, up, level, 1)
        face = mm(recs[idx], picker(level, jnp.where(ok, off, NOWHERE), 0))
        ok_c = ok & (x_link(links, q) >= 0)
        idx, off, _ = locate(s, c, up, level, 1)
        xc = jnp.where(even, 0, level.nx - 1)
        face += mm(recs[idx], corner_picker(level, jnp.where(ok_c, off, NOWHERE), xc))
        rims.append(mm(face.astype(BF), rows[side]))
    return block, rims[0], rims[1]


def coords(level):
    lane = lax.broadcasted_iota(jnp.int32, (level.C, level.W), 1)
    return (lane % level.g) // level.zs, lane % level.zs


def tap_rows(level, block, low, high, store):
    W, zs = level.W, level.zs
    y, z = coords(level)
    for dy in (-1, 0, 1):
        if dy == 0:
            f = block
        elif dy == -1:
            f = jnp.where(y == 0, low, pltpu.roll(block, zs, 1))
        else:
            f = jnp.where(y == level.nx - 1, high, pltpu.roll(block, W - zs, 1))
        for dz in (-1, 0, 1):
            if dz == 0:
                v = f
            elif dz == -1:
                v = jnp.where(z == 0, 0.0, pltpu.roll(f, 1, 1))
            else:
                v = jnp.where(z == zs - 1, 0.0, pltpu.roll(f, W - 1, 1))
            store(3 * (dy + 1) + dz + 1, v.astype(BF))


def three_shifts(level, y):
    C, W, g = level.C, level.W, level.g
    total = pltpu.roll(y[:C], g, 1) + y[C : 2 * C] + pltpu.roll(y[2 * C :], W - g, 1)
    return total[:, : level.N]


def parity_order():
    def rule(r, l):
        y, z = (r % 64) // 4, r % 4
        e = 4 * (r // 64) + 2 * (y % 2) + z % 2
        return l == e * 16 + (y // 2) * 2 + z // 2

    return one_hot((128, 128), rule)


def swap_groups(arrays):
    group = lax.broadcasted_iota(jnp.int32, (64, 128), 1) // 16
    arrays = list(arrays)
    for b in (1, 2, 4):
        bit = (group & b) != 0
        for i in range(8):
            if i & b:
                continue
            lo, hi = arrays[i], arrays[i + b]
            arrays[i] = jnp.where(bit, pltpu.roll(hi, 16 * b, 1), lo)
            arrays[i + b] = jnp.where(bit, hi, pltpu.roll(lo, 128 - 16 * b, 1))
    return arrays


def faces_kernel(sc, home, x_ref, w_ref, d_ref, rec_ref, pack_ref, wide):
    s = where_am_i(sc)

    def rule(r, l):
        group, m = l // 64, l % 64
        high = (group == 0) & (r == (m // 4) * 64 + 60 + m % 4)
        low = (group == 1) & (r == (m // 4) * 64 + m % 4)
        return high | low | ((group == 2) & (r == m)) | ((group == 3) & (r == 960 + m))

    pick = one_hot((1024, 256), rule)
    for i in range(3):
        p = s.a + jnp.minimum(i, s.n - 1)
        slot = home[p] - 3 * s.dev
        rec_ref[i] = mm(x_ref[slot], pick).astype(BF)
    wide[:, 1664:1792] = jnp.zeros((16, 128), F32)
    wide[:, 0:1728] = w_ref[...].astype(F32)
    w = wide[...]
    pack_ref[0:16, :] = w[:, :640].astype(BF)
    pack_ref[16:32, :] = pltpu.roll(w, 1792 - 576, 1)[:, :640].astype(BF)
    pack_ref[32:48, :] = w[:, 1152:].astype(BF)
    pack_ref[48:80, 0:512] = d_ref[...]
    pack_ref[48:80, 512:640] = jnp.zeros((32, 128), BF)


def message_kernel(level, sub, sc, own, other, out, both):
    s = where_am_i(sc)
    g = level.g
    for k in range(3):
        both[k] = own[k]
        both[3 + k] = other[k]
    up = s.core == 0
    main = jnp.where(up, 0, g)
    corner = jnp.where(up, 3 * g, 4 * g)
    total = None
    for k in range(3):
        t = jnp.maximum(jnp.where(up, s.total - 1 - k, k), 0)
        t = jnp.minimum(t, s.total - 1)
        first = t < s.n0
        mine = first == (s.core == 0)
        idx = jnp.where(first, t, t - s.n0) + jnp.where(mine, 0, 3)
        q = s.start + t
        base = sub * k * g

        def rule(r, l):
            hit = (r - main == l - base) & (l >= base) & (l < base + g)
            if sub == 2:
                c = base + g
                hit |= (r - corner == l - c) & (l >= c) & (l < c + g)
            if k == 0:
                to = 3 * g if sub == 1 else 6 * g
                src = jnp.where(q % 2 == 0, 3 * g, 2 * g) if sub == 1 else 2 * g
                hit |= (r - src == l - to) & (l >= to) & (l < to + g)
            return hit

        part = mm(both[idx], one_hot((level.R, level.R), rule))
        total = part if total is None else total + part
    out[...] = total.astype(BF)


def stage_one_kernel(sc, home, links, x_ref, own, other, got1, got2, sw1, sw2, w_a, w_b, w_c, w_d,
                     taps, hid, slope, red, rec2, down_out,
                     recs, low_rows, high_rows, w_all, w_one, tap_buf, sems):
    s = where_am_i(sc)
    dp = sc[7]
    gather_records(recs, own, other, (got1, got2), (sw1, sw2))
    low_rows[...] = rim_rows(ONE, 0)
    high_rows[...] = rim_rows(ONE, 60)
    for k, w in enumerate((w_a, w_b, w_c, w_d)):
        w_all[k] = w[...]
    for d in range(4):
        at = jnp.bitwise_xor(jnp.int32(d), dp)
        for dx in range(3):
            w_one[dx * 64 + d * 16 : dx * 64 + d * 16 + 16, :] = w_all[
                at, dx * 16 : dx * 16 + 16, 0:576
            ]
        down_out[d * 32 : d * 32 + 32, :] = w_all[at, 48:80, 0:512]
    order = parity_order()

    @pl.loop(0, 3)
    def _(i):
        at = pl.ds(pl.multiple_of(i * 128, 128), 128)
        p = s.a + jnp.minimum(i, s.n - 1)
        slot = home[p] - 3 * s.dev
        block, low, high = extended(
            ONE, s, links, recs, (low_rows[...], high_rows[...]), x_ref[slot].astype(F32), p
        )

        def store(t, v):
            tap_buf[i, t * 64 : t * 64 + 64, :] = v

        tap_rows(ONE, block, low, high, store)
        tap_buf[i, 576:640, :] = jnp.zeros((64, 1152), BF)
        pltpu.make_async_copy(tap_buf.at[i], taps.at[i], sems.at[i]).start()
        pre = three_shifts(ONE, mm(w_one[...], tap_buf[i, 0:576, :]))
        tall = jnp.concatenate([pre[:, 128 * b : 128 * b + 128] for b in range(8)], axis=0)
        top = tall.astype(BF)
        rest = (tall - top.astype(F32)).astype(BF)
        tall = mm(top, order) + mm(rest, order)
        parts = swap_groups([tall[64 * b : 64 * b + 64] for b in range(8)])
        for e in range(8):
            v = parts[e]
            sig = 1.0 / (1.0 + jnp.exp(-v))
            hid[e * 64 : e * 64 + 64, at] = (v * sig).astype(BF)
            slope[e * 64 : e * 64 + 64, at] = sig * (1.0 + v * (1.0 - sig))

    red[...] = mm(down_out[...], hid[...]).astype(BF)

    def rule(r, l):
        group, m = l // 16, l % 16
        high = (group == 0) & (r == (m // 2) * 16 + 14 + m % 2)
        low = (group == 1) & (r == (m // 2) * 16 + m % 2)
        return high | low | ((group == 2) & (r == m)) | ((group == 3) & (r == 112 + m))

    pick = one_hot((128, 128), rule)
    for i in range(3):
        rec2[i] = mm(red[:, i * 128 : i * 128 + 128], pick).astype(BF)
    for i in range(3):
        pltpu.make_async_copy(tap_buf.at[i], taps.at[i], sems.at[i]).wait()


def stage_two_kernel(scale, sc, home, links, red, cot, own, other, got1, got2, sw1, sw2,
                     w_a, w_b, w_c, w_d, out, keep, give, grad, brec,
                     recs, low_rows, high_rows, w_all, w_two, taps, spread):
    s = where_am_i(sc)
    dp = sc[7]
    gather_records(recs, own, other, (got1, got2), (sw1, sw2))
    low_rows[...] = rim_rows(TWO, 0)
    high_rows[...] = rim_rows(TWO, 14)
    for k, w in enumerate((w_a, w_b, w_c, w_d)):
        w_all[k] = w[...]
    for d in range(4):
        at = jnp.bitwise_xor(jnp.int32(d), dp)
        for dx in range(3):
            w_two[dx * 128 + d * 32 : dx * 128 + d * 32 + 32, :] = w_all[
                at, :, dx * 1152 : dx * 1152 + 1152
            ]
    for i in range(3):
        p = s.a + jnp.minimum(i, s.n - 1)
        block, low, high = extended(
            TWO, s, links, recs, (low_rows[...], high_rows[...]),
            red[:, i * 128 : i * 128 + 128].astype(F32), p,
        )

        def store(t, v):
            taps[t * 128 : t * 128 + 128, i * 256 : i * 256 + 256] = v

        tap_rows(TWO, block, low, high, store)
    y = mm(w_two[...], taps[...])
    out[...] = jnp.zeros_like(out)
    for i in range(3):
        p = s.a + jnp.minimum(i, s.n - 1)
        slot = home[p] - 3 * s.dev
        v = three_shifts(TWO, y[:, i * 256 : i * 256 + 256])
        sig = 1.0 / (1.0 + jnp.exp(-v))

        @pl.when(i < s.n)
        def _():
            out[slot] = (v * sig).astype(BF)

        g = cot[slot].astype(F32) * (sig * (1.0 + v * (1.0 - sig))) * scale
        g = jnp.where(i < s.n, g, 0.0).astype(BF).astype(F32)
        g = jnp.concatenate([g, jnp.zeros_like(g)], axis=1)
        for dx in (-1, 0, 1):
            w = g if dx == 0 else pltpu.roll(g, (dx * 16) % 256, 1)
            spread[(dx + 1) * 128 : (dx + 2) * 128, i * 256 : i * 256 + 256] = w.astype(BF)
    whole = mm(spread[...], taps[...], NT)
    for dx in range(3):
        for j in range(9):
            for d in range(4):
                at, lanes = dx * 128 + d * 32, slice(j * 128, j * 128 + 128)
                first, second = whole[at : at + 16, lanes], whole[at + 16 : at + 32, lanes]
                keep[dx * 9 + j, d] = jnp.where(s.core == 0, first, second).astype(BF)
                give[dx * 9 + j, d] = jnp.where(s.core == 0, second, first).astype(BF)
    keep[27:, :, :, :] = jnp.zeros((5, 4, 16, 128), BF)
    give[27:, :, :, :] = jnp.zeros((5, 4, 16, 128), BF)
    back = mm(w_two[...], spread[...], TN)
    yy, zz = coords(TWO)
    for i in range(3):
        p = s.a + jnp.minimum(i, s.n - 1)
        even = p % 2 == 0
        by_dy = []
        for dy in range(3):
            total = None
            for dz in (-1, 0, 1):
                t = 3 * dy + dz + 1
                v = back[t * 128 : t * 128 + 128, i * 256 : i * 256 + 256]
                if dz == -1:
                    v = pltpu.roll(jnp.where(zz == 0, 0.0, v), 255, 1)
                elif dz == 1:
                    v = pltpu.roll(jnp.where(zz == 1, 0.0, v), 1, 1)
                total = v if total is None else total + v
            by_dy.append(total)
        mid = (
            by_dy[1]
            + pltpu.roll(jnp.where(yy == 0, 0.0, by_dy[0]), 254, 1)
            + pltpu.roll(jnp.where(yy == 7, 0.0, by_dy[2]), 2, 1)
        )
        grad[:, i * 128 : i * 128 + 128] = mid[:, :128]
        rim_low = mm(by_dy[0].astype(BF), low_rows[...], NT).astype(BF)
        rim_high = mm(by_dy[2].astype(BF), high_rows[...], NT).astype(BF)
        xc = jnp.where(even, 0, 7)

        def side(main_to, corner_to):
            def rule(r, l):
                main = (l >= main_to) & (l < main_to + 16) & (r == l - main_to)
                m = l - corner_to
                return main | ((m >= 0) & (m < 16) & (r - 16 == m) & (m // 2 == xc))

            return one_hot((128, 128), rule)

        x_off = jnp.where(even, 0, 112)
        x_pick = one_hot((128, 128), lambda r, l: (l >= 32) & (l < 48) & (r - x_off == l - 32))
        brec[i] = (
            mm(rim_high, side(0, 48))
            + mm(rim_low, side(16, 64))
            + mm(mid[:, 128:].astype(BF), x_pick)
        ).astype(BF)


def stage_three_kernel(sc, links, grad, own, other, got1, got2, sw1, sw2, down, hid, slope, taps,
                       out, recs, gred, g_one, spread, dw, tap_buf, sems):
    for i in range(3):
        pltpu.make_async_copy(taps.at[i], tap_buf.at[i], sems.at[i]).start()
    s = where_am_i(sc)
    gather_records(recs, own, other, (got1, got2), (sw1, sw2))

    def rows(y_off):
        return one_hot(
            (128, 128), lambda r, l: (r < 32) & (l == ((r % 16) // 2) * 16 + r % 2 + y_off)
        )

    side_rows = (rows(0), rows(14))
    for i in range(3):
        p = s.a + jnp.minimum(i, s.n - 1)
        even = p % 2 == 0
        partner = jnp.where(even, p + 1, p - 1)
        ok_x = x_link(links, p) >= 0
        idx, off = locate_x(s, partner, TWO, 2)
        off = jnp.where(ok_x, off, NOWHERE)
        total = grad[:, i * 128 : i * 128 + 128] + mm(
            recs[idx], picker(TWO, off, jnp.where(even, 112, 0))
        )
        for side, up in ((0, True), (1, False)):
            q = p - 2 if up else p + 2
            c = partner - 2 if up else partner + 2
            ok = link_at(links, p, 2 + side) >= 0
            idx, off, _ = locate(s, q, up, TWO, 2)
            face = mm(recs[idx], picker(TWO, jnp.where(ok, off, NOWHERE), 0))
            ok_c = ok_x & (link_at(links, partner, 2 + side) >= 0)
            idx, _, off = locate(s, c, up, TWO, 2)
            face += mm(recs[idx], picker(TWO, jnp.where(ok_c, off, NOWHERE), 16))
            total += mm(face.astype(BF), side_rows[side])
        gred[:, i * 128 : i * 128 + 128] = jnp.where(i < s.n, total, 0.0).astype(BF)
    dw_down = mm(gred[...], hid[...], NT)
    g_one[...] = (mm(down[...], gred[...], TN) * slope[...]).astype(BF)
    order = parity_order()
    dw[...] = jnp.zeros_like(dw)

    @pl.loop(0, 3)
    def _(i):
        at = pl.ds(pl.multiple_of(i * 128, 128), 128)
        parts = [g_one[e * 64 : e * 64 + 64, at].astype(F32) for e in range(8)]
        tall = jnp.concatenate(swap_groups(parts), axis=0).astype(BF)
        tall = mm(tall, order, NT)
        g = jnp.concatenate(
            [tall[64 * b : 64 * b + 64] for b in range(8)] + [jnp.zeros((64, 128), F32)], axis=1
        )
        for dx in (-1, 0, 1):
            w = g if dx == 0 else pltpu.roll(g, (dx * 64) % 1152, 1)
            spread[(dx + 1) * 64 : (dx + 2) * 64, :] = w.astype(BF)
        pltpu.make_async_copy(taps.at[i], tap_buf.at[i], sems.at[i]).wait()
        dw[...] += mm(spread[...], tap_buf[i], NT)

    for d in range(4):
        for j in range(5):
            for dx in range(3):
                at = dx * 64 + d * 16
                out[dx * 5 + j, d] = dw[at : at + 16, j * 128 : j * 128 + 128].astype(BF)
        for og in range(2):
            for j in range(4):
                at = d * 32 + og * 16
                out[15 + og * 4 + j, d] = dw_down[
                    at : at + 16, j * 128 : j * 128 + 128
                ].astype(BF)
    out[23:, :, :, :] = jnp.zeros((9, 4, 16, 128), BF)


def final_kernel(pieces, one_out, down_out, two_out):
    lane = lax.broadcasted_iota(jnp.int32, (16, 128), 1)
    for dx in range(3):
        for og in range(2):
            for j in range(9):
                two_out[og * 16 : og * 16 + 16, dx * 1152 + j * 128 : dx * 1152 + j * 128 + 128] = (
                    pieces[dx * 9 + j, 16 + og * 16 : 32 + og * 16, :].astype(F32)
                )
    for og in range(2):
        for j in range(4):
            down_out[og * 16 : og * 16 + 16, j * 128 : j * 128 + 128] = pieces[
                15 + og * 4 + j, 0:16, :
            ].astype(F32)

    def tile(dx, j):
        return pieces[dx * 5 + j, 0:16, :].astype(F32)

    middle = jnp.concatenate([tile(1, j) for j in range(5)], axis=1)
    middle = pltpu.roll(middle, 64, 1)
    for j in range(4):
        one_out[:, j * 128 : j * 128 + 128] = tile(0, j)
        one_out[:, 1152 + j * 128 : 1280 + j * 128] = tile(2, j)
    one_out[:, 512:640] = jnp.where(lane < 64, tile(0, 4), middle[:, :128])
    one_out[:, 640:1152] = middle[:, 128:]
    one_out[:, 1664:1728] = tile(2, 4)[:, :64]


def call(kernel, scalars, arrays, outs, scratch, far_in=(), far_out=(), copies=0):
    smem = pl.BlockSpec(memory_space=pltpu.SMEM)
    vmem = pl.BlockSpec(memory_space=pltpu.VMEM)
    far = pl.BlockSpec(memory_space=pl.ANY)
    sems = [pltpu.SemaphoreType.DMA((copies,))] if copies else []
    return pl.pallas_call(
        kernel,
        out_shape=[jax.ShapeDtypeStruct(*o) for o in outs],
        in_specs=[smem] * len(scalars)
        + [far if k in far_in else vmem for k in range(len(arrays))],
        out_specs=[far if k in far_out else vmem for k in range(len(outs))],
        scratch_shapes=[pltpu.VMEM(*t) for t in scratch] + sems,
        compiler_params=pltpu.CompilerParams(vmem_limit_bytes=60 << 20),
    )(*scalars, *arrays)


def swap_cores(v):
    return lax.ppermute(v, "core", [(0, 1), (1, 0)])


def chips_on(v, by):
    up = [(2 * c, 2 * (c + by)) for c in range(NCHIP - by)]
    down = [(2 * c + 1, 2 * (c - by) + 1) for c in range(by, NCHIP)]
    return lax.ppermute(v, SPACE, up + down)


def across(v, axis, k):
    return lax.ppermute(v, axis, [(i, i ^ k) for i in range(lax.axis_size(axis))])


def exchange(level, sub, sc, own):
    other = swap_cores(own)
    (message,) = call(
        functools.partial(message_kernel, level, sub), (sc,), (own, other),
        [((level.C, level.R), BF)], [((6, level.C, level.R), BF)],
    )
    got1, got2 = chips_on(message, 1), chips_on(message, 2)
    return other, got1, got2, swap_cores(got1), swap_cores(got2)


def gathered(shard):
    return [shard] + [across(shard, "dp", k) for k in (1, 2, 3)]


def on_device(features, cotangent, conv_one, down_weight, conv_two, patch_home, patch_links):
    core, dp = lax.axis_index("core"), lax.axis_index("dp")
    dev = lax.axis_index(SPACE)
    chip = dev // 2
    slots = jnp.arange(8, dtype=jnp.int32)
    marks = jnp.where(slots == 0, -2, jnp.where(slots == 4, 4, slots - 1))
    starts = jnp.sum(
        (patch_home[None, :] < 3 * (2 * chip + marks)[:, None]).astype(jnp.int32), axis=1
    )
    sc = jnp.where(
        slots < 5, starts, jnp.where(slots == 5, dev, jnp.where(slots == 6, core, dp))
    ).astype(jnp.int32)
    links = patch_links.T
    x = features[0]
    rec_one, packed = call(
        faces_kernel, (sc, patch_home), (x, conv_one, down_weight),
        [((3, 64, 256), BF), ((80, 640), BF)], [((16, 1792), F32)],
    )
    rims_one = exchange(ONE, 1, sc, rec_one)
    w_one = gathered(packed)
    w_two = gathered(conv_two)
    taps, hid, slope, red, rec_two, down_full = call(
        stage_one_kernel, (sc, patch_home, links),
        (x, rec_one, *rims_one, *w_one),
        [((3, 640, 1152), BF), ((512, 384), BF), ((512, 384), F32), ((128, 384), BF),
         ((3, 128, 128), BF), ((128, 512), BF)],
        [((10, 64, 256), BF), ((128, 1152), BF), ((128, 1152), BF), ((4, 80, 640), BF),
         ((192, 576), BF), ((3, 640, 1152), BF)],
        far_out=(0,), copies=3,
    )
    rims_two = exchange(TWO, 1, sc, rec_two)
    cells = lax.axis_size("dp") * patch_links.shape[0] * 128
    out, keep, give, grad, rec_back = call(
        functools.partial(stage_two_kernel, float(cells) ** (-0.5)), (sc, patch_home, links),
        (red, cotangent[0], rec_two, *rims_two, *w_two),
        [((3, 128, 128), BF), ((32, 4, 16, 128), BF), ((32, 4, 16, 128), BF),
         ((128, 384), F32), ((3, 128, 128), BF)],
        [((10, 128, 128), BF), ((128, 256), BF), ((128, 256), BF), ((4, 32, 3456), BF),
         ((384, 1152), BF), ((1152, 768), BF), ((384, 768), BF)],
    )
    rims_back = exchange(TWO, 2, sc, rec_back)
    two = (keep.astype(F32) + swap_cores(give).astype(F32)).astype(BF)
    two = lax.all_to_all(two, ("x", "y", "core"), 0, 0, tiled=True)
    (small,) = call(
        stage_three_kernel, (sc, links),
        (grad, rec_back, *rims_back, down_full, hid, slope, taps),
        [((32, 4, 16, 128), BF)],
        [((10, 128, 128), BF), ((128, 384), BF), ((512, 384), BF), ((192, 1152), BF),
         ((192, 640), F32), ((3, 640, 1152), BF)],
        far_in=(10,), copies=3,
    )
    two = two.astype(F32).reshape(16, 2, 4, 16, 128).sum(axis=0).astype(BF)
    two, small = lax.optimization_barrier((two, small))
    small = lax.all_to_all(small, ("x", "y", "core"), 0, 0, tiled=True)
    small = small.astype(F32).sum(axis=0).astype(BF)
    mine = jnp.concatenate([small, two[0], two[1]], axis=1)
    got = lax.all_to_all(jnp.concatenate([mine, mine]), ("zh", "dp"), 0, 0, tiled=True)
    mine = got.astype(F32).sum(axis=0).astype(BF)
    copies = jnp.broadcast_to(mine[None], (32, *mine.shape))
    pieces = lax.all_to_all(copies, ("x", "y", "core"), 0, 0, tiled=True)
    grads = call(
        final_kernel, (), (pieces,),
        [((16, 1728), F32), ((32, 512), F32), ((32, 3456), F32)], [],
    )
    return (out[None], *grads)


def solution(mesh):
    split = Mesh(
        mesh.devices.reshape(mesh.shape["dp"], 4, 2, 4, 2), ("dp", "x", "zh", "y", "core")
    )
    return jax.shard_map(
        on_device,
        mesh=split,
        in_specs=(
            P("dp", SPACE, None, None),
            P("dp", SPACE, None, None),
            P("dp", None),
            P("dp", None),
            P("dp", None),
            P(),
            P(),
        ),
        out_specs=(P("dp", SPACE, None, None), P("dp", None), P("dp", None), P("dp", None)),
        check_vma=False,
    )
```

```python
import functools
import types

import jax
import jax.numpy as jnp
from jax import lax
from jax.experimental import pallas as pl
from jax.experimental.pallas import tpu as pltpu
from jax.sharding import Mesh
from jax.sharding import PartitionSpec as P


BF = jnp.bfloat16
F32 = jnp.float32
SPACE = ("x", "zh", "y", "core")
NCHIP = 32
ONE = types.SimpleNamespace(C=64, g=64, R=256, N=1024, W=1152, zs=4, nx=16)
TWO = types.SimpleNamespace(C=128, g=16, R=128, N=128, W=256, zs=2, nx=8)
NOWHERE = -8192


def mm(a, b, contract=((1,), (0,))):
    return lax.dot_general(a, b, (contract, ((), ())), preferred_element_type=F32)


NT = ((1,), (1,))
TN = ((0,), (0,))


def div(v, n):
    return lax.shift_right_arithmetic(v, jnp.int32(n.bit_length() - 1))


def mod(v, n):
    return lax.bitwise_and(v, jnp.int32(n - 1))


def one_hot(shape, rule):
    r = lax.broadcasted_iota(jnp.int32, shape, 0)
    l = lax.broadcasted_iota(jnp.int32, shape, 1)
    return jnp.where(rule(r, l), 1.0, 0.0).astype(BF)


def picker(level, off, dst):
    return one_hot(
        (level.R, 128),
        lambda r, l: (r - off == l - dst) & (l >= dst) & (l < dst + level.g),
    )


def corner_picker(level, off, xc):
    g, zs = level.g, level.zs
    return one_hot(
        (level.R, 128),
        lambda r, l: (r - off == l - g) & (l >= g) & (l < 2 * g) & (div(l - g, zs) == xc),
    )


def rim_rows(level, y_off):
    g, zs, N, W = level.g, level.zs, level.N, level.W

    def rule(r, l):
        face = (r < g) & (l == div(r, zs) * g + mod(r, zs) + y_off)
        q = r - g
        low = (q >= 0) & (q < zs) & (l == N + q + y_off)
        high = (q >= g - zs) & (q < g) & (l == W - g + q - (g - zs) + y_off)
        return face | low | high

    return one_hot((128, W), rule)


def where_am_i(sc):
    core = sc[6]
    s = types.SimpleNamespace(core=core, dev=sc[5])
    n0, n1 = sc[2] - sc[1], sc[3] - sc[2]
    s.n0 = n0
    s.total = n0 + n1
    s.start = sc[1]
    s.a = jnp.where(core == 0, sc[1], sc[2])
    s.n = jnp.where(core == 0, n0, n1)
    s.other = jnp.where(core == 0, n1, n0)
    s.chip_before = sc[1] - sc[0]
    s.chip_after = sc[4] - sc[3]
    return s


def locate(s, q, up, level, sub):
    g = level.g
    rec_off = jnp.int32(0 if up else g)
    own = (q >= s.a) & (q < s.a + s.n)
    if up:
        k = s.a - q
        near = jnp.where(s.core == 1, s.other, 0)
        o_idx = 3 + s.other - k
        m_idx = jnp.where(s.core == 0, 6, 8)
        chip = s.chip_before
    else:
        k = q - (s.a + s.n) + 1
        near = jnp.where(s.core == 0, s.other, 0)
        o_idx = 3 + k - 1
        m_idx = jnp.where(s.core == 0, 8, 6)
        chip = s.chip_after
    t = k - near
    in_o = k <= near
    far = t > chip
    idx = jnp.where(own, q - s.a, jnp.where(in_o, o_idx, jnp.where(far, m_idx + 1, m_idx)))
    in_rec = own | in_o
    main = jnp.where(in_rec, rec_off, jnp.where(far, 0, sub * (t - 1) * g))
    corner = jnp.where(in_rec, 3 * g if up else 4 * g, main + g) if sub == 2 else main
    return jnp.clip(idx, 0, 9), main, corner


def locate_x(s, q, level, sub):
    g = level.g
    rec_off = jnp.where(q % 2 == 0, 3 * g, 2 * g) if sub == 1 else jnp.int32(2 * g)
    msg_off = 3 * g if sub == 1 else 6 * g
    own = (q >= s.a) & (q < s.a + s.n)
    before = q < s.a
    in_o = jnp.where(before, s.core == 1, s.core == 0)
    o_idx = jnp.where(before, 3 + s.other - 1, 3)
    m_idx = jnp.where(before == (s.core == 0), 6, 8)
    idx = jnp.where(own, q - s.a, jnp.where(in_o, o_idx, m_idx))
    return jnp.clip(idx, 0, 9), jnp.where(own | in_o, rec_off, msg_off)


def gather_records(recs, own, other, got, swapped):
    for k in range(3):
        recs[k] = own[k]
        recs[3 + k] = other[k]
    for k in range(2):
        recs[6 + k] = got[k][...]
        recs[8 + k] = swapped[k][...]


def link_at(links, q, column):
    return links[column, jnp.clip(q, 0, 127)]


def x_link(links, q):
    return link_at(links, q, jnp.where(q % 2 == 0, 1, 0))


def extended(level, s, links, recs, rows, field, p):
    even = p % 2 == 0
    partner = jnp.where(even, p + 1, p - 1)
    idx, off = locate_x(s, partner, level, 1)
    off = jnp.where(x_link(links, p) >= 0, off, NOWHERE)
    rim = mm(recs[idx], picker(level, off, jnp.where(even, 0, 128 - level.g)))
    block = jnp.concatenate([field, rim], axis=1)
    rims = []
    for side, up in ((0, True), (1, False)):
        q = p - 2 if up else p + 2
        c = jnp.where(even, q + 1, q - 1)
        ok = link_at(links, p, 2 + side) >= 0
        idx, off, _ = locate(s, q, up, level, 1)
        face = mm(recs[idx], picker(level, jnp.where(ok, off, NOWHERE), 0))
        ok_c = ok & (x_link(links, q) >= 0)
        idx, off, _ = locate(s, c, up, level, 1)
        xc = jnp.where(even, 0, level.nx - 1)
        face += mm(recs[idx], corner_picker(level, jnp.where(ok_c, off, NOWHERE), xc))
        rims.append(mm(face.astype(BF), rows[side]))
    return block, rims[0], rims[1]


def coords(level):
    lane = lax.broadcasted_iota(jnp.int32, (level.C, level.W), 1)
    return div(mod(lane, level.g), level.zs), mod(lane, level.zs)


def tap_rows(level, block, low, high, store):
    W, zs = level.W, level.zs
    y, z = coords(level)
    for dy in (-1, 0, 1):
        if dy == 0:
            f = block
        elif dy == -1:
            f = jnp.where(y == 0, low, pltpu.roll(block, zs, 1))
        else:
            f = jnp.where(y == level.nx - 1, high, pltpu.roll(block, W - zs, 1))
        for dz in (-1, 0, 1):
            if dz == 0:
                v = f
            elif dz == -1:
                v = jnp.where(z == 0, 0.0, pltpu.roll(f, 1, 1))
            else:
                v = jnp.where(z == zs - 1, 0.0, pltpu.roll(f, W - 1, 1))
            store(3 * (dy + 1) + dz + 1, v.astype(BF))


def three_shifts(level, y):
    C, W, g = level.C, level.W, level.g
    total = pltpu.roll(y[:C], g, 1) + y[C : 2 * C] + pltpu.roll(y[2 * C :], W - g, 1)
    return total[:, : level.N]


def parity_order():
    def rule(r, l):
        y, z = div(mod(r, 64), 4), mod(r, 4)
        e = 4 * div(r, 64) + 2 * mod(y, 2) + mod(z, 2)
        return l == e * 16 + div(y, 2) * 2 + div(z, 2)

    return one_hot((128, 128), rule)


def swap_groups(arrays):
    group = div(lax.broadcasted_iota(jnp.int32, (64, 128), 1), 16)
    arrays = list(arrays)
    for b in (1, 2, 4):
        bit = (group & b) != 0
        for i in range(8):
            if i & b:
                continue
            lo, hi = arrays[i], arrays[i + b]
            arrays[i] = jnp.where(bit, pltpu.roll(hi, 16 * b, 1), lo)
            arrays[i + b] = jnp.where(bit, hi, pltpu.roll(lo, 128 - 16 * b, 1))
    return arrays


def faces_kernel(sc, home, x_ref, w_ref, d_ref, rec_ref, pack_ref, wide):
    s = where_am_i(sc)

    def rule(r, l):
        group, m = div(l, 64), mod(l, 64)
        at = div(m, 4) * 64 + mod(m, 4)
        at = jnp.where(group == 0, at + 60, at)
        return r == jnp.where(group == 2, m, jnp.where(group == 3, m + 960, at))

    pick = one_hot((1024, 256), rule)
    for i in range(3):
        p = s.a + jnp.minimum(i, s.n - 1)
        slot = home[p] - 3 * s.dev
        rec_ref[i] = mm(x_ref[slot], pick).astype(BF)
    wide[:, 1664:1792] = jnp.zeros((16, 128), F32)
    wide[:, 0:1728] = w_ref[...].astype(F32)
    w = wide[...]
    pack_ref[0:16, :] = w[:, :640].astype(BF)
    pack_ref[16:32, :] = pltpu.roll(w, 1792 - 576, 1)[:, :640].astype(BF)
    pack_ref[32:48, :] = w[:, 1152:].astype(BF)
    pack_ref[48:80, 0:512] = d_ref[...]
    pack_ref[48:80, 512:640] = jnp.zeros((32, 128), BF)


def message_kernel(level, sub, sc, own, other, out, both):
    s = where_am_i(sc)
    g = level.g
    for k in range(3):
        both[k] = own[k]
        both[3 + k] = other[k]
    up = s.core == 0
    main = jnp.where(up, 0, g)
    corner = jnp.where(up, 3 * g, 4 * g)
    total = None
    for k in range(3):
        t = jnp.maximum(jnp.where(up, s.total - 1 - k, k), 0)
        t = jnp.minimum(t, s.total - 1)
        first = t < s.n0
        mine = first == (s.core == 0)
        idx = jnp.where(first, t, t - s.n0) + jnp.where(mine, 0, 3)
        q = s.start + t
        base = sub * k * g

        def rule(r, l):
            hit = (r - main == l - base) & (l >= base) & (l < base + g)
            if sub == 2:
                c = base + g
                hit |= (r - corner == l - c) & (l >= c) & (l < c + g)
            if k == 0:
                to = 3 * g if sub == 1 else 6 * g
                src = jnp.where(q % 2 == 0, 3 * g, 2 * g) if sub == 1 else 2 * g
                hit |= (r - src == l - to) & (l >= to) & (l < to + g)
            return hit

        part = mm(both[idx], one_hot((level.R, level.R), rule))
        total = part if total is None else total + part
    out[...] = total.astype(BF)


def stage_one_kernel(sc, home, links, x_ref, own, other, got1, got2, sw1, sw2, w_a, w_b, w_c, w_d,
                     taps, hid, slope, red, rec2, down_out,
                     recs, low_rows, high_rows, w_all, w_one, tap_buf, sems):
    s = where_am_i(sc)
    dp = sc[7]
    gather_records(recs, own, other, (got1, got2), (sw1, sw2))
    low_rows[...] = rim_rows(ONE, 0)
    high_rows[...] = rim_rows(ONE, 60)
    for k, w in enumerate((w_a, w_b, w_c, w_d)):
        w_all[k] = w[...]
    for d in range(4):
        at = jnp.bitwise_xor(jnp.int32(d), dp)
        for dx in range(3):
            w_one[dx * 64 + d * 16 : dx * 64 + d * 16 + 16, :] = w_all[
                at, dx * 16 : dx * 16 + 16, 0:576
            ]
        down_out[d * 32 : d * 32 + 32, :] = w_all[at, 48:80, 0:512]
    order = parity_order()

    @pl.loop(0, 3)
    def _(i):
        at = pl.ds(pl.multiple_of(i * 128, 128), 128)
        p = s.a + jnp.minimum(i, s.n - 1)
        slot = home[p] - 3 * s.dev
        block, low, high = extended(
            ONE, s, links, recs, (low_rows[...], high_rows[...]), x_ref[slot].astype(F32), p
        )

        def store(t, v):
            tap_buf[i, t * 64 : t * 64 + 64, :] = v

        tap_rows(ONE, block, low, high, store)
        tap_buf[i, 576:640, :] = jnp.zeros((64, 1152), BF)
        pltpu.make_async_copy(tap_buf.at[i], taps.at[i], sems.at[i]).start()
        pre = three_shifts(ONE, mm(w_one[...], tap_buf[i, 0:576, :]))
        tall = jnp.concatenate([pre[:, 128 * b : 128 * b + 128] for b in range(8)], axis=0)
        top = tall.astype(BF)
        rest = (tall - top.astype(F32)).astype(BF)
        tall = mm(top, order) + mm(rest, order)
        parts = swap_groups([tall[64 * b : 64 * b + 64] for b in range(8)])
        for e in range(8):
            v = parts[e]
            sig = 1.0 / (1.0 + jnp.exp(-v))
            hid[e * 64 : e * 64 + 64, at] = (v * sig).astype(BF)
            slope[e * 64 : e * 64 + 64, at] = sig * (1.0 + v * (1.0 - sig))

    red[...] = mm(down_out[...], hid[...]).astype(BF)

    def rule(r, l):
        group, m = div(l, 16), mod(l, 16)
        at = div(m, 2) * 16 + mod(m, 2)
        at = jnp.where(group == 0, at + 14, at)
        at = jnp.where(group == 2, m, jnp.where(group == 3, m + 112, at))
        return (group < 4) & (r == at)

    pick = one_hot((128, 128), rule)
    for i in range(3):
        rec2[i] = mm(red[:, i * 128 : i * 128 + 128], pick).astype(BF)
    for i in range(3):
        pltpu.make_async_copy(tap_buf.at[i], taps.at[i], sems.at[i]).wait()


def stage_two_kernel(scale, sc, home, links, red, cot, own, other, got1, got2, sw1, sw2,
                     w_a, w_b, w_c, w_d, out, keep, give, grad, brec,
                     recs, low_rows, high_rows, w_all, w_two, taps, spread):
    s = where_am_i(sc)
    dp = sc[7]
    gather_records(recs, own, other, (got1, got2), (sw1, sw2))
    low_rows[...] = rim_rows(TWO, 0)
    high_rows[...] = rim_rows(TWO, 14)
    for k, w in enumerate((w_a, w_b, w_c, w_d)):
        w_all[k] = w[...]
    for d in range(4):
        at = jnp.bitwise_xor(jnp.int32(d), dp)
        for dx in range(3):
            w_two[dx * 128 + d * 32 : dx * 128 + d * 32 + 32, :] = w_all[
                at, :, dx * 1152 : dx * 1152 + 1152
            ]
    for i in range(3):
        p = s.a + jnp.minimum(i, s.n - 1)
        block, low, high = extended(
            TWO, s, links, recs, (low_rows[...], high_rows[...]),
            red[:, i * 128 : i * 128 + 128].astype(F32), p,
        )

        def store(t, v):
            taps[t * 128 : t * 128 + 128, i * 256 : i * 256 + 256] = v

        tap_rows(TWO, block, low, high, store)
    y = mm(w_two[...], taps[...])
    out[...] = jnp.zeros_like(out)
    for i in range(3):
        p = s.a + jnp.minimum(i, s.n - 1)
        slot = home[p] - 3 * s.dev
        v = three_shifts(TWO, y[:, i * 256 : i * 256 + 256])
        sig = 1.0 / (1.0 + jnp.exp(-v))

        @pl.when(i < s.n)
        def _():
            out[slot] = (v * sig).astype(BF)

        g = cot[slot].astype(F32) * (sig * (1.0 + v * (1.0 - sig))) * scale
        g = jnp.where(i < s.n, g, 0.0).astype(BF).astype(F32)
        g = jnp.concatenate([g, jnp.zeros_like(g)], axis=1)
        for dx in (-1, 0, 1):
            w = g if dx == 0 else pltpu.roll(g, (dx * 16) % 256, 1)
            spread[(dx + 1) * 128 : (dx + 2) * 128, i * 256 : i * 256 + 256] = w.astype(BF)
    whole = mm(spread[...], taps[...], NT)
    for dx in range(3):
        for j in range(9):
            for d in range(4):
                at, lanes = dx * 128 + d * 32, slice(j * 128, j * 128 + 128)
                first, second = whole[at : at + 16, lanes], whole[at + 16 : at + 32, lanes]
                keep[dx * 9 + j, d] = jnp.where(s.core == 0, first, second).astype(BF)
                give[dx * 9 + j, d] = jnp.where(s.core == 0, second, first).astype(BF)
    keep[27:, :, :, :] = jnp.zeros((5, 4, 16, 128), BF)
    give[27:, :, :, :] = jnp.zeros((5, 4, 16, 128), BF)
    back = mm(w_two[...], spread[...], TN)
    yy, zz = coords(TWO)
    for i in range(3):
        p = s.a + jnp.minimum(i, s.n - 1)
        even = p % 2 == 0
        by_dy = []
        for dy in range(3):
            total = None
            for dz in (-1, 0, 1):
                t = 3 * dy + dz + 1
                v = back[t * 128 : t * 128 + 128, i * 256 : i * 256 + 256]
                if dz == -1:
                    v = pltpu.roll(jnp.where(zz == 0, 0.0, v), 255, 1)
                elif dz == 1:
                    v = pltpu.roll(jnp.where(zz == 1, 0.0, v), 1, 1)
                total = v if total is None else total + v
            by_dy.append(total)
        mid = (
            by_dy[1]
            + pltpu.roll(jnp.where(yy == 0, 0.0, by_dy[0]), 254, 1)
            + pltpu.roll(jnp.where(yy == 7, 0.0, by_dy[2]), 2, 1)
        )
        grad[:, i * 128 : i * 128 + 128] = mid[:, :128]
        rim_low = mm(by_dy[0].astype(BF), low_rows[...], NT).astype(BF)
        rim_high = mm(by_dy[2].astype(BF), high_rows[...], NT).astype(BF)
        xc = jnp.where(even, 0, 7)

        def side(main_to, corner_to):
            def rule(r, l):
                main = (l >= main_to) & (l < main_to + 16) & (r == l - main_to)
                m = l - corner_to
                return main | ((m >= 0) & (m < 16) & (r - 16 == m) & (div(m, 2) == xc))

            return one_hot((128, 128), rule)

        x_off = jnp.where(even, 0, 112)
        x_pick = one_hot((128, 128), lambda r, l: (l >= 32) & (l < 48) & (r - x_off == l - 32))
        brec[i] = (
            mm(rim_high, side(0, 48))
            + mm(rim_low, side(16, 64))
            + mm(mid[:, 128:].astype(BF), x_pick)
        ).astype(BF)


def stage_three_kernel(sc, links, grad, own, other, got1, got2, sw1, sw2, down, hid, slope, taps,
                       out, recs, gred, g_one, spread, dw, tap_buf, sems):
    for i in range(3):
        pltpu.make_async_copy(taps.at[i], tap_buf.at[i], sems.at[i]).start()
    s = where_am_i(sc)
    gather_records(recs, own, other, (got1, got2), (sw1, sw2))

    def rows(y_off):
        return one_hot(
            (128, 128), lambda r, l: (r < 32) & (l == div(mod(r, 16), 2) * 16 + mod(r, 2) + y_off)
        )

    side_rows = (rows(0), rows(14))
    for i in range(3):
        p = s.a + jnp.minimum(i, s.n - 1)
        even = p % 2 == 0
        partner = jnp.where(even, p + 1, p - 1)
        ok_x = x_link(links, p) >= 0
        idx, off = locate_x(s, partner, TWO, 2)
        off = jnp.where(ok_x, off, NOWHERE)
        total = grad[:, i * 128 : i * 128 + 128] + mm(
            recs[idx], picker(TWO, off, jnp.where(even, 112, 0))
        )
        for side, up in ((0, True), (1, False)):
            q = p - 2 if up else p + 2
            c = partner - 2 if up else partner + 2
            ok = link_at(links, p, 2 + side) >= 0
            idx, off, _ = locate(s, q, up, TWO, 2)
            face = mm(recs[idx], picker(TWO, jnp.where(ok, off, NOWHERE), 0))
            ok_c = ok_x & (link_at(links, partner, 2 + side) >= 0)
            idx, _, off = locate(s, c, up, TWO, 2)
            face += mm(recs[idx], picker(TWO, jnp.where(ok_c, off, NOWHERE), 16))
            total += mm(face.astype(BF), side_rows[side])
        gred[:, i * 128 : i * 128 + 128] = jnp.where(i < s.n, total, 0.0).astype(BF)
    dw_down = mm(gred[...], hid[...], NT)
    g_one[...] = (mm(down[...], gred[...], TN) * slope[...]).astype(BF)
    order = parity_order()
    dw[...] = jnp.zeros_like(dw)

    @pl.loop(0, 3)
    def _(i):
        at = pl.ds(pl.multiple_of(i * 128, 128), 128)
        parts = [g_one[e * 64 : e * 64 + 64, at].astype(F32) for e in range(8)]
        tall = jnp.concatenate(swap_groups(parts), axis=0).astype(BF)
        tall = mm(tall, order, NT)
        g = jnp.concatenate(
            [tall[64 * b : 64 * b + 64] for b in range(8)] + [jnp.zeros((64, 128), F32)], axis=1
        )
        for dx in (-1, 0, 1):
            w = g if dx == 0 else pltpu.roll(g, (dx * 64) % 1152, 1)
            spread[(dx + 1) * 64 : (dx + 2) * 64, :] = w.astype(BF)
        pltpu.make_async_copy(taps.at[i], tap_buf.at[i], sems.at[i]).wait()
        dw[...] += mm(spread[...], tap_buf[i], NT)

    for d in range(4):
        for j in range(5):
            for dx in range(3):
                at = dx * 64 + d * 16
                out[dx * 5 + j, d] = dw[at : at + 16, j * 128 : j * 128 + 128].astype(BF)
        for og in range(2):
            for j in range(4):
                at = d * 32 + og * 16
                out[15 + og * 4 + j, d] = dw_down[
                    at : at + 16, j * 128 : j * 128 + 128
                ].astype(BF)
    out[23:, :, :, :] = jnp.zeros((9, 4, 16, 128), BF)


def final_kernel(pieces, one_out, down_out, two_out):
    lane = lax.broadcasted_iota(jnp.int32, (16, 128), 1)
    for dx in range(3):
        for og in range(2):
            for j in range(9):
                two_out[og * 16 : og * 16 + 16, dx * 1152 + j * 128 : dx * 1152 + j * 128 + 128] = (
                    pieces[dx * 9 + j, 16 + og * 16 : 32 + og * 16, :].astype(F32)
                )
    for og in range(2):
        for j in range(4):
            down_out[og * 16 : og * 16 + 16, j * 128 : j * 128 + 128] = pieces[
                15 + og * 4 + j, 0:16, :
            ].astype(F32)

    def tile(dx, j):
        return pieces[dx * 5 + j, 0:16, :].astype(F32)

    middle = jnp.concatenate([tile(1, j) for j in range(5)], axis=1)
    middle = pltpu.roll(middle, 64, 1)
    for j in range(4):
        one_out[:, j * 128 : j * 128 + 128] = tile(0, j)
        one_out[:, 1152 + j * 128 : 1280 + j * 128] = tile(2, j)
    one_out[:, 512:640] = jnp.where(lane < 64, tile(0, 4), middle[:, :128])
    one_out[:, 640:1152] = middle[:, 128:]
    one_out[:, 1664:1728] = tile(2, 4)[:, :64]


def call(kernel, scalars, arrays, outs, scratch, far_in=(), far_out=(), copies=0):
    smem = pl.BlockSpec(memory_space=pltpu.SMEM)
    vmem = pl.BlockSpec(memory_space=pltpu.VMEM)
    far = pl.BlockSpec(memory_space=pl.ANY)
    sems = [pltpu.SemaphoreType.DMA((copies,))] if copies else []
    return pl.pallas_call(
        kernel,
        out_shape=[jax.ShapeDtypeStruct(*o) for o in outs],
        in_specs=[smem] * len(scalars)
        + [far if k in far_in else vmem for k in range(len(arrays))],
        out_specs=[far if k in far_out else vmem for k in range(len(outs))],
        scratch_shapes=[pltpu.VMEM(*t) for t in scratch] + sems,
        compiler_params=pltpu.CompilerParams(vmem_limit_bytes=60 << 20),
    )(*scalars, *arrays)


def swap_cores(v):
    return lax.ppermute(v, "core", [(0, 1), (1, 0)])


def chips_on(v, by):
    up = [(2 * c, 2 * (c + by)) for c in range(NCHIP - by)]
    down = [(2 * c + 1, 2 * (c - by) + 1) for c in range(by, NCHIP)]
    return lax.ppermute(v, SPACE, up + down)


def across(v, axis, k):
    return lax.ppermute(v, axis, [(i, i ^ k) for i in range(lax.axis_size(axis))])


def exchange(level, sub, sc, own):
    other = swap_cores(own)
    (message,) = call(
        functools.partial(message_kernel, level, sub), (sc,), (own, other),
        [((level.C, level.R), BF)], [((6, level.C, level.R), BF)],
    )
    got1, got2 = chips_on(message, 1), chips_on(message, 2)
    return other, got1, got2, swap_cores(got1), swap_cores(got2)


def gathered(shard):
    return [shard] + [across(shard, "dp", k) for k in (1, 2, 3)]


def on_device(features, cotangent, conv_one, down_weight, conv_two, patch_home, patch_links):
    core, dp = lax.axis_index("core"), lax.axis_index("dp")
    dev = lax.axis_index(SPACE)
    chip = dev // 2
    slots = jnp.arange(8, dtype=jnp.int32)
    marks = jnp.where(slots == 0, -2, jnp.where(slots == 4, 4, slots - 1))
    starts = jnp.sum(
        (patch_home[None, :] < 3 * (2 * chip + marks)[:, None]).astype(jnp.int32), axis=1
    )
    sc = jnp.where(
        slots < 5, starts, jnp.where(slots == 5, dev, jnp.where(slots == 6, core, dp))
    ).astype(jnp.int32)
    links = patch_links.T
    x = features[0]
    rec_one, packed = call(
        faces_kernel, (sc, patch_home), (x, conv_one, down_weight),
        [((3, 64, 256), BF), ((80, 640), BF)], [((16, 1792), F32)],
    )
    rims_one = exchange(ONE, 1, sc, rec_one)
    w_one = gathered(packed)
    w_two = gathered(conv_two)
    taps, hid, slope, red, rec_two, down_full = call(
        stage_one_kernel, (sc, patch_home, links),
        (x, rec_one, *rims_one, *w_one),
        [((3, 640, 1152), BF), ((512, 384), BF), ((512, 384), F32), ((128, 384), BF),
         ((3, 128, 128), BF), ((128, 512), BF)],
        [((10, 64, 256), BF), ((128, 1152), BF), ((128, 1152), BF), ((4, 80, 640), BF),
         ((192, 576), BF), ((3, 640, 1152), BF)],
        far_out=(0,), copies=3,
    )
    rims_two = exchange(TWO, 1, sc, rec_two)
    cells = lax.axis_size("dp") * patch_links.shape[0] * 128
    out, keep, give, grad, rec_back = call(
        functools.partial(stage_two_kernel, float(cells) ** (-0.5)), (sc, patch_home, links),
        (red, cotangent[0], rec_two, *rims_two, *w_two),
        [((3, 128, 128), BF), ((32, 4, 16, 128), BF), ((32, 4, 16, 128), BF),
         ((128, 384), F32), ((3, 128, 128), BF)],
        [((10, 128, 128), BF), ((128, 256), BF), ((128, 256), BF), ((4, 32, 3456), BF),
         ((384, 1152), BF), ((1152, 768), BF), ((384, 768), BF)],
    )
    rims_back = exchange(TWO, 2, sc, rec_back)
    two = (keep.astype(F32) + swap_cores(give).astype(F32)).astype(BF)
    two = lax.all_to_all(two, ("x", "y", "core"), 0, 0, tiled=True)
    (small,) = call(
        stage_three_kernel, (sc, links),
        (grad, rec_back, *rims_back, down_full, hid, slope, taps),
        [((32, 4, 16, 128), BF)],
        [((10, 128, 128), BF), ((128, 384), BF), ((512, 384), BF), ((192, 1152), BF),
         ((192, 640), F32), ((3, 640, 1152), BF)],
        far_in=(10,), copies=3,
    )
    two = two.astype(F32).reshape(16, 2, 4, 16, 128).sum(axis=0).astype(BF)
    two, small = lax.optimization_barrier((two, small))
    small = lax.all_to_all(small, ("x", "y", "core"), 0, 0, tiled=True)
    small = small.astype(F32).sum(axis=0).astype(BF)
    mine = jnp.concatenate([small, two[0], two[1]], axis=1)
    got = lax.all_to_all(jnp.concatenate([mine, mine]), ("zh", "dp"), 0, 0, tiled=True)
    mine = got.astype(F32).sum(axis=0).astype(BF)
    copies = jnp.broadcast_to(mine[None], (32, *mine.shape))
    pieces = lax.all_to_all(copies, ("x", "y", "core"), 0, 0, tiled=True)
    grads = call(
        final_kernel, (), (pieces,),
        [((16, 1728), F32), ((32, 512), F32), ((32, 3456), F32)], [],
    )
    return (out[None], *grads)


def solution(mesh):
    split = Mesh(
        mesh.devices.reshape(mesh.shape["dp"], 4, 2, 4, 2), ("dp", "x", "zh", "y", "core")
    )
    return jax.shard_map(
        on_device,
        mesh=split,
        in_specs=(
            P("dp", SPACE, None, None),
            P("dp", SPACE, None, None),
            P("dp", None),
            P("dp", None),
            P("dp", None),
            P(),
            P(),
        ),
        out_specs=(P("dp", SPACE, None, None), P("dp", None), P("dp", None), P("dp", None)),
        check_vma=False,
    )
```
